32 devices in a mesh: dp: 8 (over z, x), tensor: 4 (over y, core).
Axes of the slice: x: 2, y: 2, z: 4, core: 2. Of those that a mesh axis runs over, the one named last changes fastest.
Arguments:
- context: bfloat16 [8192, 7168], P('dp', 'tensor'), may hold values from -6 to 6
- resid: bfloat16 [8192, 7168], P(('dp', 'tensor')), may hold values from -6 to 6
- o_weight: bfloat16 [7168, 7168], P('tensor', 'dp'), may hold values from -0.0625 to 0.0625
- norm_gain: float32 [7168], replicated, may hold values from 0.5 to 1.5
- queries: float32 [32, 7168], P('dp'), may hold values from -6 to 6
- positive_ids: int32 [32], P('dp'), may hold values from 0 to 15
- negative_ids: int32 [32, 7], P('dp'), may hold values from 0 to 15
- margins: float32 [32, 7], P('dp'), may hold values from -6 to 6
- pair_counts: int32 [32], P('dp'), may hold values from 1 to 7, as said below
Outputs:
- hidden_grad: float32 [8192, 7168], P(('dp', 'tensor'))
- loss: float32 [], replicated
The draws below stay inside these ranges and needn't reach their ends.
Inputs may be any that keep to these rules, and one draw needn't show every extreme that they name: `pair_counts`: some query has all 7 negatives live.
All inputs are finite; a program needn't handle non-finite values.
Results may differ from the reference program's by a relative error of at most 0.0003.
Values may be sent and summed in bfloat16 or wider, within the bound.
A program may use at most 192 MiB of HBM per device.

```python
import jax
import jax.numpy as jnp
from jax import lax

D = 7168
SEQ = 512
PASS_DEV = 2
Q_DEV = 4
NEG = 7
NPASS = 16
QUERIES = 32
TOKENS = 8192
N_DP = 8
N_TENSOR = 4


def draw_pair_counts(key, part):
    counts = jax.random.randint(key, (QUERIES,), 1, NEG + 1)
    return counts.at[0].set(NEG).astype(jnp.int32)


def set_ends(drawn, stream_key, smallest, high):
    longest = drawn.shape.index(max(drawn.shape))
    spots = []
    for shift in (0, 1):
        where = [jax.random.randint(jax.random.fold_in(stream_key, axis), (), 0, length) for axis, length in enumerate(drawn.shape)]
        where[longest] = (where[longest] + shift) % drawn.shape[longest]
        spots.append(tuple(where))
    return drawn.at[spots[0]].set(smallest).at[spots[1]].set(high)


def steps_of(rng, shape, split, least, top_value):
    loudness, own = 1.0, jax.random.fold_in(rng, 6)
    for axis_at, parts in split:
        draws = jnp.exp(jax.random.uniform(jax.random.fold_in(own, axis_at), (parts,), jnp.float32, least / len(split), top_value / len(split)))
        loudness = loudness * jnp.repeat(draws, shape[axis_at] // parts).reshape([-1 if axis == axis_at else 1 for axis in range(len(shape))])
    return loudness


def bell_draw(stream_key, dims, scale, reach, split=(), kind=jnp.bfloat16):
    result = scale * jax.random.normal(stream_key, dims, jnp.float32)
    if split:
        result = result * steps_of(stream_key, dims, split, -0.22, 0.18)
    return jnp.clip(result, -reach, reach).astype(kind)


def setup_inputs(seed: int = 0) -> dict:
    arg_keys = jax.random.split(jax.random.key(seed), 10)
    return {
        "context": bell_draw(arg_keys[0], (TOKENS, D), 1.0, 6.0, ((0, 8), (1, 4))),
        "resid": bell_draw(arg_keys[1], (TOKENS, D), 1.0, 6.0, ((0, 32),)),
        "o_weight": bell_draw(arg_keys[2], (D, D), D ** -0.5, 0.0625, ((0, 4), (1, 8))),
        "norm_gain": jnp.clip(1.0 + 0.1 * jax.random.normal(arg_keys[3], (D,), jnp.float32), 0.5, 1.5),
        "queries": bell_draw(arg_keys[4], (QUERIES, D), 1.0, 6.0, ((0, 8),), jnp.float32),
        "positive_ids": set_ends(jax.random.randint(arg_keys[5], (QUERIES,), 0, NPASS), jax.random.fold_in(arg_keys[5], 1), 0, NPASS - 1).astype(jnp.int32),
        "negative_ids": set_ends(jax.random.randint(arg_keys[6], (QUERIES, NEG), 0, NPASS), jax.random.fold_in(arg_keys[6], 1), 0, NPASS - 1).astype(jnp.int32),
        "margins": bell_draw(arg_keys[7], (QUERIES, NEG), 1.0, 6.0, ((0, 8),), jnp.float32),
        "pair_counts": draw_pair_counts(jax.random.fold_in(arg_keys[9], 71), 0),
    }


def block_hidden(inputs, o_weight):
    ctx_block, res_block = inputs
    width = D // N_TENSOR
    ctx_groups = ctx_block.reshape(ctx_block.shape[0], N_TENSOR, width).transpose(1, 0, 2)
    weight_groups = o_weight.reshape(N_TENSOR, width, D)

    def add_group(total, pair):
        part = jnp.dot(pair[0], pair[1], preferred_element_type=jnp.float32)
        return (total + part, None)
    start = jnp.zeros((ctx_block.shape[0], D), jnp.float32)
    total, _ = lax.scan(add_group, start, (ctx_groups, weight_groups))
    return res_block.astype(jnp.float32) + total

def reference(context, resid, o_weight, norm_gain, queries, positive_ids, negative_ids, margins, pair_counts):
    rows = PASS_DEV * SEQ
    ctx_blocks = context.reshape(N_DP, rows, D)
    res_blocks = resid.reshape(N_DP, rows, D)
    hidden = lax.map(lambda pair: block_hidden(pair, o_weight), (ctx_blocks, res_blocks))
    inv = lax.rsqrt(lax.optimization_barrier(jnp.mean(hidden * hidden, axis=-1, keepdims=True)) + 1e-05)
    normed = hidden * inv * norm_gain
    pooled = lax.optimization_barrier(jnp.sum(normed.reshape(N_DP * PASS_DEV, SEQ, D), axis=1))
    scale = 1.0 / jnp.sqrt(jnp.float32(D * SEQ))
    scores = jnp.dot(queries, pooled.T, precision=lax.Precision.HIGHEST) * scale
    npass = N_DP * PASS_DEV
    nquery = N_DP * Q_DEV
    passes = jnp.arange(npass, dtype=jnp.int32)
    onehot_pos = (positive_ids[:, None] == passes[None, :]).astype(jnp.float32)
    onehot_neg = (negative_ids[:, :, None] == passes[None, None, :]).astype(jnp.float32)
    score_pos = lax.optimization_barrier(jnp.sum(onehot_pos * scores, axis=-1))
    score_neg = lax.optimization_barrier(jnp.sum(onehot_neg * scores[:, None, :], axis=-1))
    err = score_pos[:, None] - score_neg - margins
    live = (jnp.arange(NEG, dtype=jnp.int32)[None, :] < pair_counts[:, None]).astype(jnp.float32)
    counts = pair_counts.astype(jnp.float32)
    loss = jnp.sum(lax.optimization_barrier(jnp.sum(live * err * err, axis=1)) / counts) / nquery
    weight = 2.0 * live * err / (counts[:, None] * nquery)
    coef = onehot_pos * lax.optimization_barrier(jnp.sum(weight, axis=1))[:, None] - lax.optimization_barrier(jnp.sum(weight[:, :, None] * onehot_neg, axis=1))
    pass_grad = jnp.dot(coef.T, queries, precision=lax.Precision.HIGHEST) * scale
    token_grad = jnp.repeat(pass_grad, SEQ, axis=0).reshape(N_DP, rows, D)
    upward = token_grad * norm_gain
    inner = lax.optimization_barrier(jnp.mean(hidden * upward, axis=-1, keepdims=True))
    grad = 65536.0 * (inv * upward - hidden * inv * inv * inv * inner)
    return (grad.reshape(npass * SEQ, D), loss)
```

```python
import functools

import jax
import jax.numpy as jnp
from jax import lax
from jax.experimental import pallas as pl
from jax.experimental.pallas import tpu as pltpu
from jax.sharding import PartitionSpec as P

D = 7168
SEQ = 512
PASS_DEV = 2
Q_DEV = 4
NEG = 7


def shards(
    context, resid, o_weight, norm_gain, queries, positive_ids, negative_ids, margins, pair_counts
):
    full_weight = lax.all_gather(o_weight, "dp", axis=1, tiled=True)
    tok_rows = resid.shape[0]
    attn = lax.psum_scatter(
        jnp.dot(context, full_weight, preferred_element_type=jnp.float32),
        "tensor",
        scatter_dimension=0,
        tiled=True,
    )
    hidden = resid.astype(jnp.float32) + attn
    inv = lax.rsqrt(jnp.mean(hidden * hidden, axis=-1, keepdims=True) + 1e-05)
    normed = hidden * inv * norm_gain
    first = lax.axis_index("tensor") * tok_rows
    passage_of = (first + jnp.arange(tok_rows, dtype=jnp.int32)) // SEQ
    member = (passage_of[None, :] == jnp.arange(PASS_DEV, dtype=jnp.int32)[:, None]).astype(
        jnp.float32
    )
    partial_value = jnp.dot(member, normed, precision=lax.Precision.HIGHEST)
    scale = 1.0 / jnp.sqrt(jnp.float32(D * SEQ))
    npass = PASS_DEV * lax.axis_size("dp")
    nquery = Q_DEV * lax.axis_size("dp")
    pooled = lax.psum(partial_value, "tensor")
    every_pass = lax.all_gather(pooled, "dp", axis=0, tiled=True)
    scores = jnp.dot(queries, every_pass.T, precision=lax.Precision.HIGHEST) * scale
    passes = jnp.arange(npass, dtype=jnp.int32)
    onehot_pos = (positive_ids[:, None] == passes[None, :]).astype(jnp.float32)
    onehot_neg = (negative_ids[:, :, None] == passes[None, None, :]).astype(jnp.float32)
    score_pos = jnp.sum(onehot_pos * scores, axis=-1)
    score_neg = jnp.sum(onehot_neg * scores[:, None, :], axis=-1)
    err = score_pos[:, None] - score_neg - margins
    live = (jnp.arange(NEG, dtype=jnp.int32)[None, :] < pair_counts[:, None]).astype(jnp.float32)
    counts = pair_counts.astype(jnp.float32)
    local_loss = jnp.sum(jnp.sum(live * err * err, axis=1) / counts) / nquery
    weight = 2.0 * live * err / (counts[:, None] * nquery)
    coef = onehot_pos * jnp.sum(weight, axis=1)[:, None] - jnp.sum(
        weight[:, :, None] * onehot_neg, axis=1
    )
    grad_terms = jnp.dot(coef.T, queries, precision=lax.Precision.HIGHEST) * scale
    pass_grad = lax.psum_scatter(grad_terms, "dp", scatter_dimension=0, tiled=True)
    loss = lax.psum(local_loss, "dp")
    upward = jnp.dot(member.T, pass_grad, precision=lax.Precision.HIGHEST) * norm_gain
    inner = jnp.mean(hidden * upward, axis=-1, keepdims=True)
    grad = 65536.0 * (inv * upward - hidden * inv * inv * inv * inner)
    return (grad, loss)


MESH = pl.DeviceIdType.MESH
LANES = 128
LAG = 2
RING = 4


def tile_kernel(
    nz,
    ctx_ref,
    weight_ref,
    resid_ref,
    out_ref,
    ctx,
    wgt,
    from_y,
    hid,
    res,
    stage,
    hold,
    ctx_load,
    ctx_core,
    ctx_x,
    w_load,
    w_right,
    w_left,
    w_recv,
    w_core,
    y_send,
    y_recv,
    x_send,
    x_recv,
    res_sem,
    out_sem,
):
    dp_at, t_at = lax.axis_index("dp"), lax.axis_index("tensor")
    z, x = dp_at // 2, dp_at % 2
    y, core = t_at // 2, t_at % 2
    chunks = wgt.shape[2]
    rows = hid.shape[1]
    other_core = (dp_at, 2 * y + 1 - core)
    y_peer = (dp_at, 2 * (1 - y) + core)
    x_peer = (2 * z + 1 - x, t_at)
    right, left = (dp_at + 2, t_at), (dp_at - 2, t_at)
    has_right, has_left = z < nz - 1, z > 0

    barrier = pltpu.get_barrier_semaphore()
    for peer in (other_core, y_peer, x_peer):
        pl.semaphore_signal(barrier, inc=1, device_id=peer, device_id_type=MESH)

    @pl.when(has_right)
    def _():
        pl.semaphore_signal(barrier, inc=1, device_id=right, device_id_type=MESH)

    @pl.when(has_left)
    def _():
        pl.semaphore_signal(barrier, inc=1, device_id=left, device_id_type=MESH)

    def remote(src, dst, send, recv, peer):
        return pltpu.make_async_remote_copy(
            src_ref=src,
            dst_ref=dst,
            send_sem=send,
            recv_sem=recv,
            device_id=peer,
            device_id_type=MESH,
        )

    def load_weight(j):
        return pltpu.make_async_copy(
            weight_ref.at[:, pl.ds(j * LANES, LANES)], wgt.at[0, z, j], w_load.at[j]
        )

    def quarter(r, c):
        return pl.ds(pl.multiple_of((2 * ((y + r) % 2) + c) * rows, rows), rows)

    def load_ctx(r):
        return pltpu.make_async_copy(
            ctx_ref.at[quarter(r, core)], ctx.at[0, 0, pl.ds(r * rows, rows)], ctx_load.at[r]
        )

    def core_ctx(r):
        return remote(
            ctx_ref.at[quarter(r, 1 - core)],
            ctx.at[1, 0, pl.ds(r * rows, rows)],
            ctx_core.at[0, r],
            ctx_core.at[1, r],
            other_core,
        )

    def swap_ctx(k, r):
        part = pl.ds(r * rows, rows)
        return remote(
            ctx.at[k, 0, part], ctx.at[k, 1, part], ctx_x.at[0, k, r], ctx_x.at[1, k, r], x_peer
        )

    def to_right(zt, j):
        return remote(wgt.at[0, zt, j], wgt.at[0, zt, j], w_right.at[zt, j], w_recv.at[zt, j], right)

    def to_left(zt, j):
        return remote(wgt.at[0, zt, j], wgt.at[0, zt, j], w_left.at[zt, j], w_recv.at[zt, j], left)

    def to_core(zt, j):
        return remote(
            wgt.at[0, zt, j], wgt.at[1, zt, j], w_core.at[0, zt, j], w_core.at[1, zt, j], other_core
        )

    def to_y(zt, j, rx, slot):
        return remote(
            stage.at[slot], from_y.at[zt, j, rx], y_send.at[slot], y_recv.at[zt, j, rx], y_peer
        )

    def piece(zt, xt, j):
        return (2 * zt + xt) * chunks + j

    def to_x(zt, j):
        return remote(
            from_y.at[zt, j, 1], hid.at[piece(zt, x, j)], x_send.at[zt, j], x_recv.at[zt, j], x_peer
        )

    def lanes(k):
        return pl.ds(pl.multiple_of(k * LANES, LANES), LANES)

    def write_out(k):
        return pltpu.make_async_copy(hid.at[k], out_ref.at[:, lanes(k)], out_sem.at[k])

    load_res = pltpu.make_async_copy(resid_ref, res, res_sem)

    for j in range(chunks):
        load_weight(j).start()
    for r in range(2):
        load_ctx(r).start()
    load_res.start()
    pl.semaphore_wait(
        barrier, 3 + jnp.where(has_right, 1, 0) + jnp.where(has_left, 1, 0)
    )
    for r in range(2):
        core_ctx(r).start()
    for j in range(chunks):
        load_weight(j).wait()

        @pl.when(has_right)
        def _():
            to_right(z, j).start()

        @pl.when(has_left)
        def _():
            to_left(z, j).start()

        to_core(z, j).start()
    for r in range(2):
        load_ctx(r).wait()
        swap_ctx(0, r).start()
    for r in range(2):
        core_ctx(r).wait_recv()
        swap_ctx(1, r).start()
    load_res.wait()

    ends = (z == 0) | (z == nz - 1)
    steps = 8 * chunks

    def task(i):
        two, three, four, six = 2 * chunks, 3 * chunks, 4 * chunks, 6 * chunks
        late = i - four
        k_e = jnp.where(i < two, i // chunks, jnp.where(i < four, (i - two) // chunks, 2 + late // two))
        j_e = jnp.where(i < four, i % chunks, (late % two) // 2)
        rx_e = jnp.where(i < two, 0, jnp.where(i < four, 1, late % 2))
        first = i < three
        m = jnp.where(first, i, i - three)
        n = m - chunks
        last = i - six
        k_m = jnp.where(i < six, jnp.where(m < chunks, 0, 1 + n % 2), 3)
        j_m = jnp.where(i < six, jnp.where(m < chunks, m, n // 2), last // 2)
        rx_m = jnp.where(first, 0, jnp.where(i < six, 1, last % 2))
        k = jnp.where(ends, k_e, k_m)
        j = jnp.where(ends, j_e, j_m)
        rx = jnp.where(ends, rx_e, rx_m)
        near = jnp.where(ends, k, jnp.where(k == 0, 1, jnp.where(k == 1, 0, k)))
        zt = jnp.where(z >= nz // 2, nz - 1 - near, near)
        return zt, j, rx

    def compute(i):
        zt, j, rx = task(i)
        slot = i % RING

        @pl.when((rx == 0) & (zt != z))
        def _():
            to_right(zt, j).wait_recv()

            @pl.when((zt < z) & has_right)
            def _():
                to_right(zt, j).start()

            @pl.when((zt > z) & has_left)
            def _():
                to_left(zt, j).start()

            to_core(zt, j).start()

        @pl.when(rx == 0)
        def _():
            to_core(zt, j).wait_recv()

        @pl.when(i == jnp.where(ends, 2 * chunks, 3 * chunks))
        def _():
            for k in range(2):
                for r in range(2):
                    swap_ctx(k, r).wait_recv()

        part = jnp.dot(
            ctx[0, rx], wgt[0, zt, j], preferred_element_type=jnp.float32
        ) + jnp.dot(ctx[1, rx], wgt[1, zt, j], preferred_element_type=jnp.float32)

        @pl.when(i >= RING)
        def _():
            to_y(zt, j, rx, slot).wait_send()

        stage[slot] = part[rows:]
        to_y(zt, j, rx, slot).start()

        @pl.when(rx == 0)
        def _():
            hid[piece(zt, x, j)] = part[:rows]

        @pl.when(rx == 1)
        def _():
            hold[slot] = part[:rows]

    def add_y(i):
        zt, j, rx = task(i)
        slot = i % RING
        to_y(zt, j, rx, slot).wait_recv()

        @pl.when(rx == 0)
        def _():
            k = piece(zt, x, j)
            hid[k] = hid[k] + from_y[zt, j, 0] + res[:, lanes(k)].astype(jnp.float32)
            write_out(k).start()

        @pl.when(rx == 1)
        def _():
            from_y[zt, j, 1] = from_y[zt, j, 1] + hold[slot]
            to_x(zt, j).start()

    def add_x(i):
        zt, j, rx = task(i)

        @pl.when(rx == 1)
        def _():
            to_x(zt, j).wait_recv()
            k = piece(zt, 1 - x, j)
            hid[k] = hid[k] + res[:, lanes(k)].astype(jnp.float32)
            write_out(k).start()

    def step(i, carry):
        @pl.when(i >= 2 * LAG)
        def _():
            add_x(i - 2 * LAG)

        @pl.when((i >= LAG) & (i < steps + LAG))
        def _():
            add_y(i - LAG)

        @pl.when(i < steps)
        def _():
            compute(i)

        return carry

    lax.fori_loop(0, steps + 2 * LAG, step, 0)

    for s in range(RING):
        to_y(0, 0, 0, s).wait_send()
    for r in range(2):
        core_ctx(r).wait_send()
        for k in range(2):
            swap_ctx(k, r).wait_send()

    def drain(n, carry):
        zt, j = n // chunks, n % chunks
        to_core(zt, j).wait_send()
        to_x(zt, j).wait_send()

        @pl.when((zt <= z) & has_right)
        def _():
            to_right(zt, j).wait_send()

        @pl.when((zt >= z) & has_left)
        def _():
            to_left(zt, j).wait_send()

        for xt in range(2):
            write_out(piece(zt, xt, j)).wait()
        return carry

    lax.fori_loop(0, nz * chunks, drain, 0)


def tile_hidden(context, o_weight, resid):
    rows, width = resid.shape
    depth, columns = o_weight.shape
    chunks = columns // LANES
    nz = width // (2 * columns)
    f32, bf16 = jnp.float32, jnp.bfloat16
    dma = pltpu.SemaphoreType.DMA
    return pl.pallas_call(
        functools.partial(tile_kernel, nz),
        out_shape=jax.ShapeDtypeStruct((rows, width), f32),
        in_specs=[pl.BlockSpec(memory_space=pl.ANY)] * 3,
        out_specs=pl.BlockSpec(memory_space=pl.ANY),
        scratch_shapes=[
            pltpu.VMEM((2, 2, 2 * rows, depth), bf16),
            pltpu.VMEM((2, nz, chunks, depth, LANES), bf16),
            pltpu.VMEM((nz, chunks, 2, rows, LANES), f32),
            pltpu.VMEM((2 * nz * chunks, rows, LANES), f32),
            pltpu.VMEM((rows, width), bf16),
            pltpu.VMEM((RING, rows, LANES), f32),
            pltpu.VMEM((RING, rows, LANES), f32),
            dma((2,)),
            dma((2, 2)),
            dma((2, 2, 2)),
            dma((chunks,)),
            dma((nz, chunks)),
            dma((nz, chunks)),
            dma((nz, chunks)),
            dma((2, nz, chunks)),
            dma((RING,)),
            dma((nz, chunks, 2)),
            dma((nz, chunks)),
            dma((nz, chunks)),
            dma,
            dma((2 * nz * chunks,)),
        ],
        compiler_params=pltpu.CompilerParams(
            collective_id=0, has_side_effects=True, vmem_limit_bytes=58 << 20
        ),
        cost_estimate=pl.CostEstimate(
            flops=2 * 4 * rows * depth * width, bytes_accessed=4 * rows * width, transcendentals=0
        ),
    )(context, o_weight, resid)


def line_shards(
    context, resid, o_weight, norm_gain, queries, positive_ids, negative_ids, margins, pair_counts
):
    f32 = jnp.float32
    dp_at, t_at = lax.axis_index("dp"), lax.axis_index("tensor")
    tok_rows = resid.shape[0]
    small = jnp.concatenate(
        [
            queries,
            positive_ids.astype(f32)[:, None],
            negative_ids.astype(f32),
            margins,
            pair_counts.astype(f32)[:, None],
        ],
        axis=1,
    )
    for bit in (1, 2, 4):
        other = lax.ppermute(small, "dp", [(i, i ^ bit) for i in range(8)])
        small = jnp.where(
            (dp_at & bit) == 0,
            jnp.concatenate([small, other]),
            jnp.concatenate([other, small]),
        )
    queries = small[:, :D]
    positive_ids = small[:, D].astype(jnp.int32)
    negative_ids = small[:, D + 1 : D + 1 + NEG].astype(jnp.int32)
    margins = small[:, D + 1 + NEG : D + 1 + 2 * NEG]
    counts = small[:, D + 1 + 2 * NEG]
    hidden = tile_hidden(context, o_weight, resid)
    inv = lax.rsqrt(jnp.mean(hidden * hidden, axis=-1, keepdims=True) + 1e-05)
    pooled = jnp.sum(hidden * inv, axis=0) * norm_gain
    scale = 1.0 / jnp.sqrt(f32(D * SEQ))
    npass = PASS_DEV * lax.axis_size("dp")
    nquery = Q_DEV * lax.axis_size("dp")
    passes = jnp.arange(npass, dtype=jnp.int32)
    passage = PASS_DEV * dp_at + (t_at * tok_rows) // SEQ
    here = (passes == passage).astype(f32)
    scores = jnp.sum(queries * pooled[None, :], axis=1)[:, None] * here[None, :] * scale
    for bit in (1, 2, 4, 8, 16):
        scores = scores + lax.ppermute(
            scores, ("dp", "tensor"), [(i, i ^ bit) for i in range(32)]
        )
    onehot_pos = (positive_ids[:, None] == passes[None, :]).astype(f32)
    onehot_neg = (negative_ids[:, :, None] == passes[None, None, :]).astype(f32)
    score_pos = jnp.sum(onehot_pos * scores, axis=-1)
    score_neg = jnp.sum(onehot_neg * scores[:, None, :], axis=-1)
    err = score_pos[:, None] - score_neg - margins
    live = (jnp.arange(NEG, dtype=f32)[None, :] < counts[:, None]).astype(f32)
    loss = jnp.sum(jnp.sum(live * err * err, axis=1) / counts) / nquery
    weight = 2.0 * live * err / (counts[:, None] * nquery)
    at_pos = jnp.sum(onehot_pos * here[None, :], axis=1)
    at_neg = jnp.sum(onehot_neg * here[None, None, :], axis=2)
    coef = at_pos * jnp.sum(weight, axis=1) - jnp.sum(weight * at_neg, axis=1)
    pass_grad = jnp.sum(coef[:, None] * queries, axis=0) * scale
    upward = (pass_grad * norm_gain)[None, :]
    inner = jnp.mean(hidden * upward, axis=-1, keepdims=True)
    grad = 65536.0 * (inv * upward - hidden * (inv * inv * inv * inner))
    return (grad, loss)


def solution(mesh):
    body = line_shards if dict(mesh.shape) == {"dp": 8, "tensor": 4} else shards
    return jax.shard_map(
        body,
        mesh=mesh,
        in_specs=(
            P("dp", "tensor"),
            P(("dp", "tensor"), None),
            P("tensor", "dp"),
            P(),
            P("dp", None),
            P("dp"),
            P("dp", None),
            P("dp", None),
            P("dp"),
        ),
        out_specs=(P(("dp", "tensor"), None), P()),
        check_vma=False,
    )
```

```python
import functools
import math

import jax
import jax.numpy as jnp
from jax import lax
from jax.experimental import pallas as pl
from jax.experimental.pallas import tpu as pltpu
from jax.sharding import PartitionSpec as P

D = 7168
SEQ = 512
PASS_DEV = 2
Q_DEV = 4
NEG = 7


def shards(
    context, resid, o_weight, norm_gain, queries, positive_ids, negative_ids, margins, pair_counts
):
    full_weight = lax.all_gather(o_weight, "dp", axis=1, tiled=True)
    tok_rows = resid.shape[0]
    attn = lax.psum_scatter(
        jnp.dot(context, full_weight, preferred_element_type=jnp.float32),
        "tensor",
        scatter_dimension=0,
        tiled=True,
    )
    hidden = resid.astype(jnp.float32) + attn
    inv = lax.rsqrt(jnp.mean(hidden * hidden, axis=-1, keepdims=True) + 1e-05)
    normed = hidden * inv * norm_gain
    first = lax.axis_index("tensor") * tok_rows
    passage_of = (first + jnp.arange(tok_rows, dtype=jnp.int32)) // SEQ
    member = (passage_of[None, :] == jnp.arange(PASS_DEV, dtype=jnp.int32)[:, None]).astype(
        jnp.float32
    )
    partial_value = jnp.dot(member, normed, precision=lax.Precision.HIGHEST)
    scale = 1.0 / jnp.sqrt(jnp.float32(D * SEQ))
    npass = PASS_DEV * lax.axis_size("dp")
    nquery = Q_DEV * lax.axis_size("dp")
    pooled = lax.psum(partial_value, "tensor")
    every_pass = lax.all_gather(pooled, "dp", axis=0, tiled=True)
    scores = jnp.dot(queries, every_pass.T, precision=lax.Precision.HIGHEST) * scale
    passes = jnp.arange(npass, dtype=jnp.int32)
    onehot_pos = (positive_ids[:, None] == passes[None, :]).astype(jnp.float32)
    onehot_neg = (negative_ids[:, :, None] == passes[None, None, :]).astype(jnp.float32)
    score_pos = jnp.sum(onehot_pos * scores, axis=-1)
    score_neg = jnp.sum(onehot_neg * scores[:, None, :], axis=-1)
    err = score_pos[:, None] - score_neg - margins
    live = (jnp.arange(NEG, dtype=jnp.int32)[None, :] < pair_counts[:, None]).astype(jnp.float32)
    counts = pair_counts.astype(jnp.float32)
    local_loss = jnp.sum(jnp.sum(live * err * err, axis=1) / counts) / nquery
    weight = 2.0 * live * err / (counts[:, None] * nquery)
    coef = onehot_pos * jnp.sum(weight, axis=1)[:, None] - jnp.sum(
        weight[:, :, None] * onehot_neg, axis=1
    )
    grad_terms = jnp.dot(coef.T, queries, precision=lax.Precision.HIGHEST) * scale
    pass_grad = lax.psum_scatter(grad_terms, "dp", scatter_dimension=0, tiled=True)
    loss = lax.psum(local_loss, "dp")
    upward = jnp.dot(member.T, pass_grad, precision=lax.Precision.HIGHEST) * norm_gain
    inner = jnp.mean(hidden * upward, axis=-1, keepdims=True)
    grad = 65536.0 * (inv * upward - hidden * inv * inv * inv * inner)
    return (grad, loss)


MESH = pl.DeviceIdType.MESH
LANES = 128
LAG = 2
RING = 4


def tile_kernel(
    nz,
    ctx_ref,
    weight_ref,
    resid_ref,
    small_ref,
    gain_ref,
    out_ref,
    factor_ref,
    up_ref,
    loss_ref,
    ctx,
    wgt,
    from_y,
    hid,
    res,
    stage,
    hold,
    ctx_load,
    ctx_core,
    ctx_x,
    w_load,
    w_right,
    w_left,
    w_recv,
    w_core,
    y_send,
    y_recv,
    x_send,
    x_recv,
    res_sem,
    out_sem,
    every_q,
    square,
    pooled,
    board,
    q_load,
    q_z,
    q_x,
    q_y,
    q_core,
    s_z,
    s_plane,
):
    dp_at, t_at = lax.axis_index("dp"), lax.axis_index("tensor")
    z, x = dp_at // 2, dp_at % 2
    y, core = t_at // 2, t_at % 2
    chunks = wgt.shape[2]
    rows = hid.shape[1]
    group = 4 * x + t_at
    other_core = (dp_at, 2 * y + 1 - core)
    y_peer = (dp_at, 2 * (1 - y) + core)
    x_peer = (2 * z + 1 - x, t_at)
    right, left = (dp_at + 2, t_at), (dp_at - 2, t_at)
    has_right, has_left = z < nz - 1, z > 0

    def z_peer(other):
        return (2 * other + x, t_at)

    def plane_peer(other):
        return (2 * z + other // 4, other % 4)

    def other_groups():
        return [(group + m) % 8 for m in range(1, 8)]

    def other_planes():
        return [(z + m) % nz for m in range(1, nz)]

    barrier = pltpu.get_barrier_semaphore()
    for other in other_groups():
        pl.semaphore_signal(barrier, inc=1, device_id=plane_peer(other), device_id_type=MESH)
    for other in other_planes():
        pl.semaphore_signal(barrier, inc=1, device_id=z_peer(other), device_id_type=MESH)

    def remote(src, dst, send, recv, peer):
        return pltpu.make_async_remote_copy(
            src_ref=src,
            dst_ref=dst,
            send_sem=send,
            recv_sem=recv,
            device_id=peer,
            device_id_type=MESH,
        )

    def load_weight(j):
        return pltpu.make_async_copy(
            weight_ref.at[:, pl.ds(j * LANES, LANES)], wgt.at[0, z, j], w_load.at[j]
        )

    def quarter(r, c):
        return pl.ds(pl.multiple_of((2 * ((y + r) % 2) + c) * rows, rows), rows)

    def load_ctx(r):
        return pltpu.make_async_copy(
            ctx_ref.at[quarter(r, core)], ctx.at[0, 0, pl.ds(r * rows, rows)], ctx_load.at[r]
        )

    def core_ctx(r):
        return remote(
            ctx_ref.at[quarter(r, 1 - core)],
            ctx.at[1, 0, pl.ds(r * rows, rows)],
            ctx_core.at[0, r],
            ctx_core.at[1, r],
            other_core,
        )

    def swap_ctx(k, r):
        part = pl.ds(r * rows, rows)
        return remote(
            ctx.at[k, 0, part], ctx.at[k, 1, part], ctx_x.at[0, k, r], ctx_x.at[1, k, r], x_peer
        )

    def to_right(zt, j):
        return remote(wgt.at[0, zt, j], wgt.at[0, zt, j], w_right.at[zt, j], w_recv.at[zt, j], right)

    def to_left(zt, j):
        return remote(wgt.at[0, zt, j], wgt.at[0, zt, j], w_left.at[zt, j], w_recv.at[zt, j], left)

    def to_core(zt, j):
        return remote(
            wgt.at[0, zt, j], wgt.at[1, zt, j], w_core.at[0, zt, j], w_core.at[1, zt, j], other_core
        )

    def to_y(zt, j, rx, slot):
        return remote(
            stage.at[slot], from_y.at[zt, j, rx], y_send.at[slot], y_recv.at[zt, j, rx], y_peer
        )

    def piece(zt, xt, j):
        return (2 * zt + xt) * chunks + j

    def to_x(zt, j):
        return remote(
            from_y.at[zt, j, 1], hid.at[piece(zt, x, j)], x_send.at[zt, j], x_recv.at[zt, j], x_peer
        )

    def lanes(k):
        return pl.ds(pl.multiple_of(k * LANES, LANES), LANES)

    def write_out(k):
        return pltpu.make_async_copy(hid.at[k], out_ref.at[:, lanes(k)], out_sem.at[k])

    load_res = pltpu.make_async_copy(resid_ref, res, res_sem)

    def queries_z(source, target):
        mine = every_q.at[t_at, x, source]
        return remote(mine, mine, q_z.at[0, target], q_z.at[1, source], z_peer(target))

    def queries_x(xs):
        mine = every_q.at[t_at, xs]
        return remote(mine, mine, q_x.at[0], q_x.at[1], x_peer)

    def queries_y(ts):
        return remote(every_q.at[ts], every_q.at[ts], q_y.at[0], q_y.at[1], y_peer)

    def queries_core(n, ts):
        return remote(
            every_q.at[ts], every_q.at[ts], q_core.at[0, n], q_core.at[1, n], other_core
        )

    def scores_z(source, target):
        mine = board.at[group, source]
        return remote(mine, mine, s_z.at[0, target], s_z.at[1, source], z_peer(target))

    def scores_plane(source, target):
        return remote(
            board.at[source],
            board.at[source],
            s_plane.at[0, target],
            s_plane.at[1, source],
            plane_peer(target),
        )

    load_small = pltpu.make_async_copy(small_ref, every_q.at[t_at, x, z], q_load)
    load_small.start()
    for j in range(chunks):
        load_weight(j).start()
    for r in range(2):
        load_ctx(r).start()
    load_res.start()
    square[...] = jnp.zeros_like(square)
    pooled[...] = jnp.zeros_like(pooled)
    load_small.wait()
    pl.semaphore_wait(barrier, 7 + nz - 1)
    for other in other_planes():
        queries_z(z, other).start()
    for r in range(2):
        core_ctx(r).start()
    for j in range(chunks):
        load_weight(j).wait()

        @pl.when(has_right)
        def _():
            to_right(z, j).start()

        @pl.when(has_left)
        def _():
            to_left(z, j).start()

        to_core(z, j).start()
    for r in range(2):
        load_ctx(r).wait()
        swap_ctx(0, r).start()
    for r in range(2):
        core_ctx(r).wait_recv()
        swap_ctx(1, r).start()
    for other in other_planes():
        queries_z(other, z).wait_recv()
    queries_x(x).start()
    load_res.wait()

    ends = (z == 0) | (z == nz - 1)
    steps = 8 * chunks

    def task(i):
        two, three, four, six = 2 * chunks, 3 * chunks, 4 * chunks, 6 * chunks
        late = i - four
        k_e = jnp.where(i < two, i // chunks, jnp.where(i < four, (i - two) // chunks, 2 + late // two))
        j_e = jnp.where(i < four, i % chunks, (late % two) // 2)
        rx_e = jnp.where(i < two, 0, jnp.where(i < four, 1, late % 2))
        first = i < three
        m = jnp.where(first, i, i - three)
        n = m - chunks
        last = i - six
        k_m = jnp.where(i < six, jnp.where(m < chunks, 0, 1 + n % 2), 3)
        j_m = jnp.where(i < six, jnp.where(m < chunks, m, n // 2), last // 2)
        rx_m = jnp.where(first, 0, jnp.where(i < six, 1, last % 2))
        k = jnp.where(ends, k_e, k_m)
        j = jnp.where(ends, j_e, j_m)
        rx = jnp.where(ends, rx_e, rx_m)
        near = jnp.where(ends, k, jnp.where(k == 0, 1, jnp.where(k == 1, 0, k)))
        zt = jnp.where(z >= nz // 2, nz - 1 - near, near)
        return zt, j, rx

    def compute(i):
        zt, j, rx = task(i)
        slot = i % RING

        @pl.when((rx == 0) & (zt != z))
        def _():
            to_right(zt, j).wait_recv()

            @pl.when((zt < z) & has_right)
            def _():
                to_right(zt, j).start()

            @pl.when((zt > z) & has_left)
            def _():
                to_left(zt, j).start()

            to_core(zt, j).start()

        @pl.when(rx == 0)
        def _():
            to_core(zt, j).wait_recv()

        @pl.when(i == jnp.where(ends, 2 * chunks, 3 * chunks))
        def _():
            for k in range(2):
                for r in range(2):
                    swap_ctx(k, r).wait_recv()
            queries_x(1 - x).wait_recv()
            queries_y(t_at).start()
            queries_core(0, t_at).start()

        @pl.when(i == 6 * chunks)
        def _():
            queries_y((t_at + 2) % 4).wait_recv()
            queries_core(1, (t_at + 2) % 4).start()

        part = jnp.dot(
            ctx[0, rx], wgt[0, zt, j], preferred_element_type=jnp.float32
        ) + jnp.dot(ctx[1, rx], wgt[1, zt, j], preferred_element_type=jnp.float32)

        @pl.when(i >= RING)
        def _():
            to_y(zt, j, rx, slot).wait_send()

        stage[slot] = part[rows:]
        to_y(zt, j, rx, slot).start()

        @pl.when(rx == 0)
        def _():
            hid[piece(zt, x, j)] = part[:rows]

        @pl.when(rx == 1)
        def _():
            hold[slot] = part[:rows]

    def add_y(i):
        zt, j, rx = task(i)
        slot = i % RING
        to_y(zt, j, rx, slot).wait_recv()

        @pl.when(rx == 0)
        def _():
            k = piece(zt, x, j)
            total = hid[k] + from_y[zt, j, 0] + res[:, lanes(k)].astype(jnp.float32)
            hid[k] = total
            square[...] += total * total
            write_out(k).start()

        @pl.when(rx == 1)
        def _():
            from_y[zt, j, 1] = from_y[zt, j, 1] + hold[slot]
            to_x(zt, j).start()

    def add_x(i):
        zt, j, rx = task(i)

        @pl.when(rx == 1)
        def _():
            to_x(zt, j).wait_recv()
            k = piece(zt, 1 - x, j)
            total = hid[k] + res[:, lanes(k)].astype(jnp.float32)
            hid[k] = total
            square[...] += total * total
            write_out(k).start()

    def step(i, carry):
        @pl.when(i >= 2 * LAG)
        def _():
            add_x(i - 2 * LAG)

        @pl.when((i >= LAG) & (i < steps + LAG))
        def _():
            add_y(i - LAG)

        @pl.when(i < steps)
        def _():
            compute(i)

        return carry

    lax.fori_loop(0, steps + 2 * LAG, step, 0)

    f32, high = jnp.float32, lax.Precision.HIGHEST
    near_core = t_at + 1 - 2 * core
    queries_core(0, near_core).wait_recv()
    queries_core(1, (near_core + 2) % 4).wait_recv()
    width = 2 * nz * chunks * LANES
    half, share = nz * chunks, every_q.shape[4] - 2 * LANES
    inv = lax.rsqrt(jnp.sum(square[...], axis=1, keepdims=True) / width + 1e-05)
    inv_lanes = jnp.broadcast_to(inv, (rows, LANES))
    square[...] = inv_lanes

    def pool(n, carry):
        for h in range(2):
            pooled[h : h + 1, lanes(n)] = jnp.sum(
                hid[h * half + n] * square[...], axis=0, keepdims=True
            )
        return carry

    lax.fori_loop(0, half, pool, 0)
    scale = 1.0 / math.sqrt(width * SEQ)
    count = 8 * 2 * nz
    found = jnp.zeros((8, count), f32)
    for t in range(4):
        here = pl.ds(t * share, share)
        block = every_q[t, :, :, :, :share].reshape(count, share)
        found += lax.dot_general(
            pooled[:, here] * gain_ref[:, here],
            block,
            (((1,), (1,)), ((), ())),
            precision=high,
            preferred_element_type=f32,
        )
    found = jnp.concatenate([found, jnp.zeros((8, LANES - count), f32)], axis=1) * scale
    row = lax.broadcasted_iota(jnp.int32, (8, LANES), 0)
    lane = lax.broadcasted_iota(jnp.int32, (8, LANES), 1)
    kept = jnp.sum(jnp.where(row == lane % 2, found, 0.0), axis=0, keepdims=True)
    kept = jnp.broadcast_to(kept, (8, LANES))
    after, before = pltpu.roll(kept, LANES - 1, 1), pltpu.roll(kept, 1, 1)
    board[group, z] = kept + jnp.where(lane % 2 == 0, after, before)

    for other in other_planes():
        scores_z(z, other).start()
    info = jnp.zeros((8, 2 * LANES), f32)
    for xs in range(2):
        for zs in range(nz):
            info += every_q[0, xs, zs, :, share:]
    ids, facts = info[:, :LANES], info[:, LANES:]
    for other in other_planes():
        scores_z(other, z).wait_recv()
    for other in other_groups():
        scores_plane(group, other).start()
    for other in other_groups():
        scores_plane(other, group).wait_recv()

    picked = jnp.zeros((8, LANES), f32)
    for zs in range(nz):
        for xs in range(2):
            for ys in range(2):
                score = board[4 * xs + 2 * ys, zs] + board[4 * xs + 2 * ys + 1, zs]
                picked += jnp.where(ids == 2 * (2 * zs + xs) + ys, score, 0.0)
    counts = jnp.broadcast_to(facts[0:1], (8, LANES))
    err = jnp.broadcast_to(picked[0:1], (8, LANES)) - picked - facts
    live = (row >= 1) & ((row - 1).astype(f32) < counts)
    err = jnp.where(live, err, 0.0)
    counts = jnp.where(counts > 0, counts, 1.0)
    nquery = Q_DEV * 2 * nz
    terms = jnp.where(lane % 2 == 0, err * err / counts, 0.0)
    loss_ref[...] = jnp.broadcast_to(jnp.sum(terms, keepdims=True) / nquery, (8, LANES))
    weight = 2.0 * err / (counts * nquery)
    passage = (PASS_DEV * dp_at + y).astype(f32)
    at_pos = jnp.broadcast_to(jnp.where(ids[0:1] == passage, 1.0, 0.0), (8, LANES))
    at_neg = jnp.where(ids == passage, 1.0, 0.0)
    coef = jnp.sum(weight * (at_pos - at_neg), axis=0, keepdims=True)
    coef = jnp.where(row == lane % 2, jnp.broadcast_to(coef, (8, LANES)), 0.0)[:, :count]
    for t in range(4):
        here = pl.ds(t * share, share)
        block = every_q[t, :, :, :, :share].reshape(count, share)
        grad = jnp.dot(coef, block, precision=high, preferred_element_type=f32)
        up_ref[:, here] = grad * scale * gain_ref[:, here]

    def align(n, total):
        for h in range(2):
            total += hid[h * half + n] * up_ref[h : h + 1, lanes(n)]
        return total

    total = lax.fori_loop(0, half, align, jnp.zeros((rows, LANES), f32))
    inner = jnp.sum(total, axis=1, keepdims=True) / width
    factor_ref[0] = 65536.0 * square[...]
    factor_ref[1] = jnp.broadcast_to(-65536.0 * (inv * inv * inv * inner), (rows, LANES))

    for other in other_planes():
        queries_z(z, other).wait_send()
        scores_z(z, other).wait_send()
    for other in other_groups():
        scores_plane(group, other).wait_send()
    queries_x(x).wait_send()
    queries_y(t_at).wait_send()
    for n in range(2):
        queries_core(n, t_at).wait_send()

    for s in range(RING):
        to_y(0, 0, 0, s).wait_send()
    for r in range(2):
        core_ctx(r).wait_send()
        for k in range(2):
            swap_ctx(k, r).wait_send()

    def drain(n, carry):
        zt, j = n // chunks, n % chunks
        to_core(zt, j).wait_send()
        to_x(zt, j).wait_send()

        @pl.when((zt <= z) & has_right)
        def _():
            to_right(zt, j).wait_send()

        @pl.when((zt >= z) & has_left)
        def _():
            to_left(zt, j).wait_send()

        for xt in range(2):
            write_out(piece(zt, xt, j)).wait()
        return carry

    lax.fori_loop(0, nz * chunks, drain, 0)


def tile_hidden(context, o_weight, resid, small, gain):
    rows, width = resid.shape
    depth, columns = o_weight.shape
    chunks = columns // LANES
    nz = width // (2 * columns)
    f32, bf16 = jnp.float32, jnp.bfloat16
    dma = pltpu.SemaphoreType.DMA
    return pl.pallas_call(
        functools.partial(tile_kernel, nz),
        out_shape=(
            jax.ShapeDtypeStruct((rows, width), f32),
            jax.ShapeDtypeStruct((2, rows, LANES), f32),
            jax.ShapeDtypeStruct((8, width // 2), f32),
            jax.ShapeDtypeStruct((8, LANES), f32),
        ),
        in_specs=[pl.BlockSpec(memory_space=pl.ANY)] * 4 + [pl.BlockSpec(memory_space=pltpu.VMEM)],
        out_specs=(
            pl.BlockSpec(memory_space=pl.ANY),
            pl.BlockSpec(memory_space=pltpu.VMEM),
            pl.BlockSpec(memory_space=pltpu.VMEM),
            pl.BlockSpec(memory_space=pltpu.VMEM),
        ),
        scratch_shapes=[
            pltpu.VMEM((2, 2, 2 * rows, depth), bf16),
            pltpu.VMEM((2, nz, chunks, depth, LANES), bf16),
            pltpu.VMEM((nz, chunks, 2, rows, LANES), f32),
            pltpu.VMEM((2 * nz * chunks, rows, LANES), f32),
            pltpu.VMEM((rows, width), bf16),
            pltpu.VMEM((RING, rows, LANES), f32),
            pltpu.VMEM((RING, rows, LANES), f32),
            dma((2,)),
            dma((2, 2)),
            dma((2, 2, 2)),
            dma((chunks,)),
            dma((nz, chunks)),
            dma((nz, chunks)),
            dma((nz, chunks)),
            dma((2, nz, chunks)),
            dma((RING,)),
            dma((nz, chunks, 2)),
            dma((nz, chunks)),
            dma((nz, chunks)),
            dma,
            dma((2 * nz * chunks,)),
            pltpu.VMEM((4, 2, nz) + small.shape, f32),
            pltpu.VMEM((rows, LANES), f32),
            pltpu.VMEM((8, width // 2), f32),
            pltpu.VMEM((8, nz, 8, LANES), f32),
            dma,
            dma((2, nz)),
            dma((2,)),
            dma((2,)),
            dma((2, 2)),
            dma((2, nz)),
            dma((2, 8)),
        ],
        compiler_params=pltpu.CompilerParams(
            collective_id=0, has_side_effects=True, vmem_limit_bytes=58 << 20
        ),
        cost_estimate=pl.CostEstimate(
            flops=2 * 4 * rows * depth * width, bytes_accessed=4 * rows * width, transcendentals=0
        ),
    )(context, o_weight, resid, small, gain)


def line_shards(
    context, resid, o_weight, norm_gain, queries, positive_ids, negative_ids, margins, pair_counts
):
    f32 = jnp.float32
    dp_at, t_at = lax.axis_index("dp"), lax.axis_index("tensor")
    z, x = dp_at // 2, dp_at % 2
    halves = queries.reshape(2 * Q_DEV, D // 2)
    share = D // 8
    mine = lax.dynamic_slice(halves, (0, t_at * share), (2 * Q_DEV, share))
    facts = jnp.concatenate(
        [
            positive_ids.astype(f32)[:, None],
            negative_ids.astype(f32),
            pair_counts.astype(f32)[:, None],
            margins,
        ],
        axis=1,
    )
    first = 4 * lax.axis_size("dp") * x + 2 * Q_DEV * z
    at = (jnp.arange(LANES, dtype=jnp.int32) - first)[None, :]
    spot = jnp.arange(Q_DEV, dtype=jnp.int32)[:, None]
    place = (at >= 0) & (at // 2 == spot)
    info = jnp.sum(jnp.where(place[:, None, :], facts[:, :, None], 0.0), axis=0)
    small = jnp.concatenate([mine, info[:8], info[8:]], axis=1)
    gain = jnp.zeros((8, D // 2), f32).at[:2].set(norm_gain.reshape(2, D // 2))
    hidden, factors, upward, loss = tile_hidden(context, o_weight, resid, small, gain)
    upward = upward[:2].reshape(1, D)
    grad = factors[0, :, :1] * upward + factors[1, :, :1] * hidden
    return (grad, loss[0, 0])


def solution(mesh):
    body = line_shards if dict(mesh.shape) == {"dp": 8, "tensor": 4} else shards
    return jax.shard_map(
        body,
        mesh=mesh,
        in_specs=(
            P("dp", "tensor"),
            P(("dp", "tensor"), None),
            P("tensor", "dp"),
            P(),
            P("dp", None),
            P("dp"),
            P("dp", None),
            P("dp", None),
            P("dp"),
        ),
        out_specs=(P(("dp", "tensor"), None), P()),
        check_vma=False,
    )
```

```python
import functools
import math

import jax
import jax.numpy as jnp
from jax import lax
from jax.experimental import pallas as pl
from jax.experimental.pallas import tpu as pltpu
from jax.sharding import PartitionSpec as P

D = 7168
SEQ = 512
PASS_DEV = 2
Q_DEV = 4
NEG = 7


def shards(
    context, resid, o_weight, norm_gain, queries, positive_ids, negative_ids, margins, pair_counts
):
    full_weight = lax.all_gather(o_weight, "dp", axis=1, tiled=True)
    tok_rows = resid.shape[0]
    attn = lax.psum_scatter(
        jnp.dot(context, full_weight, preferred_element_type=jnp.float32),
        "tensor",
        scatter_dimension=0,
        tiled=True,
    )
    hidden = resid.astype(jnp.float32) + attn
    inv = lax.rsqrt(jnp.mean(hidden * hidden, axis=-1, keepdims=True) + 1e-05)
    normed = hidden * inv * norm_gain
    first = lax.axis_index("tensor") * tok_rows
    passage_of = (first + jnp.arange(tok_rows, dtype=jnp.int32)) // SEQ
    member = (passage_of[None, :] == jnp.arange(PASS_DEV, dtype=jnp.int32)[:, None]).astype(
        jnp.float32
    )
    partial_value = jnp.dot(member, normed, precision=lax.Precision.HIGHEST)
    scale = 1.0 / jnp.sqrt(jnp.float32(D * SEQ))
    npass = PASS_DEV * lax.axis_size("dp")
    nquery = Q_DEV * lax.axis_size("dp")
    pooled = lax.psum(partial_value, "tensor")
    every_pass = lax.all_gather(pooled, "dp", axis=0, tiled=True)
    scores = jnp.dot(queries, every_pass.T, precision=lax.Precision.HIGHEST) * scale
    passes = jnp.arange(npass, dtype=jnp.int32)
    onehot_pos = (positive_ids[:, None] == passes[None, :]).astype(jnp.float32)
    onehot_neg = (negative_ids[:, :, None] == passes[None, None, :]).astype(jnp.float32)
    score_pos = jnp.sum(onehot_pos * scores, axis=-1)
    score_neg = jnp.sum(onehot_neg * scores[:, None, :], axis=-1)
    err = score_pos[:, None] - score_neg - margins
    live = (jnp.arange(NEG, dtype=jnp.int32)[None, :] < pair_counts[:, None]).astype(jnp.float32)
    counts = pair_counts.astype(jnp.float32)
    local_loss = jnp.sum(jnp.sum(live * err * err, axis=1) / counts) / nquery
    weight = 2.0 * live * err / (counts[:, None] * nquery)
    coef = onehot_pos * jnp.sum(weight, axis=1)[:, None] - jnp.sum(
        weight[:, :, None] * onehot_neg, axis=1
    )
    grad_terms = jnp.dot(coef.T, queries, precision=lax.Precision.HIGHEST) * scale
    pass_grad = lax.psum_scatter(grad_terms, "dp", scatter_dimension=0, tiled=True)
    loss = lax.psum(local_loss, "dp")
    upward = jnp.dot(member.T, pass_grad, precision=lax.Precision.HIGHEST) * norm_gain
    inner = jnp.mean(hidden * upward, axis=-1, keepdims=True)
    grad = 65536.0 * (inv * upward - hidden * inv * inv * inv * inner)
    return (grad, loss)


MESH = pl.DeviceIdType.MESH
LANES = 128
LAG = 2
RING = 4


def tile_kernel(
    nz,
    ctx_ref,
    weight_ref,
    resid_ref,
    gain_ref,
    query_ref,
    positive_ref,
    negative_ref,
    margin_ref,
    count_ref,
    out_ref,
    factor_ref,
    up_ref,
    loss_ref,
    ctx,
    wgt,
    from_y,
    hid,
    res,
    stage,
    hold,
    ctx_load,
    ctx_core,
    ctx_x,
    w_load,
    w_right,
    w_left,
    w_recv,
    w_core,
    y_send,
    y_recv,
    x_send,
    x_recv,
    res_sem,
    out_sem,
    every_q,
    square,
    pooled,
    board,
    q_z,
    q_x,
    q_y,
    q_core,
    s_z,
    s_plane,
):
    dp_at, t_at = lax.axis_index("dp"), lax.axis_index("tensor")
    z, x = dp_at // 2, dp_at % 2
    y, core = t_at // 2, t_at % 2
    chunks = wgt.shape[2]
    rows = hid.shape[1]
    group = 4 * x + t_at
    other_core = (dp_at, 2 * y + 1 - core)
    y_peer = (dp_at, 2 * (1 - y) + core)
    x_peer = (2 * z + 1 - x, t_at)
    right, left = (dp_at + 2, t_at), (dp_at - 2, t_at)
    has_right, has_left = z < nz - 1, z > 0

    def z_peer(other):
        return (2 * other + x, t_at)

    def plane_peer(other):
        return (2 * z + other // 4, other % 4)

    def other_groups():
        return [(group + m) % 8 for m in range(1, 8)]

    def other_planes():
        return [(z + m) % nz for m in range(1, nz)]

    barrier = pltpu.get_barrier_semaphore()
    for other in other_groups():
        pl.semaphore_signal(barrier, inc=1, device_id=plane_peer(other), device_id_type=MESH)
    for other in other_planes():
        pl.semaphore_signal(barrier, inc=1, device_id=z_peer(other), device_id_type=MESH)

    def remote(src, dst, send, recv, peer):
        return pltpu.make_async_remote_copy(
            src_ref=src,
            dst_ref=dst,
            send_sem=send,
            recv_sem=recv,
            device_id=peer,
            device_id_type=MESH,
        )

    def load_weight(j):
        return pltpu.make_async_copy(
            weight_ref.at[:, pl.ds(j * LANES, LANES)], wgt.at[0, z, j], w_load.at[j]
        )

    def quarter(r, c):
        return pl.ds(pl.multiple_of((2 * ((y + r) % 2) + c) * rows, rows), rows)

    def load_ctx(r):
        return pltpu.make_async_copy(
            ctx_ref.at[quarter(r, core)], ctx.at[0, 0, pl.ds(r * rows, rows)], ctx_load.at[r]
        )

    def core_ctx(r):
        return remote(
            ctx_ref.at[quarter(r, 1 - core)],
            ctx.at[1, 0, pl.ds(r * rows, rows)],
            ctx_core.at[0, r],
            ctx_core.at[1, r],
            other_core,
        )

    def swap_ctx(k, r):
        part = pl.ds(r * rows, rows)
        return remote(
            ctx.at[k, 0, part], ctx.at[k, 1, part], ctx_x.at[0, k, r], ctx_x.at[1, k, r], x_peer
        )

    def to_right(zt, j):
        return remote(wgt.at[0, zt, j], wgt.at[0, zt, j], w_right.at[zt, j], w_recv.at[zt, j], right)

    def to_left(zt, j):
        return remote(wgt.at[0, zt, j], wgt.at[0, zt, j], w_left.at[zt, j], w_recv.at[zt, j], left)

    def to_core(zt, j):
        return remote(
            wgt.at[0, zt, j], wgt.at[1, zt, j], w_core.at[0, zt, j], w_core.at[1, zt, j], other_core
        )

    def to_y(zt, j, rx, slot):
        return remote(
            stage.at[slot], from_y.at[zt, j, rx], y_send.at[slot], y_recv.at[zt, j, rx], y_peer
        )

    def piece(zt, xt, j):
        return (2 * zt + xt) * chunks + j

    def to_x(zt, j):
        return remote(
            from_y.at[zt, j, 1], hid.at[piece(zt, x, j)], x_send.at[zt, j], x_recv.at[zt, j], x_peer
        )

    def lanes(k):
        return pl.ds(pl.multiple_of(k * LANES, LANES), LANES)

    def write_out(k):
        return pltpu.make_async_copy(hid.at[k], out_ref.at[:, lanes(k)], out_sem.at[k])

    load_res = pltpu.make_async_copy(resid_ref, res, res_sem)

    def queries_z(source, target):
        mine = every_q.at[t_at, x, source]
        return remote(mine, mine, q_z.at[0, target], q_z.at[1, source], z_peer(target))

    def queries_x(xs):
        mine = every_q.at[t_at, xs]
        return remote(mine, mine, q_x.at[0], q_x.at[1], x_peer)

    def queries_y(ts):
        return remote(every_q.at[ts], every_q.at[ts], q_y.at[0], q_y.at[1], y_peer)

    def queries_core(n, ts):
        return remote(
            every_q.at[ts], every_q.at[ts], q_core.at[0, n], q_core.at[1, n], other_core
        )

    def scores_z(source, target):
        mine = board.at[group, source]
        return remote(mine, mine, s_z.at[0, target], s_z.at[1, source], z_peer(target))

    def scores_plane(source, target):
        return remote(
            board.at[source],
            board.at[source],
            s_plane.at[0, target],
            s_plane.at[1, source],
            plane_peer(target),
        )

    for j in range(chunks):
        load_weight(j).start()
    for r in range(2):
        load_ctx(r).start()
    load_res.start()
    square[...] = jnp.zeros_like(square)
    pooled[...] = jnp.zeros_like(pooled)

    f32, high = jnp.float32, lax.Precision.HIGHEST
    width = 2 * nz * chunks * LANES
    half, share = nz * chunks, every_q.shape[4] - 2 * LANES
    row = lax.broadcasted_iota(jnp.int32, (8, LANES), 0)
    lane = lax.broadcasted_iota(jnp.int32, (8, LANES), 1)
    own_q = every_q.at[t_at, x, z]
    at = lane - 8 * (nz * x + z)
    ids = jnp.zeros((8, LANES), f32)
    facts = jnp.zeros((8, LANES), f32)
    for r in range(Q_DEV):
        for h in range(2):
            part = pl.ds(pl.multiple_of(h * (width // 2) + t_at * share, LANES), share)
            own_q[2 * r + h : 2 * r + h + 1, :share] = query_ref[r : r + 1, part]
        mine = (at == 2 * r) | (at == 2 * r + 1)
        ids = jnp.where(mine & (row == 0), positive_ref[r].astype(f32), ids)
        facts = jnp.where(mine & (row == 0), count_ref[r].astype(f32), facts)
        for k in range(NEG):
            ids = jnp.where(mine & (row == k + 1), negative_ref[r, k].astype(f32), ids)
            facts = jnp.where(mine & (row == k + 1), margin_ref[r, k], facts)
    own_q[:, share : share + LANES] = ids
    own_q[:, share + LANES :] = facts
    pl.semaphore_wait(barrier, 7 + nz - 1)
    for other in other_planes():
        queries_z(z, other).start()
    for r in range(2):
        core_ctx(r).start()
    for j in range(chunks):
        load_weight(j).wait()

        @pl.when(has_right)
        def _():
            to_right(z, j).start()

        @pl.when(has_left)
        def _():
            to_left(z, j).start()

        to_core(z, j).start()
    for r in range(2):
        load_ctx(r).wait()
        swap_ctx(0, r).start()
    for r in range(2):
        core_ctx(r).wait_recv()
        swap_ctx(1, r).start()
    for other in other_planes():
        queries_z(other, z).wait_recv()
    queries_x(x).start()
    load_res.wait()

    ends = (z == 0) | (z == nz - 1)
    steps = 8 * chunks

    def task(i):
        two, three, four, six = 2 * chunks, 3 * chunks, 4 * chunks, 6 * chunks
        late = i - four
        k_e = jnp.where(i < two, i // chunks, jnp.where(i < four, (i - two) // chunks, 2 + late // two))
        j_e = jnp.where(i < four, i % chunks, (late % two) // 2)
        rx_e = jnp.where(i < two, 0, jnp.where(i < four, 1, 1 - late % 2))
        first = i < three
        m = jnp.where(first, i, i - three)
        n = m - chunks
        last = i - six
        k_m = jnp.where(i < six, jnp.where(m < chunks, 0, 1 + n % 2), 3)
        j_m = jnp.where(i < six, jnp.where(m < chunks, m, n // 2), last // 2)
        rx_m = jnp.where(first, 0, jnp.where(i < six, 1, 1 - last % 2))
        k = jnp.where(ends, k_e, k_m)
        j = jnp.where(ends, j_e, j_m)
        rx = jnp.where(ends, rx_e, rx_m)
        near = jnp.where(ends, k, jnp.where(k == 0, 1, jnp.where(k == 1, 0, k)))
        zt = jnp.where(z >= nz // 2, nz - 1 - near, near)
        return zt, j, rx

    def compute(i):
        zt, j, rx = task(i)
        new = jnp.where(i < jnp.where(ends, 4 * chunks, 6 * chunks), rx == 0, rx == 1)
        slot = i % RING

        @pl.when(new & (zt != z))
        def _():
            to_right(zt, j).wait_recv()

            @pl.when((zt < z) & has_right)
            def _():
                to_right(zt, j).start()

            @pl.when((zt > z) & has_left)
            def _():
                to_left(zt, j).start()

            to_core(zt, j).start()

        @pl.when(new)
        def _():
            to_core(zt, j).wait_recv()

        @pl.when(i == jnp.where(ends, 2 * chunks, 3 * chunks))
        def _():
            for k in range(2):
                for r in range(2):
                    swap_ctx(k, r).wait_recv()
            queries_x(1 - x).wait_recv()
            queries_y(t_at).start()
            queries_core(0, t_at).start()

        @pl.when(i == 6 * chunks)
        def _():
            queries_y((t_at + 2) % 4).wait_recv()
            queries_core(1, (t_at + 2) % 4).start()

        part = jnp.dot(
            ctx[0, rx], wgt[0, zt, j], preferred_element_type=jnp.float32
        ) + jnp.dot(ctx[1, rx], wgt[1, zt, j], preferred_element_type=jnp.float32)

        @pl.when(i >= RING)
        def _():
            to_y(zt, j, rx, slot).wait_send()

        stage[slot] = part[rows:]
        to_y(zt, j, rx, slot).start()

        @pl.when(rx == 0)
        def _():
            hid[piece(zt, x, j)] = part[:rows]

        @pl.when(rx == 1)
        def _():
            hold[slot] = part[:rows]

    def add_y(i):
        zt, j, rx = task(i)
        slot = i % RING
        to_y(zt, j, rx, slot).wait_recv()

        @pl.when(rx == 0)
        def _():
            k = piece(zt, x, j)
            total = hid[k] + from_y[zt, j, 0] + res[:, lanes(k)].astype(jnp.float32)
            hid[k] = total
            square[...] += total * total
            write_out(k).start()

        @pl.when(rx == 1)
        def _():
            from_y[zt, j, 1] = from_y[zt, j, 1] + hold[slot]
            to_x(zt, j).start()

    def add_x(i):
        zt, j, rx = task(i)

        @pl.when(rx == 1)
        def _():
            to_x(zt, j).wait_recv()
            k = piece(zt, 1 - x, j)
            total = hid[k] + res[:, lanes(k)].astype(jnp.float32)
            hid[k] = total
            square[...] += total * total
            write_out(k).start()

    def step(i, carry):
        @pl.when(i >= 2 * LAG)
        def _():
            add_x(i - 2 * LAG)

        @pl.when((i >= LAG) & (i < steps + LAG))
        def _():
            add_y(i - LAG)

        @pl.when(i < steps)
        def _():
            compute(i)

        return carry

    lax.fori_loop(0, steps + 2 * LAG, step, 0)

    near_core = t_at + 1 - 2 * core
    queries_core(0, near_core).wait_recv()
    queries_core(1, (near_core + 2) % 4).wait_recv()
    inv = lax.rsqrt(jnp.sum(square[...], axis=1, keepdims=True) / width + 1e-05)
    inv_lanes = jnp.broadcast_to(inv, (rows, LANES))
    square[...] = inv_lanes

    def pool(n, carry):
        for h in range(2):
            k = h * half + n
            total = jnp.sum(hid[k] * square[...], axis=0, keepdims=True)
            pooled[h : h + 1, lanes(n)] = total * gain_ref[pl.ds(k, 1), :]
        return carry

    lax.fori_loop(0, half, pool, 0)
    scale = 1.0 / math.sqrt(width * SEQ)
    count = 8 * 2 * nz
    found = jnp.zeros((8, count), f32)
    for t in range(4):
        here = pl.ds(t * share, share)
        block = every_q[t, :, :, :, :share].reshape(count, share)
        found += lax.dot_general(
            pooled[:, here],
            block,
            (((1,), (1,)), ((), ())),
            precision=high,
            preferred_element_type=f32,
        )
    found = jnp.concatenate([found, jnp.zeros((8, LANES - count), f32)], axis=1) * scale
    kept = jnp.sum(jnp.where(row == lane % 2, found, 0.0), axis=0, keepdims=True)
    kept = jnp.broadcast_to(kept, (8, LANES))
    after, before = pltpu.roll(kept, LANES - 1, 1), pltpu.roll(kept, 1, 1)
    board[group, z] = kept + jnp.where(lane % 2 == 0, after, before)

    for other in other_planes():
        scores_z(z, other).start()
    info = jnp.zeros((8, 2 * LANES), f32)
    for xs in range(2):
        for zs in range(nz):
            info += every_q[0, xs, zs, :, share:]
    ids, facts = info[:, :LANES], info[:, LANES:]
    for other in other_planes():
        scores_z(other, z).wait_recv()
    for other in other_groups():
        scores_plane(group, other).start()
    for other in other_groups():
        scores_plane(other, group).wait_recv()

    picked = jnp.zeros((8, LANES), f32)
    for zs in range(nz):
        for xs in range(2):
            for ys in range(2):
                score = board[4 * xs + 2 * ys, zs] + board[4 * xs + 2 * ys + 1, zs]
                picked += jnp.where(ids == 2 * (2 * zs + xs) + ys, score, 0.0)
    counts = jnp.broadcast_to(facts[0:1], (8, LANES))
    err = jnp.broadcast_to(picked[0:1], (8, LANES)) - picked - facts
    live = (row >= 1) & ((row - 1).astype(f32) < counts)
    err = jnp.where(live, err, 0.0)
    counts = jnp.where(counts > 0, counts, 1.0)
    nquery = Q_DEV * 2 * nz
    terms = jnp.where(lane % 2 == 0, err * err / counts, 0.0)
    loss_ref[...] = jnp.broadcast_to(jnp.sum(terms, keepdims=True) / nquery, (8, LANES))
    weight = 2.0 * err / (counts * nquery)
    passage = (PASS_DEV * dp_at + y).astype(f32)
    at_pos = jnp.broadcast_to(jnp.where(ids[0:1] == passage, 1.0, 0.0), (8, LANES))
    at_neg = jnp.where(ids == passage, 1.0, 0.0)
    coef = jnp.sum(weight * (at_pos - at_neg), axis=0, keepdims=True)
    coef = jnp.where(row == lane % 2, jnp.broadcast_to(coef, (8, LANES)), 0.0)[:, :count]
    for t in range(4):
        here = pl.ds(t * share, share)
        block = every_q[t, :, :, :, :share].reshape(count, share)
        grad = jnp.dot(coef, block, precision=high, preferred_element_type=f32)
        pooled[:, here] = grad * scale

    def align(n, total):
        for h in range(2):
            k = h * half + n
            up = pooled[h : h + 1, lanes(n)] * gain_ref[pl.ds(k, 1), :]
            up_ref[0:1, lanes(k)] = up
            total += hid[k] * up
        return total

    total = lax.fori_loop(0, half, align, jnp.zeros((rows, LANES), f32))
    inner = jnp.sum(total, axis=1, keepdims=True) / width
    up_ref[1:, :] = jnp.zeros((7, width), f32)
    factor_ref[0] = 65536.0 * square[...]
    factor_ref[1] = jnp.broadcast_to(-65536.0 * (inv * inv * inv * inner), (rows, LANES))

    for other in other_planes():
        queries_z(z, other).wait_send()
        scores_z(z, other).wait_send()
    for other in other_groups():
        scores_plane(group, other).wait_send()
    queries_x(x).wait_send()
    queries_y(t_at).wait_send()
    for n in range(2):
        queries_core(n, t_at).wait_send()

    for s in range(RING):
        to_y(0, 0, 0, s).wait_send()
    for r in range(2):
        core_ctx(r).wait_send()
        for k in range(2):
            swap_ctx(k, r).wait_send()

    def drain(n, carry):
        zt, j = n // chunks, n % chunks
        to_core(zt, j).wait_send()
        to_x(zt, j).wait_send()

        @pl.when((zt <= z) & has_right)
        def _():
            to_right(zt, j).wait_send()

        @pl.when((zt >= z) & has_left)
        def _():
            to_left(zt, j).wait_send()

        for xt in range(2):
            write_out(piece(zt, xt, j)).wait()
        return carry

    lax.fori_loop(0, nz * chunks, drain, 0)


def tile_hidden(context, o_weight, resid, gain, queries, facts):
    rows, width = resid.shape
    depth, columns = o_weight.shape
    chunks = columns // LANES
    nz = width // (2 * columns)
    f32, bf16 = jnp.float32, jnp.bfloat16
    dma = pltpu.SemaphoreType.DMA
    return pl.pallas_call(
        functools.partial(tile_kernel, nz),
        out_shape=(
            jax.ShapeDtypeStruct((rows, width), f32),
            jax.ShapeDtypeStruct((2, rows, LANES), f32),
            jax.ShapeDtypeStruct((8, width), f32),
            jax.ShapeDtypeStruct((8, LANES), f32),
        ),
        in_specs=[pl.BlockSpec(memory_space=pl.ANY)] * 3
        + [pl.BlockSpec(memory_space=pltpu.VMEM)] * 2
        + [pl.BlockSpec(memory_space=pltpu.SMEM)] * 4,
        out_specs=(
            pl.BlockSpec(memory_space=pl.ANY),
            pl.BlockSpec(memory_space=pltpu.VMEM),
            pl.BlockSpec(memory_space=pltpu.VMEM),
            pl.BlockSpec(memory_space=pltpu.VMEM),
        ),
        scratch_shapes=[
            pltpu.VMEM((2, 2, 2 * rows, depth), bf16),
            pltpu.VMEM((2, nz, chunks, depth, LANES), bf16),
            pltpu.VMEM((nz, chunks, 2, rows, LANES), f32),
            pltpu.VMEM((2 * nz * chunks, rows, LANES), f32),
            pltpu.VMEM((rows, width), bf16),
            pltpu.VMEM((RING, rows, LANES), f32),
            pltpu.VMEM((RING, rows, LANES), f32),
            dma((2,)),
            dma((2, 2)),
            dma((2, 2, 2)),
            dma((chunks,)),
            dma((nz, chunks)),
            dma((nz, chunks)),
            dma((nz, chunks)),
            dma((2, nz, chunks)),
            dma((RING,)),
            dma((nz, chunks, 2)),
            dma((nz, chunks)),
            dma((nz, chunks)),
            dma,
            dma((2 * nz * chunks,)),
            pltpu.VMEM((4, 2, nz, 2 * Q_DEV, width // 8 + 2 * LANES), f32),
            pltpu.VMEM((rows, LANES), f32),
            pltpu.VMEM((8, width // 2), f32),
            pltpu.VMEM((8, nz, 8, LANES), f32),
            dma((2, nz)),
            dma((2,)),
            dma((2,)),
            dma((2, 2)),
            dma((2, nz)),
            dma((2, 8)),
        ],
        compiler_params=pltpu.CompilerParams(
            collective_id=0, has_side_effects=True, vmem_limit_bytes=58 << 20
        ),
        cost_estimate=pl.CostEstimate(
            flops=2 * 4 * rows * depth * width, bytes_accessed=4 * rows * width, transcendentals=0
        ),
    )(context, o_weight, resid, gain, queries, *facts)


def grad_kernel(hidden_ref, factor_ref, up_ref, grad_ref):
    for n in range(grad_ref.shape[1] // LANES):
        here = pl.ds(n * LANES, LANES)
        grad_ref[:, here] = factor_ref[0] * up_ref[0:1, here] + factor_ref[1] * hidden_ref[:, here]


def gradient(hidden, factors, upward):
    rows, width = hidden.shape
    step = width // 8
    return pl.pallas_call(
        grad_kernel,
        out_shape=jax.ShapeDtypeStruct((rows, width), jnp.float32),
        grid=(width // step,),
        in_specs=[
            pl.BlockSpec((rows, step), lambda n: (0, n)),
            pl.BlockSpec((2, rows, LANES), lambda n: (0, 0, 0)),
            pl.BlockSpec((8, step), lambda n: (0, n)),
        ],
        out_specs=pl.BlockSpec((rows, step), lambda n: (0, n)),
        compiler_params=pltpu.CompilerParams(vmem_limit_bytes=58 << 20),
    )(hidden, factors, upward)


def line_shards(
    context, resid, o_weight, norm_gain, queries, positive_ids, negative_ids, margins, pair_counts
):
    gain = norm_gain.reshape(-1, LANES)
    facts = (positive_ids, negative_ids, margins, pair_counts)
    hidden, factors, upward, loss = tile_hidden(context, o_weight, resid, gain, queries, facts)
    return (gradient(hidden, factors, upward), loss[0, 0])


def solution(mesh):
    body = line_shards if dict(mesh.shape) == {"dp": 8, "tensor": 4} else shards
    return jax.shard_map(
        body,
        mesh=mesh,
        in_specs=(
            P("dp", "tensor"),
            P(("dp", "tensor"), None),
            P("tensor", "dp"),
            P(),
            P("dp", None),
            P("dp"),
            P("dp", None),
            P("dp", None),
            P("dp"),
        ),
        out_specs=(P(("dp", "tensor"), None), P()),
        check_vma=False,
    )
```

```python
import functools
import math

import jax
import jax.numpy as jnp
from jax import lax
from jax.experimental import pallas as pl
from jax.experimental.pallas import tpu as pltpu
from jax.sharding import PartitionSpec as P

D = 7168
SEQ = 512
PASS_DEV = 2
Q_DEV = 4
NEG = 7


def shards(
    context, resid, o_weight, norm_gain, queries, positive_ids, negative_ids, margins, pair_counts
):
    full_weight = lax.all_gather(o_weight, "dp", axis=1, tiled=True)
    tok_rows = resid.shape[0]
    attn = lax.psum_scatter(
        jnp.dot(context, full_weight, preferred_element_type=jnp.float32),
        "tensor",
        scatter_dimension=0,
        tiled=True,
    )
    hidden = resid.astype(jnp.float32) + attn
    inv = lax.rsqrt(jnp.mean(hidden * hidden, axis=-1, keepdims=True) + 1e-05)
    normed = hidden * inv * norm_gain
    first = lax.axis_index("tensor") * tok_rows
    passage_of = (first + jnp.arange(tok_rows, dtype=jnp.int32)) // SEQ
    member = (passage_of[None, :] == jnp.arange(PASS_DEV, dtype=jnp.int32)[:, None]).astype(
        jnp.float32
    )
    partial_value = jnp.dot(member, normed, precision=lax.Precision.HIGHEST)
    scale = 1.0 / jnp.sqrt(jnp.float32(D * SEQ))
    npass = PASS_DEV * lax.axis_size("dp")
    nquery = Q_DEV * lax.axis_size("dp")
    pooled = lax.psum(partial_value, "tensor")
    every_pass = lax.all_gather(pooled, "dp", axis=0, tiled=True)
    scores = jnp.dot(queries, every_pass.T, precision=lax.Precision.HIGHEST) * scale
    passes = jnp.arange(npass, dtype=jnp.int32)
    onehot_pos = (positive_ids[:, None] == passes[None, :]).astype(jnp.float32)
    onehot_neg = (negative_ids[:, :, None] == passes[None, None, :]).astype(jnp.float32)
    score_pos = jnp.sum(onehot_pos * scores, axis=-1)
    score_neg = jnp.sum(onehot_neg * scores[:, None, :], axis=-1)
    err = score_pos[:, None] - score_neg - margins
    live = (jnp.arange(NEG, dtype=jnp.int32)[None, :] < pair_counts[:, None]).astype(jnp.float32)
    counts = pair_counts.astype(jnp.float32)
    local_loss = jnp.sum(jnp.sum(live * err * err, axis=1) / counts) / nquery
    weight = 2.0 * live * err / (counts[:, None] * nquery)
    coef = onehot_pos * jnp.sum(weight, axis=1)[:, None] - jnp.sum(
        weight[:, :, None] * onehot_neg, axis=1
    )
    grad_terms = jnp.dot(coef.T, queries, precision=lax.Precision.HIGHEST) * scale
    pass_grad = lax.psum_scatter(grad_terms, "dp", scatter_dimension=0, tiled=True)
    loss = lax.psum(local_loss, "dp")
    upward = jnp.dot(member.T, pass_grad, precision=lax.Precision.HIGHEST) * norm_gain
    inner = jnp.mean(hidden * upward, axis=-1, keepdims=True)
    grad = 65536.0 * (inv * upward - hidden * inv * inv * inv * inner)
    return (grad, loss)


MESH = pl.DeviceIdType.MESH
LANES = 128
LAG = 3
RING = 6


def tile_kernel(
    nz,
    ctx_ref,
    weight_ref,
    resid_ref,
    gain_ref,
    query_ref,
    positive_ref,
    negative_ref,
    margin_ref,
    count_ref,
    out_ref,
    factor_ref,
    up_ref,
    loss_ref,
    ctx,
    wgt,
    from_y,
    hid,
    res,
    stage,
    hold,
    ctx_load,
    ctx_core,
    ctx_x,
    w_load,
    w_right,
    w_left,
    w_recv,
    w_core,
    y_send,
    y_recv,
    x_send,
    x_recv,
    res_sem,
    out_sem,
    every_q,
    square,
    pooled,
    board,
    q_z,
    q_x,
    q_y,
    q_core,
    s_z,
    s_plane,
):
    dp_at, t_at = lax.axis_index("dp"), lax.axis_index("tensor")
    z, x = dp_at // 2, dp_at % 2
    y, core = t_at // 2, t_at % 2
    chunks = wgt.shape[2]
    rows = hid.shape[1]
    group = 4 * x + t_at
    other_core = (dp_at, 2 * y + 1 - core)
    y_peer = (dp_at, 2 * (1 - y) + core)
    x_peer = (2 * z + 1 - x, t_at)
    right, left = (dp_at + 2, t_at), (dp_at - 2, t_at)
    has_right, has_left = z < nz - 1, z > 0

    def z_peer(other):
        return (2 * other + x, t_at)

    def plane_peer(other):
        return (2 * z + other // 4, other % 4)

    def other_groups():
        return [(group + m) % 8 for m in range(1, 8)]

    def other_planes():
        return [(z + m) % nz for m in range(1, nz)]

    barrier = pltpu.get_barrier_semaphore()
    for other in other_groups():
        pl.semaphore_signal(barrier, inc=1, device_id=plane_peer(other), device_id_type=MESH)
    for other in other_planes():
        pl.semaphore_signal(barrier, inc=1, device_id=z_peer(other), device_id_type=MESH)

    def remote(src, dst, send, recv, peer):
        return pltpu.make_async_remote_copy(
            src_ref=src,
            dst_ref=dst,
            send_sem=send,
            recv_sem=recv,
            device_id=peer,
            device_id_type=MESH,
        )

    def load_weight(j):
        return pltpu.make_async_copy(
            weight_ref.at[:, pl.ds(j * LANES, LANES)], wgt.at[0, z, j], w_load.at[j]
        )

    def quarter(r, c):
        return pl.ds(pl.multiple_of((2 * ((y + r) % 2) + c) * rows, rows), rows)

    def load_ctx(r):
        return pltpu.make_async_copy(
            ctx_ref.at[quarter(r, core)], ctx.at[0, 0, pl.ds(r * rows, rows)], ctx_load.at[r]
        )

    def core_ctx(r):
        return remote(
            ctx_ref.at[quarter(r, 1 - core)],
            ctx.at[1, 0, pl.ds(r * rows, rows)],
            ctx_core.at[0, r],
            ctx_core.at[1, r],
            other_core,
        )

    def swap_ctx(k, r):
        part = pl.ds(r * rows, rows)
        return remote(
            ctx.at[k, 0, part], ctx.at[k, 1, part], ctx_x.at[0, k, r], ctx_x.at[1, k, r], x_peer
        )

    def to_right(zt, j):
        return remote(wgt.at[0, zt, j], wgt.at[0, zt, j], w_right.at[zt, j], w_recv.at[zt, j], right)

    def to_left(zt, j):
        return remote(wgt.at[0, zt, j], wgt.at[0, zt, j], w_left.at[zt, j], w_recv.at[zt, j], left)

    def to_core(zt, j):
        return remote(
            wgt.at[0, zt, j], wgt.at[1, zt, j], w_core.at[0, zt, j], w_core.at[1, zt, j], other_core
        )

    def to_y(zt, j, rx, slot):
        return remote(
            stage.at[slot], from_y.at[zt, j, rx], y_send.at[slot], y_recv.at[zt, j, rx], y_peer
        )

    def piece(zt, xt, j):
        return (2 * zt + xt) * chunks + j

    def to_x(zt, j):
        return remote(
            from_y.at[zt, j, 1], hid.at[piece(zt, x, j)], x_send.at[zt, j], x_recv.at[zt, j], x_peer
        )

    def lanes(k):
        return pl.ds(pl.multiple_of(k * LANES, LANES), LANES)

    def write_out(k):
        return pltpu.make_async_copy(hid.at[k], out_ref.at[:, lanes(k)], out_sem.at[k])

    load_res = pltpu.make_async_copy(resid_ref, res, res_sem)

    def queries_z(source, target):
        mine = every_q.at[t_at, x, source]
        return remote(mine, mine, q_z.at[0, target], q_z.at[1, source], z_peer(target))

    def queries_x(xs):
        mine = every_q.at[t_at, xs]
        return remote(mine, mine, q_x.at[0], q_x.at[1], x_peer)

    def queries_y(ts):
        return remote(every_q.at[ts], every_q.at[ts], q_y.at[0], q_y.at[1], y_peer)

    def queries_core(n, ts):
        return remote(
            every_q.at[ts], every_q.at[ts], q_core.at[0, n], q_core.at[1, n], other_core
        )

    def scores_z(source, target):
        mine = board.at[group, source]
        return remote(mine, mine, s_z.at[0, target], s_z.at[1, source], z_peer(target))

    def scores_plane(source, target):
        return remote(
            board.at[source],
            board.at[source],
            s_plane.at[0, target],
            s_plane.at[1, source],
            plane_peer(target),
        )

    for j in range(chunks):
        load_weight(j).start()
    for r in range(2):
        load_ctx(r).start()
    load_res.start()
    square[...] = jnp.zeros_like(square)
    pooled[...] = jnp.zeros_like(pooled)

    f32, high = jnp.float32, lax.Precision.HIGHEST
    width = 2 * nz * chunks * LANES
    half, share = nz * chunks, every_q.shape[4] - 2 * LANES
    row = lax.broadcasted_iota(jnp.int32, (8, LANES), 0)
    lane = lax.broadcasted_iota(jnp.int32, (8, LANES), 1)
    own_q = every_q.at[t_at, x, z]
    at = lane - 8 * (nz * x + z)
    ids = jnp.zeros((8, LANES), f32)
    facts = jnp.zeros((8, LANES), f32)
    for r in range(Q_DEV):
        for h in range(2):
            part = pl.ds(pl.multiple_of(h * (width // 2) + t_at * share, LANES), share)
            own_q[2 * r + h : 2 * r + h + 1, :share] = query_ref[r : r + 1, part]
        mine = (at == 2 * r) | (at == 2 * r + 1)
        ids = jnp.where(mine & (row == 0), positive_ref[r].astype(f32), ids)
        facts = jnp.where(mine & (row == 0), count_ref[r].astype(f32), facts)
        for k in range(NEG):
            ids = jnp.where(mine & (row == k + 1), negative_ref[r, k].astype(f32), ids)
            facts = jnp.where(mine & (row == k + 1), margin_ref[r, k], facts)
    own_q[:, share : share + LANES] = ids
    own_q[:, share + LANES :] = facts
    pl.semaphore_wait(barrier, 7 + nz - 1)
    for other in other_planes():
        queries_z(z, other).start()
    for r in range(2):
        core_ctx(r).start()
    for j in range(chunks):
        load_weight(j).wait()

        @pl.when(has_right)
        def _():
            to_right(z, j).start()

        @pl.when(has_left)
        def _():
            to_left(z, j).start()

        to_core(z, j).start()
    for r in range(2):
        load_ctx(r).wait()
        swap_ctx(0, r).start()
    for r in range(2):
        core_ctx(r).wait_recv()
        swap_ctx(1, r).start()
    load_res.wait()

    ends = (z == 0) | (z == nz - 1)
    steps = 8 * chunks

    def task(i):
        two, three, four, six = 2 * chunks, 3 * chunks, 4 * chunks, 6 * chunks
        late = i - four
        k_e = jnp.where(i < two, i // chunks, jnp.where(i < four, (i - two) // chunks, 2 + late // two))
        j_e = jnp.where(i < four, i % chunks, (late % two) // 2)
        rx_e = jnp.where(i < two, 0, jnp.where(i < four, 1, 1 - late % 2))
        first = i < three
        m = jnp.where(first, i, i - three)
        n = m - chunks
        last = i - six
        k_m = jnp.where(i < six, jnp.where(m < chunks, 0, 1 + n % 2), 3)
        j_m = jnp.where(i < six, jnp.where(m < chunks, m, n // 2), last // 2)
        rx_m = jnp.where(first, 0, jnp.where(i < six, 1, 1 - last % 2))
        k = jnp.where(ends, k_e, k_m)
        j = jnp.where(ends, j_e, j_m)
        rx = jnp.where(ends, rx_e, rx_m)
        near = jnp.where(ends, k, jnp.where(k == 0, 1, jnp.where(k == 1, 0, k)))
        zt = jnp.where(z >= nz // 2, nz - 1 - near, near)
        return zt, j, rx

    def relay(zt, j):
        to_right(zt, j).wait_recv()

        @pl.when((zt < z) & has_right)
        def _():
            to_right(zt, j).start()

        @pl.when((zt > z) & has_left)
        def _():
            to_left(zt, j).start()

        to_core(zt, j).start()

    def compute(i):
        zt, j, rx = task(i)
        new = jnp.where(i < jnp.where(ends, 4 * chunks, 6 * chunks), rx == 0, rx == 1)
        slot = i % RING

        @pl.when(new & (zt != z) & (ends | (i < 6 * chunks)))
        def _():
            relay(zt, j)

        @pl.when(new)
        def _():
            to_core(zt, j).wait_recv()

        begin = jnp.where(ends, 2 * chunks, 3 * chunks)

        @pl.when(i == begin)
        def _():
            for k in range(2):
                for r in range(2):
                    swap_ctx(k, r).wait_recv()
            for other in other_planes():
                queries_z(other, z).wait_recv()
            queries_x(x).start()

        @pl.when(i == begin + chunks)
        def _():
            queries_x(1 - x).wait_recv()
            queries_y(t_at).start()
            queries_core(0, t_at).start()

        @pl.when(i == 6 * chunks)
        def _():
            queries_y((t_at + 2) % 4).wait_recv()
            queries_core(1, (t_at + 2) % 4).start()

        @pl.when(jnp.logical_not(ends) & (i >= begin) & (i < 6 * chunks) & ((i - begin) % 3 == 2))
        def _():
            relay(jnp.where(z >= nz // 2, 0, nz - 1), (i - begin) // 3)

        part = jnp.dot(
            ctx[0, rx], wgt[0, zt, j], preferred_element_type=jnp.float32
        ) + jnp.dot(ctx[1, rx], wgt[1, zt, j], preferred_element_type=jnp.float32)

        @pl.when(i >= RING)
        def _():
            to_y(zt, j, rx, slot).wait_send()

        stage[slot] = part[rows:]
        to_y(zt, j, rx, slot).start()

        @pl.when(rx == 0)
        def _():
            hid[piece(zt, x, j)] = part[:rows]

        @pl.when(rx == 1)
        def _():
            hold[slot] = part[:rows]

    def add_y(i):
        zt, j, rx = task(i)
        slot = i % RING
        to_y(zt, j, rx, slot).wait_recv()

        @pl.when(rx == 0)
        def _():
            k = piece(zt, x, j)
            total = hid[k] + from_y[zt, j, 0] + res[:, lanes(k)].astype(jnp.float32)
            hid[k] = total
            square[...] += total * total
            write_out(k).start()

        @pl.when(rx == 1)
        def _():
            from_y[zt, j, 1] = from_y[zt, j, 1] + hold[slot]
            to_x(zt, j).start()

    def add_x(i):
        zt, j, rx = task(i)

        @pl.when(rx == 1)
        def _():
            to_x(zt, j).wait_recv()
            k = piece(zt, 1 - x, j)
            total = hid[k] + res[:, lanes(k)].astype(jnp.float32)
            hid[k] = total
            square[...] += total * total
            write_out(k).start()

    def step(i, carry):
        @pl.when(i >= 2 * LAG)
        def _():
            add_x(i - 2 * LAG)

        @pl.when((i >= LAG) & (i < steps + LAG))
        def _():
            add_y(i - LAG)

        @pl.when(i < steps)
        def _():
            compute(i)

        return carry

    lax.fori_loop(0, steps + 2 * LAG, step, 0)

    near_core = t_at + 1 - 2 * core
    queries_core(0, near_core).wait_recv()
    queries_core(1, (near_core + 2) % 4).wait_recv()
    inv = lax.rsqrt(jnp.sum(square[...], axis=1, keepdims=True) / width + 1e-05)
    inv_lanes = jnp.broadcast_to(inv, (rows, LANES))
    square[...] = inv_lanes

    def pool(n, carry):
        for h in range(2):
            k = h * half + n
            total = jnp.sum(hid[k] * square[...], axis=0, keepdims=True)
            pooled[h : h + 1, lanes(n)] = total * gain_ref[pl.ds(k, 1), :]
        return carry

    lax.fori_loop(0, half, pool, 0)
    scale = 1.0 / math.sqrt(width * SEQ)
    count = 8 * 2 * nz
    found = jnp.zeros((8, count), f32)
    for t in range(4):
        here = pl.ds(t * share, share)
        block = every_q[t, :, :, :, :share].reshape(count, share)
        found += lax.dot_general(
            pooled[:, here],
            block,
            (((1,), (1,)), ((), ())),
            precision=high,
            preferred_element_type=f32,
        )
    found = jnp.concatenate([found, jnp.zeros((8, LANES - count), f32)], axis=1) * scale
    kept = jnp.sum(jnp.where(row == lane % 2, found, 0.0), axis=0, keepdims=True)
    kept = jnp.broadcast_to(kept, (8, LANES))
    after, before = pltpu.roll(kept, LANES - 1, 1), pltpu.roll(kept, 1, 1)
    board[group, z] = kept + jnp.where(lane % 2 == 0, after, before)

    for other in other_planes():
        scores_z(z, other).start()
    info = jnp.zeros((8, 2 * LANES), f32)
    for xs in range(2):
        for zs in range(nz):
            info += every_q[0, xs, zs, :, share:]
    ids, facts = info[:, :LANES], info[:, LANES:]
    for other in other_planes():
        scores_z(other, z).wait_recv()
    for other in other_groups():
        scores_plane(group, other).start()
    for other in other_groups():
        scores_plane(other, group).wait_recv()

    picked = jnp.zeros((8, LANES), f32)
    for zs in range(nz):
        for xs in range(2):
            for ys in range(2):
                score = board[4 * xs + 2 * ys, zs] + board[4 * xs + 2 * ys + 1, zs]
                picked += jnp.where(ids == 2 * (2 * zs + xs) + ys, score, 0.0)
    counts = jnp.broadcast_to(facts[0:1], (8, LANES))
    err = jnp.broadcast_to(picked[0:1], (8, LANES)) - picked - facts
    live = (row >= 1) & ((row - 1).astype(f32) < counts)
    err = jnp.where(live, err, 0.0)
    counts = jnp.where(counts > 0, counts, 1.0)
    nquery = Q_DEV * 2 * nz
    terms = jnp.where(lane % 2 == 0, err * err / counts, 0.0)
    loss_ref[0, 0] = jnp.sum(terms) / nquery
    weight = 2.0 * err / (counts * nquery)
    passage = (PASS_DEV * dp_at + y).astype(f32)
    at_pos = jnp.broadcast_to(jnp.where(ids[0:1] == passage, 1.0, 0.0), (8, LANES))
    at_neg = jnp.where(ids == passage, 1.0, 0.0)
    coef = jnp.sum(weight * (at_pos - at_neg), axis=0, keepdims=True)
    coef = jnp.where(row == lane % 2, jnp.broadcast_to(coef, (8, LANES)), 0.0)[:, :count]
    for t in range(4):
        here = pl.ds(t * share, share)
        block = every_q[t, :, :, :, :share].reshape(count, share)
        grad = jnp.dot(coef, block, precision=high, preferred_element_type=f32)
        pooled[:, here] = grad * scale

    def align(n, total):
        for h in range(2):
            k = h * half + n
            up = pooled[h : h + 1, lanes(n)] * gain_ref[pl.ds(k, 1), :]
            up_ref[0:1, lanes(k)] = up
            total += hid[k] * up
        return total

    total = lax.fori_loop(0, half, align, jnp.zeros((rows, LANES), f32))
    inner = jnp.sum(total, axis=1, keepdims=True) / width
    up_ref[1:, :] = jnp.zeros((7, width), f32)
    factor_ref[0] = 65536.0 * square[...]
    factor_ref[1] = jnp.broadcast_to(-65536.0 * (inv * inv * inv * inner), (rows, LANES))

    for other in other_planes():
        queries_z(z, other).wait_send()
        scores_z(z, other).wait_send()
    for other in other_groups():
        scores_plane(group, other).wait_send()
    queries_x(x).wait_send()
    queries_y(t_at).wait_send()
    for n in range(2):
        queries_core(n, t_at).wait_send()

    for s in range(RING):
        to_y(0, 0, 0, s).wait_send()
    for r in range(2):
        core_ctx(r).wait_send()
        for k in range(2):
            swap_ctx(k, r).wait_send()

    def drain(n, carry):
        zt, j = n // chunks, n % chunks
        to_core(zt, j).wait_send()
        to_x(zt, j).wait_send()

        @pl.when((zt <= z) & has_right)
        def _():
            to_right(zt, j).wait_send()

        @pl.when((zt >= z) & has_left)
        def _():
            to_left(zt, j).wait_send()

        for xt in range(2):
            write_out(piece(zt, xt, j)).wait()
        return carry

    lax.fori_loop(0, nz * chunks, drain, 0)


def tile_hidden(context, o_weight, resid, gain, queries, facts):
    rows, width = resid.shape
    depth, columns = o_weight.shape
    chunks = columns // LANES
    nz = width // (2 * columns)
    f32, bf16 = jnp.float32, jnp.bfloat16
    dma = pltpu.SemaphoreType.DMA
    return pl.pallas_call(
        functools.partial(tile_kernel, nz),
        out_shape=(
            jax.ShapeDtypeStruct((rows, width), f32),
            jax.ShapeDtypeStruct((2, rows, LANES), f32),
            jax.ShapeDtypeStruct((8, width), f32),
            jax.ShapeDtypeStruct((1, 1), f32),
        ),
        in_specs=[pl.BlockSpec(memory_space=pl.ANY)] * 3
        + [pl.BlockSpec(memory_space=pltpu.VMEM)] * 2
        + [pl.BlockSpec(memory_space=pltpu.SMEM)] * 4,
        out_specs=(
            pl.BlockSpec(memory_space=pl.ANY),
            pl.BlockSpec(memory_space=pltpu.VMEM),
            pl.BlockSpec(memory_space=pltpu.VMEM),
            pl.BlockSpec(memory_space=pltpu.SMEM),
        ),
        scratch_shapes=[
            pltpu.VMEM((2, 2, 2 * rows, depth), bf16),
            pltpu.VMEM((2, nz, chunks, depth, LANES), bf16),
            pltpu.VMEM((nz, chunks, 2, rows, LANES), f32),
            pltpu.VMEM((2 * nz * chunks, rows, LANES), f32),
            pltpu.VMEM((rows, width), bf16),
            pltpu.VMEM((RING, rows, LANES), f32),
            pltpu.VMEM((RING, rows, LANES), f32),
            dma((2,)),
            dma((2, 2)),
            dma((2, 2, 2)),
            dma((chunks,)),
            dma((nz, chunks)),
            dma((nz, chunks)),
            dma((nz, chunks)),
            dma((2, nz, chunks)),
            dma((RING,)),
            dma((nz, chunks, 2)),
            dma((nz, chunks)),
            dma((nz, chunks)),
            dma,
            dma((2 * nz * chunks,)),
            pltpu.VMEM((4, 2, nz, 2 * Q_DEV, width // 8 + 2 * LANES), f32),
            pltpu.VMEM((rows, LANES), f32),
            pltpu.VMEM((8, width // 2), f32),
            pltpu.VMEM((8, nz, 8, LANES), f32),
            dma((2, nz)),
            dma((2,)),
            dma((2,)),
            dma((2, 2)),
            dma((2, nz)),
            dma((2, 8)),
        ],
        compiler_params=pltpu.CompilerParams(
            collective_id=0, has_side_effects=True, vmem_limit_bytes=58 << 20
        ),
        cost_estimate=pl.CostEstimate(
            flops=2 * 4 * rows * depth * width, bytes_accessed=4 * rows * width, transcendentals=0
        ),
    )(context, o_weight, resid, gain, queries, *facts)


def grad_kernel(hidden_ref, factor_ref, up_ref, grad_ref):
    for n in range(grad_ref.shape[1] // LANES):
        here = pl.ds(n * LANES, LANES)
        grad_ref[:, here] = factor_ref[0] * up_ref[0:1, here] + factor_ref[1] * hidden_ref[:, here]


def gradient(hidden, factors, upward):
    rows, width = hidden.shape
    step = rows // 8
    return pl.pallas_call(
        grad_kernel,
        out_shape=jax.ShapeDtypeStruct((rows, width), jnp.float32),
        grid=(rows // step,),
        in_specs=[
            pl.BlockSpec((step, width), lambda n: (n, 0)),
            pl.BlockSpec((2, step, LANES), lambda n: (0, n, 0)),
            pl.BlockSpec((8, width), lambda n: (0, 0)),
        ],
        out_specs=pl.BlockSpec((step, width), lambda n: (n, 0)),
        compiler_params=pltpu.CompilerParams(vmem_limit_bytes=58 << 20),
    )(hidden, factors, upward)


def line_shards(
    context, resid, o_weight, norm_gain, queries, positive_ids, negative_ids, margins, pair_counts
):
    gain = norm_gain.reshape(-1, LANES)
    facts = (positive_ids, negative_ids, margins, pair_counts)
    hidden, factors, upward, loss = tile_hidden(context, o_weight, resid, gain, queries, facts)
    return (gradient(hidden, factors, upward), loss.reshape(()))


def solution(mesh):
    body = line_shards if dict(mesh.shape) == {"dp": 8, "tensor": 4} else shards
    return jax.shard_map(
        body,
        mesh=mesh,
        in_specs=(
            P("dp", "tensor"),
            P(("dp", "tensor"), None),
            P("tensor", "dp"),
            P(),
            P("dp", None),
            P("dp"),
            P("dp", None),
            P("dp", None),
            P("dp"),
        ),
        out_specs=(P(("dp", "tensor"), None), P()),
        check_vma=False,
    )
```

```python
import functools
import math

import jax
import jax.numpy as jnp
from jax import lax
from jax.experimental import pallas as pl
from jax.experimental.pallas import tpu as pltpu
from jax.sharding import PartitionSpec as P

D = 7168
SEQ = 512
PASS_DEV = 2
Q_DEV = 4
NEG = 7


def shards(
    context, resid, o_weight, norm_gain, queries, positive_ids, negative_ids, margins, pair_counts
):
    full_weight = lax.all_gather(o_weight, "dp", axis=1, tiled=True)
    tok_rows = resid.shape[0]
    attn = lax.psum_scatter(
        jnp.dot(context, full_weight, preferred_element_type=jnp.float32),
        "tensor",
        scatter_dimension=0,
        tiled=True,
    )
    hidden = resid.astype(jnp.float32) + attn
    inv = lax.rsqrt(jnp.mean(hidden * hidden, axis=-1, keepdims=True) + 1e-05)
    normed = hidden * inv * norm_gain
    first = lax.axis_index("tensor") * tok_rows
    passage_of = (first + jnp.arange(tok_rows, dtype=jnp.int32)) // SEQ
    member = (passage_of[None, :] == jnp.arange(PASS_DEV, dtype=jnp.int32)[:, None]).astype(
        jnp.float32
    )
    partial_value = jnp.dot(member, normed, precision=lax.Precision.HIGHEST)
    scale = 1.0 / jnp.sqrt(jnp.float32(D * SEQ))
    npass = PASS_DEV * lax.axis_size("dp")
    nquery = Q_DEV * lax.axis_size("dp")
    pooled = lax.psum(partial_value, "tensor")
    every_pass = lax.all_gather(pooled, "dp", axis=0, tiled=True)
    scores = jnp.dot(queries, every_pass.T, precision=lax.Precision.HIGHEST) * scale
    passes = jnp.arange(npass, dtype=jnp.int32)
    onehot_pos = (positive_ids[:, None] == passes[None, :]).astype(jnp.float32)
    onehot_neg = (negative_ids[:, :, None] == passes[None, None, :]).astype(jnp.float32)
    score_pos = jnp.sum(onehot_pos * scores, axis=-1)
    score_neg = jnp.sum(onehot_neg * scores[:, None, :], axis=-1)
    err = score_pos[:, None] - score_neg - margins
    live = (jnp.arange(NEG, dtype=jnp.int32)[None, :] < pair_counts[:, None]).astype(jnp.float32)
    counts = pair_counts.astype(jnp.float32)
    local_loss = jnp.sum(jnp.sum(live * err * err, axis=1) / counts) / nquery
    weight = 2.0 * live * err / (counts[:, None] * nquery)
    coef = onehot_pos * jnp.sum(weight, axis=1)[:, None] - jnp.sum(
        weight[:, :, None] * onehot_neg, axis=1
    )
    grad_terms = jnp.dot(coef.T, queries, precision=lax.Precision.HIGHEST) * scale
    pass_grad = lax.psum_scatter(grad_terms, "dp", scatter_dimension=0, tiled=True)
    loss = lax.psum(local_loss, "dp")
    upward = jnp.dot(member.T, pass_grad, precision=lax.Precision.HIGHEST) * norm_gain
    inner = jnp.mean(hidden * upward, axis=-1, keepdims=True)
    grad = 65536.0 * (inv * upward - hidden * inv * inv * inv * inner)
    return (grad, loss)


MESH = pl.DeviceIdType.MESH
LANES = 128
LAG = 3
RING = 6
TOP = 32600.0
FULL, LOW, SIDE = 0, 1, 2
NEAR, NEXT, END, FAR = 0, 1, 2, 3
CHUNKS = 7

MIDDLE = (
    (FULL, NEAR, 0, 0, 7),
    (FULL, NEXT, 0, 0, 4),
    (SIDE, NEAR, 0, 0, 7),
    (SIDE, NEXT, 0, 0, 4),
    (FULL, NEXT, 0, 4, 5),
    (SIDE, NEXT, 0, 4, 5),
    (FULL, NEXT, 0, 5, 6),
    (SIDE, NEXT, 0, 5, 6),
    (FULL, NEXT, 0, 6, 7),
    (SIDE, NEXT, 0, 6, 7),
    (FULL, END, 0, 0, 3),
    (FULL, NEAR, 1, 0, 4),
    (SIDE, FAR, 0, 0, 1),
    (FULL, NEAR, 1, 4, 7),
    (FULL, END, 0, 3, 4),
    (SIDE, FAR, 0, 1, 2),
    (FULL, NEXT, 1, 0, 3),
    (FULL, END, 0, 4, 5),
    (SIDE, FAR, 0, 2, 3),
    (FULL, NEXT, 1, 3, 7),
    (FULL, END, 0, 5, 6),
    (SIDE, FAR, 0, 3, 4),
    (FULL, END, 0, 6, 7),
    (FULL, END, 1, 0, 2),
    (SIDE, NEAR, 1, 0, 7),
    (SIDE, FAR, 0, 4, 5),
    (SIDE, NEXT, 1, 0, 4),
    (SIDE, FAR, 0, 5, 6),
    (SIDE, NEXT, 1, 4, 7),
    (FULL, END, 1, 2, 5),
    (SIDE, FAR, 0, 6, 7),
    (SIDE, FAR, 1, 0, 7),
    (FULL, END, 1, 5, 7),
    (FULL, FAR, 1, 0, 7),
    (FULL, FAR, 0, 0, 7),
)
ENDS = ((FULL, END, 0, 0, 7), (FULL, END, 1, 0, 7)) + tuple(
    (LOW, *run[1:]) for run in MIDDLE if run[0] == SIDE
)


def listed(runs):
    return [(kind, role, rx, j) for kind, role, rx, lo, hi in runs for j in range(lo, hi)]


def coded(tasks):
    met, last, marks = set(), -1, []
    for i, (kind, role, rx, j) in enumerate(tasks):
        new = (role, j) not in met
        met.add((role, j))
        code = j + 8 * rx + 16 * role + 64 * kind + 256 * new
        if code != last + 1 or i == 0:
            marks.append((i, code - (last + 1)))
        last = code
    return marks


def tile_kernel(
    nz,
    ctx_ref,
    weight_ref,
    resid_ref,
    gain_ref,
    query_ref,
    positive_ref,
    negative_ref,
    margin_ref,
    count_ref,
    out_ref,
    factor_ref,
    up_ref,
    loss_ref,
    ctx,
    ctx_end,
    wgt,
    from_y,
    from_x,
    side,
    hid,
    res,
    stage,
    hold,
    sums,
    ctx_load,
    ctx_core,
    ctx_x,
    end_z,
    end_x,
    w_load,
    w_end,
    w_mid,
    w_recv,
    w_core,
    y_send,
    y_recv,
    side_send,
    side_recv,
    x_send,
    x_recv,
    res_sem,
    out_sem,
    every_q,
    square,
    pooled,
    board,
    q_z,
    q_x,
    q_y,
    q_core,
    s_z,
    s_plane,
):
    dp_at, t_at = lax.axis_index("dp"), lax.axis_index("tensor")
    z, x = dp_at // 2, dp_at % 2
    y, core = t_at // 2, t_at % 2
    chunks = wgt.shape[2]
    depth = wgt.shape[3]
    low, deep = pl.ds(0, depth // 2), pl.ds(depth // 2, depth // 2)
    rows = hid.shape[1]
    group = 4 * x + t_at
    mid_z = jnp.where(z < nz // 2, 1, nz - 2)
    end_z_at = jnp.where(z < nz // 2, 0, nz - 1)
    ends = z == end_z_at
    middle = jnp.logical_not(ends)
    own = jnp.where(ends, END, NEAR)
    other_core = (dp_at, 2 * y + 1 - core)
    y_peer = (dp_at, 2 * (1 - y) + core)
    x_peer = (2 * z + 1 - x, t_at)
    end_peer = (2 * end_z_at + x, t_at)
    mid_peer = (2 * mid_z + x, t_at)
    next_peer = (2 * (nz - 1 - mid_z) + x, t_at)

    def z_peer(other):
        return (2 * other + x, t_at)

    def plane_peer(other):
        return (2 * z + other // 4, other % 4)

    def other_groups():
        return [(group + m) % 8 for m in range(1, 8)]

    def other_planes():
        return [(z + m) % nz for m in range(1, nz)]

    barrier = pltpu.get_barrier_semaphore()
    for other in other_groups():
        pl.semaphore_signal(barrier, inc=1, device_id=plane_peer(other), device_id_type=MESH)
    for other in other_planes():
        pl.semaphore_signal(barrier, inc=1, device_id=z_peer(other), device_id_type=MESH)

    def remote(src, dst, send, recv, peer):
        return pltpu.make_async_remote_copy(
            src_ref=src,
            dst_ref=dst,
            send_sem=send,
            recv_sem=recv,
            device_id=peer,
            device_id_type=MESH,
        )

    def load_weight(j):
        return pltpu.make_async_copy(
            weight_ref.at[:, pl.ds(j * LANES, LANES)], wgt.at[0, own, j], w_load.at[j]
        )

    def quarter(r, c):
        return pl.ds(pl.multiple_of((2 * ((y + r) % 2) + c) * rows, rows), rows)

    def load_ctx(r):
        return pltpu.make_async_copy(
            ctx_ref.at[quarter(r, core)], ctx.at[0, 0, pl.ds(r * rows, rows)], ctx_load.at[r]
        )

    def core_ctx(r):
        return remote(
            ctx_ref.at[quarter(r, 1 - core)],
            ctx.at[1, 0, pl.ds(r * rows, rows)],
            ctx_core.at[0, r],
            ctx_core.at[1, r],
            other_core,
        )

    def swap_ctx(k, r):
        block = pl.ds(r * rows, rows)
        return remote(
            ctx.at[k, 0, block], ctx.at[k, 1, block], ctx_x.at[0, k, r], ctx_x.at[1, k, r], x_peer
        )

    def lend_ctx(k):
        return remote(
            ctx.at[k, 0, :, deep], ctx_end.at[k, 0], end_z.at[0, k], end_z.at[1, k], mid_peer
        )

    def lend_swap(k):
        return remote(
            ctx_end.at[k, 0], ctx_end.at[k, 1], end_x.at[0, k], end_x.at[1, k], x_peer
        )

    def to_end(role, j):
        return remote(
            wgt.at[0, role, j, low],
            wgt.at[0, role, j, low],
            w_end.at[role, j],
            w_recv.at[role, j],
            end_peer,
        )

    def to_next(role, j):
        return remote(
            wgt.at[0, role, j],
            wgt.at[0, role + 1, j],
            w_mid.at[role, j],
            w_recv.at[role + 1, j],
            next_peer,
        )

    def to_mid(j):
        return remote(
            wgt.at[0, END, j], wgt.at[0, END, j], w_mid.at[END, j], w_recv.at[END, j], mid_peer
        )

    def to_core(role, j):
        return remote(
            wgt.at[0, role, j],
            wgt.at[1, role, j],
            w_core.at[0, role, j],
            w_core.at[1, role, j],
            other_core,
        )

    def to_core_low(role, j):
        return remote(
            wgt.at[0, role, j, low],
            wgt.at[1, role, j, low],
            w_core.at[0, role, j],
            w_core.at[1, role, j],
            other_core,
        )

    def to_y(role, j, rx, slot):
        return remote(
            stage.at[slot], from_y.at[role, j, rx], y_send.at[slot], y_recv.at[role, j, rx], y_peer
        )

    def place(role):
        return jnp.minimum(role, 2)

    def side_to_y(role, j, rx, slot):
        at = place(role)
        return remote(
            stage.at[slot], side.at[at, j, rx], y_send.at[slot], side_recv.at[at, j, rx], y_peer
        )

    def side_to_end(role, j, rx):
        at = place(role)
        return remote(
            side.at[at, j, rx],
            side.at[at, j, rx],
            side_send.at[at, j, rx],
            side_recv.at[at, j, rx],
            end_peer,
        )

    def piece(role, xt, j):
        first = jnp.where(role < END, mid_z, end_z_at)
        zt = jnp.where(role % 2 == 0, first, nz - 1 - first)
        return (2 * zt + xt) * chunks + j

    def to_x(role, j):
        return remote(
            from_y.at[role, j, 1], from_x.at[role, j], x_send.at[role, j], x_recv.at[role, j], x_peer
        )

    def lanes(k):
        return pl.ds(pl.multiple_of(k * LANES, LANES), LANES)

    def write_out(k):
        return pltpu.make_async_copy(hid.at[k], out_ref.at[:, lanes(k)], out_sem.at[k])

    def scale_of(level):
        return jnp.exp2(level * (1.0 / 128.0)) * (1.0 / TOP)

    def pack(ref, value):
        top = jnp.maximum(jnp.max(jnp.abs(value), axis=0, keepdims=True), 1e-30)
        level = jnp.ceil(jnp.log2(top) * 128.0)
        ref[:rows] = jnp.round(value * (1.0 / scale_of(level))).astype(jnp.int32).astype(jnp.int16)
        level = jnp.broadcast_to(level, (16, LANES))
        ref[rows:] = level.astype(jnp.int32).astype(jnp.int16)

    def unpack(ref):
        level = ref[rows:].astype(jnp.int32).astype(jnp.float32)[:1]
        return ref[:rows].astype(jnp.int32).astype(jnp.float32) * scale_of(level)

    load_res = pltpu.make_async_copy(resid_ref, res, res_sem)

    def queries_z(source, target):
        mine = every_q.at[t_at, x, source]
        return remote(mine, mine, q_z.at[0, target], q_z.at[1, source], z_peer(target))

    def queries_x(xs):
        mine = every_q.at[t_at, xs]
        return remote(mine, mine, q_x.at[0], q_x.at[1], x_peer)

    def queries_y(ts):
        return remote(every_q.at[ts], every_q.at[ts], q_y.at[0], q_y.at[1], y_peer)

    def queries_core(n, ts):
        return remote(
            every_q.at[ts], every_q.at[ts], q_core.at[0, n], q_core.at[1, n], other_core
        )

    def scores_z(source, target):
        mine = board.at[group, source]
        return remote(mine, mine, s_z.at[0, target], s_z.at[1, source], z_peer(target))

    def scores_plane(source, target):
        return remote(
            board.at[source],
            board.at[source],
            s_plane.at[0, target],
            s_plane.at[1, source],
            plane_peer(target),
        )

    for j in range(chunks):
        load_weight(j).start()
    for r in range(2):
        load_ctx(r).start()
    load_res.start()
    square[...] = jnp.zeros_like(square)
    pooled[...] = jnp.zeros_like(pooled)

    f32, high = jnp.float32, lax.Precision.HIGHEST
    width = 2 * nz * chunks * LANES
    half, share = nz * chunks, every_q.shape[4] - 2 * LANES
    row = lax.broadcasted_iota(jnp.int32, (8, LANES), 0)
    lane = lax.broadcasted_iota(jnp.int32, (8, LANES), 1)
    own_q = every_q.at[t_at, x, z]
    at = lane - 8 * (nz * x + z)
    ids = jnp.zeros((8, LANES), f32)
    facts = jnp.zeros((8, LANES), f32)
    for r in range(Q_DEV):
        for h in range(2):
            part = pl.ds(pl.multiple_of(h * (width // 2) + t_at * share, LANES), share)
            own_q[2 * r + h : 2 * r + h + 1, :share] = query_ref[r : r + 1, part]
        mine = (at == 2 * r) | (at == 2 * r + 1)
        ids = jnp.where(mine & (row == 0), positive_ref[r].astype(f32), ids)
        facts = jnp.where(mine & (row == 0), count_ref[r].astype(f32), facts)
        for k in range(NEG):
            ids = jnp.where(mine & (row == k + 1), negative_ref[r, k].astype(f32), ids)
            facts = jnp.where(mine & (row == k + 1), margin_ref[r, k], facts)
    own_q[:, share : share + LANES] = ids
    own_q[:, share + LANES :] = facts
    pl.semaphore_wait(barrier, 7 + nz - 1)
    for other in other_planes():
        queries_z(z, other).start()
    for r in range(2):
        core_ctx(r).start()
    for r in range(2):
        load_ctx(r).wait()
        swap_ctx(0, r).start()

    @pl.when(ends)
    def _():
        lend_ctx(0).start()

    for r in range(2):
        core_ctx(r).wait_recv()
        swap_ctx(1, r).start()

    @pl.when(ends)
    def _():
        lend_ctx(1).start()

    for j in range(chunks):
        load_weight(j).wait()

        @pl.when(ends)
        def _():
            to_mid(j).start()

        @pl.when(middle)
        def _():
            to_end(NEAR, j).start()
            to_next(NEAR, j).start()

        to_core(own, j).start()
    load_res.wait()

    mid_tasks, end_tasks = listed(MIDDLE), listed(ENDS)
    mid_marks, end_marks = coded(mid_tasks), coded(end_tasks)
    steps = jnp.where(ends, len(end_tasks), len(mid_tasks))
    lent = mid_tasks.index((SIDE, NEAR, 0, 0))
    swapped = jnp.where(ends, chunks, mid_tasks.index((FULL, NEAR, 1, 0)))
    lent_swapped = mid_tasks.index((SIDE, NEAR, 1, 0))
    spread = jnp.where(ends, 2 * chunks, lent_swapped)
    spread_core = jnp.where(ends, 5 * chunks, mid_tasks.index((FULL, FAR, 1, 0)))

    def task(i):
        mid_code, end_code = i, i
        for start, more in mid_marks:
            mid_code += jnp.where(i >= start, more, 0)
        for start, more in end_marks:
            end_code += jnp.where(i >= start, more, 0)
        code = jnp.where(ends, end_code, mid_code)
        return code // 64 % 4, code // 16 % 4, code % 8, code // 8 % 2, code // 256

    def compute(i):
        kind, role, j, rx, new = task(i)
        slot = i % RING

        @pl.when((new == 1) & (role != own) & middle)
        def _():
            arriving = remote(
                wgt.at[0, role, j],
                wgt.at[0, role, j],
                w_mid.at[role, j],
                w_recv.at[role, j],
                next_peer,
            )
            arriving.wait_recv()

            @pl.when(role == END)
            def _():
                to_next(END, j).start()

            @pl.when(role != END)
            def _():
                to_end(role, j).start()

            to_core(role, j).start()

        @pl.when((new == 1) & (role != own) & ends)
        def _():
            to_end(role, j).wait_recv()
            to_core_low(role, j).start()

        @pl.when((new == 1) & (middle | (role == own)))
        def _():
            to_core(role, j).wait_recv()

        @pl.when((new == 1) & ends & (role != own))
        def _():
            to_core_low(role, j).wait_recv()

        @pl.when(middle & (i == lent))
        def _():
            for k in range(2):
                lend_ctx(k).wait_recv()
                lend_swap(k).start()

        @pl.when(middle & (i == lent_swapped))
        def _():
            for k in range(2):
                lend_swap(k).wait_recv()

        @pl.when(i == swapped)
        def _():
            for k in range(2):
                for r in range(2):
                    swap_ctx(k, r).wait_recv()
            for other in other_planes():
                queries_z(other, z).wait_recv()
            queries_x(x).start()

        @pl.when(i == spread)
        def _():
            queries_x(1 - x).wait_recv()
            queries_y(t_at).start()
            queries_core(0, t_at).start()

        @pl.when(i == spread_core)
        def _():
            queries_y((t_at + 2) % 4).wait_recv()
            queries_core(1, (t_at + 2) % 4).start()

        def product(acts, block):
            return jnp.dot(acts, block, preferred_element_type=f32)

        @pl.when(kind == FULL)
        def _():
            sums[...] = product(ctx[0, rx], wgt[0, role, j]) + product(ctx[1, rx], wgt[1, role, j])

        @pl.when(kind == LOW)
        def _():
            sums[...] = product(ctx[0, rx, :, low], wgt[0, role, j, low]) + product(
                ctx[1, rx, :, low], wgt[1, role, j, low]
            )

        @pl.when(kind == SIDE)
        def _():
            sums[...] = product(ctx_end[0, rx], wgt[0, role, j, deep]) + product(
                ctx_end[1, rx], wgt[1, role, j, deep]
            )

        @pl.when(i >= RING)
        def _():
            to_y(role, j, rx, slot).wait_send()

        pack(stage.at[slot], sums[rows:])
        hold[slot] = sums[:rows]

        @pl.when(kind == SIDE)
        def _():
            side_to_y(role, j, rx, slot).start()

        @pl.when(kind != SIDE)
        def _():
            to_y(role, j, rx, slot).start()

    def settle(k, total):
        total = total + res[:, lanes(k)].astype(f32)
        hid[k] = total
        square[...] += total * total
        write_out(k).start()

    def add_y(i):
        kind, role, j, rx, _ = task(i)
        slot = i % RING
        at = place(role)

        @pl.when(kind == SIDE)
        def _():
            side_to_y(role, j, rx, slot).wait_recv()
            pack(side.at[at, j, rx], hold[slot] + unpack(side.at[at, j, rx]))
            side_to_end(role, j, rx).start()

        @pl.when(kind != SIDE)
        def _():
            to_y(role, j, rx, slot).wait_recv()

        @pl.when(kind == LOW)
        def _():
            side_to_end(role, j, rx).wait_recv()
            hold[slot] += unpack(side.at[at, j, rx])

        @pl.when((kind != SIDE) & (rx == 0))
        def _():
            settle(piece(role, x, j), hold[slot] + unpack(from_y.at[role, j, 0]))

        @pl.when((kind != SIDE) & (rx == 1))
        def _():
            pack(from_y.at[role, j, 1], hold[slot] + unpack(from_y.at[role, j, 1]))
            to_x(role, j).start()

    def add_x(i):
        kind, role, j, rx, _ = task(i)

        @pl.when((kind != SIDE) & (rx == 1))
        def _():
            to_x(role, j).wait_recv()
            settle(piece(role, 1 - x, j), unpack(from_x.at[role, j]))

    def step(i, carry):
        @pl.when(i >= 2 * LAG)
        def _():
            add_x(i - 2 * LAG)

        @pl.when((i >= LAG) & (i < steps + LAG))
        def _():
            add_y(i - LAG)

        @pl.when(i < steps)
        def _():
            compute(i)

        return carry

    lax.fori_loop(0, steps + 2 * LAG, step, 0)

    near_core = t_at + 1 - 2 * core
    queries_core(0, near_core).wait_recv()
    queries_core(1, (near_core + 2) % 4).wait_recv()
    inv = lax.rsqrt(jnp.sum(square[...], axis=1, keepdims=True) / width + 1e-05)
    inv_lanes = jnp.broadcast_to(inv, (rows, LANES))
    square[...] = inv_lanes

    def pool(n, carry):
        for h in range(2):
            k = h * half + n
            total = jnp.sum(hid[k] * square[...], axis=0, keepdims=True)
            pooled[h : h + 1, lanes(n)] = total * gain_ref[pl.ds(k, 1), :]
        return carry

    lax.fori_loop(0, half, pool, 0)
    scale = 1.0 / math.sqrt(width * SEQ)
    count = 8 * 2 * nz
    found = jnp.zeros((8, count), f32)
    for t in range(4):
        here = pl.ds(t * share, share)
        block = every_q[t, :, :, :, :share].reshape(count, share)
        found += lax.dot_general(
            pooled[:, here],
            block,
            (((1,), (1,)), ((), ())),
            precision=high,
            preferred_element_type=f32,
        )
    found = jnp.concatenate([found, jnp.zeros((8, LANES - count), f32)], axis=1) * scale
    kept = jnp.sum(jnp.where(row == lane % 2, found, 0.0), axis=0, keepdims=True)
    kept = jnp.broadcast_to(kept, (8, LANES))
    after, before = pltpu.roll(kept, LANES - 1, 1), pltpu.roll(kept, 1, 1)
    board[group, z] = kept + jnp.where(lane % 2 == 0, after, before)

    for other in other_planes():
        scores_z(z, other).start()
    info = jnp.zeros((8, 2 * LANES), f32)
    for xs in range(2):
        for zs in range(nz):
            info += every_q[0, xs, zs, :, share:]
    ids, facts = info[:, :LANES], info[:, LANES:]
    for other in other_planes():
        scores_z(other, z).wait_recv()
    for other in other_groups():
        scores_plane(group, other).start()
    for other in other_groups():
        scores_plane(other, group).wait_recv()

    picked = jnp.zeros((8, LANES), f32)
    for zs in range(nz):
        for xs in range(2):
            for ys in range(2):
                score = board[4 * xs + 2 * ys, zs] + board[4 * xs + 2 * ys + 1, zs]
                picked += jnp.where(ids == 2 * (2 * zs + xs) + ys, score, 0.0)
    counts = jnp.broadcast_to(facts[0:1], (8, LANES))
    err = jnp.broadcast_to(picked[0:1], (8, LANES)) - picked - facts
    live = (row >= 1) & ((row - 1).astype(f32) < counts)
    err = jnp.where(live, err, 0.0)
    counts = jnp.where(counts > 0, counts, 1.0)
    nquery = Q_DEV * 2 * nz
    terms = jnp.where(lane % 2 == 0, err * err / counts, 0.0)
    loss_ref[0, 0] = jnp.sum(terms) / nquery
    weight = 2.0 * err / (counts * nquery)
    passage = (PASS_DEV * dp_at + y).astype(f32)
    at_pos = jnp.broadcast_to(jnp.where(ids[0:1] == passage, 1.0, 0.0), (8, LANES))
    at_neg = jnp.where(ids == passage, 1.0, 0.0)
    coef = jnp.sum(weight * (at_pos - at_neg), axis=0, keepdims=True)
    coef = jnp.where(row == lane % 2, jnp.broadcast_to(coef, (8, LANES)), 0.0)[:, :count]
    for t in range(4):
        here = pl.ds(t * share, share)
        block = every_q[t, :, :, :, :share].reshape(count, share)
        grad = jnp.dot(coef, block, precision=high, preferred_element_type=f32)
        pooled[:, here] = grad * scale

    def align(n, total):
        for h in range(2):
            k = h * half + n
            up = pooled[h : h + 1, lanes(n)] * gain_ref[pl.ds(k, 1), :]
            up_ref[0:1, lanes(k)] = up
            total += hid[k] * up
        return total

    total = lax.fori_loop(0, half, align, jnp.zeros((rows, LANES), f32))
    inner = jnp.sum(total, axis=1, keepdims=True) / width
    up_ref[1:, :] = jnp.zeros((7, width), f32)
    factor_ref[0] = 65536.0 * square[...]
    factor_ref[1] = jnp.broadcast_to(-65536.0 * (inv * inv * inv * inner), (rows, LANES))

    for other in other_planes():
        queries_z(z, other).wait_send()
        scores_z(z, other).wait_send()
    for other in other_groups():
        scores_plane(group, other).wait_send()
    queries_x(x).wait_send()
    queries_y(t_at).wait_send()
    for n in range(2):
        queries_core(n, t_at).wait_send()

    for n in range(RING):
        to_y(0, 0, 0, n).wait_send()
    for r in range(2):
        core_ctx(r).wait_send()
        for k in range(2):
            swap_ctx(k, r).wait_send()

    @pl.when(ends)
    def _():
        for k in range(2):
            lend_ctx(k).wait_send()

    @pl.when(middle)
    def _():
        for k in range(2):
            lend_swap(k).wait_send()

    def drain(j, carry):
        for role in (NEAR, NEXT, END, FAR):
            to_x(role, j).wait_send()
            for xt in range(2):
                write_out(piece(role, xt, j)).wait()
        to_core(END, j).wait_send()

        @pl.when(ends)
        def _():
            to_mid(j).wait_send()
            for role in (NEAR, NEXT, FAR):
                to_core_low(role, j).wait_send()

        @pl.when(middle)
        def _():
            for role in (NEAR, END):
                to_next(role, j).wait_send()
            for role in (NEAR, NEXT, FAR):
                to_core(role, j).wait_send()
                to_end(role, j).wait_send()
                for rx in range(2):
                    side_to_end(role, j, rx).wait_send()

        return carry

    lax.fori_loop(0, chunks, drain, 0)


def tile_hidden(context, o_weight, resid, gain, queries, facts):
    rows, width = resid.shape
    depth, columns = o_weight.shape
    chunks = columns // LANES
    nz = width // (2 * columns)
    f32, bf16 = jnp.float32, jnp.bfloat16
    coded_rows = rows + 16
    dma = pltpu.SemaphoreType.DMA
    return pl.pallas_call(
        functools.partial(tile_kernel, nz),
        out_shape=(
            jax.ShapeDtypeStruct((rows, width), f32),
            jax.ShapeDtypeStruct((2, rows, LANES), f32),
            jax.ShapeDtypeStruct((8, width), f32),
            jax.ShapeDtypeStruct((1, 1), f32),
        ),
        in_specs=[pl.BlockSpec(memory_space=pl.ANY)] * 3
        + [pl.BlockSpec(memory_space=pltpu.VMEM)] * 2
        + [pl.BlockSpec(memory_space=pltpu.SMEM)] * 4,
        out_specs=(
            pl.BlockSpec(memory_space=pl.ANY),
            pl.BlockSpec(memory_space=pltpu.VMEM),
            pl.BlockSpec(memory_space=pltpu.VMEM),
            pl.BlockSpec(memory_space=pltpu.SMEM),
        ),
        scratch_shapes=[
            pltpu.VMEM((2, 2, 2 * rows, depth), bf16),
            pltpu.VMEM((2, 2, 2 * rows, depth // 2), bf16),
            pltpu.VMEM((2, nz, chunks, depth, LANES), bf16),
            pltpu.VMEM((nz, chunks, 2, coded_rows, LANES), jnp.int16),
            pltpu.VMEM((nz, chunks, coded_rows, LANES), jnp.int16),
            pltpu.VMEM((nz - 1, chunks, 2, coded_rows, LANES), jnp.int16),
            pltpu.VMEM((2 * nz * chunks, rows, LANES), f32),
            pltpu.VMEM((rows, width), bf16),
            pltpu.VMEM((RING, coded_rows, LANES), jnp.int16),
            pltpu.VMEM((RING, rows, LANES), f32),
            pltpu.VMEM((2 * rows, LANES), f32),
            dma((2,)),
            dma((2, 2)),
            dma((2, 2, 2)),
            dma((2, 2)),
            dma((2, 2)),
            dma((chunks,)),
            dma((nz, chunks)),
            dma((nz, chunks)),
            dma((nz, chunks)),
            dma((2, nz, chunks)),
            dma((RING,)),
            dma((nz, chunks, 2)),
            dma((nz - 1, chunks, 2)),
            dma((nz - 1, chunks, 2)),
            dma((nz, chunks)),
            dma((nz, chunks)),
            dma,
            dma((2 * nz * chunks,)),
            pltpu.VMEM((4, 2, nz, 2 * Q_DEV, width // 8 + 2 * LANES), f32),
            pltpu.VMEM((rows, LANES), f32),
            pltpu.VMEM((8, width // 2), f32),
            pltpu.VMEM((8, nz, 8, LANES), f32),
            dma((2, nz)),
            dma((2,)),
            dma((2,)),
            dma((2, 2)),
            dma((2, nz)),
            dma((2, 8)),
        ],
        compiler_params=pltpu.CompilerParams(
            collective_id=0, has_side_effects=True, vmem_limit_bytes=58 << 20
        ),
        cost_estimate=pl.CostEstimate(
            flops=2 * 4 * rows * depth * width, bytes_accessed=4 * rows * width, transcendentals=0
        ),
    )(context, o_weight, resid, gain, queries, *facts)


def grad_kernel(hidden_ref, factor_ref, up_ref, grad_ref):
    for n in range(grad_ref.shape[1] // LANES):
        here = pl.ds(n * LANES, LANES)
        grad_ref[:, here] = factor_ref[0] * up_ref[0:1, here] + factor_ref[1] * hidden_ref[:, here]


def gradient(hidden, factors, upward):
    rows, width = hidden.shape
    step = rows // 8
    return pl.pallas_call(
        grad_kernel,
        out_shape=jax.ShapeDtypeStruct((rows, width), jnp.float32),
        grid=(rows // step,),
        in_specs=[
            pl.BlockSpec((step, width), lambda n: (n, 0)),
            pl.BlockSpec((2, step, LANES), lambda n: (0, n, 0)),
            pl.BlockSpec((8, width), lambda n: (0, 0)),
        ],
        out_specs=pl.BlockSpec((step, width), lambda n: (n, 0)),
        compiler_params=pltpu.CompilerParams(vmem_limit_bytes=58 << 20),
    )(hidden, factors, upward)


def line_shards(
    context, resid, o_weight, norm_gain, queries, positive_ids, negative_ids, margins, pair_counts
):
    gain = norm_gain.reshape(-1, LANES)
    facts = (positive_ids, negative_ids, margins, pair_counts)
    hidden, factors, upward, loss = tile_hidden(context, o_weight, resid, gain, queries, facts)
    return (gradient(hidden, factors, upward), loss.reshape(()))


def solution(mesh):
    body = line_shards if dict(mesh.shape) == {"dp": 8, "tensor": 4} else shards
    return jax.shard_map(
        body,
        mesh=mesh,
        in_specs=(
            P("dp", "tensor"),
            P(("dp", "tensor"), None),
            P("tensor", "dp"),
            P(),
            P("dp", None),
            P("dp"),
            P("dp", None),
            P("dp", None),
            P("dp"),
        ),
        out_specs=(P(("dp", "tensor"), None), P()),
        check_vma=False,
    )
```

```python
import functools
import math

import jax
import jax.numpy as jnp
from jax import lax
from jax.experimental import pallas as pl
from jax.experimental.pallas import tpu as pltpu
from jax.sharding import PartitionSpec as P

D = 7168
SEQ = 512
PASS_DEV = 2
Q_DEV = 4
NEG = 7


def shards(
    context, resid, o_weight, norm_gain, queries, positive_ids, negative_ids, margins, pair_counts
):
    full_weight = lax.all_gather(o_weight, "dp", axis=1, tiled=True)
    tok_rows = resid.shape[0]
    attn = lax.psum_scatter(
        jnp.dot(context, full_weight, preferred_element_type=jnp.float32),
        "tensor",
        scatter_dimension=0,
        tiled=True,
    )
    hidden = resid.astype(jnp.float32) + attn
    inv = lax.rsqrt(jnp.mean(hidden * hidden, axis=-1, keepdims=True) + 1e-05)
    normed = hidden * inv * norm_gain
    first = lax.axis_index("tensor") * tok_rows
    passage_of = (first + jnp.arange(tok_rows, dtype=jnp.int32)) // SEQ
    member = (passage_of[None, :] == jnp.arange(PASS_DEV, dtype=jnp.int32)[:, None]).astype(
        jnp.float32
    )
    partial_value = jnp.dot(member, normed, precision=lax.Precision.HIGHEST)
    scale = 1.0 / jnp.sqrt(jnp.float32(D * SEQ))
    npass = PASS_DEV * lax.axis_size("dp")
    nquery = Q_DEV * lax.axis_size("dp")
    pooled = lax.psum(partial_value, "tensor")
    every_pass = lax.all_gather(pooled, "dp", axis=0, tiled=True)
    scores = jnp.dot(queries, every_pass.T, precision=lax.Precision.HIGHEST) * scale
    passes = jnp.arange(npass, dtype=jnp.int32)
    onehot_pos = (positive_ids[:, None] == passes[None, :]).astype(jnp.float32)
    onehot_neg = (negative_ids[:, :, None] == passes[None, None, :]).astype(jnp.float32)
    score_pos = jnp.sum(onehot_pos * scores, axis=-1)
    score_neg = jnp.sum(onehot_neg * scores[:, None, :], axis=-1)
    err = score_pos[:, None] - score_neg - margins
    live = (jnp.arange(NEG, dtype=jnp.int32)[None, :] < pair_counts[:, None]).astype(jnp.float32)
    counts = pair_counts.astype(jnp.float32)
    local_loss = jnp.sum(jnp.sum(live * err * err, axis=1) / counts) / nquery
    weight = 2.0 * live * err / (counts[:, None] * nquery)
    coef = onehot_pos * jnp.sum(weight, axis=1)[:, None] - jnp.sum(
        weight[:, :, None] * onehot_neg, axis=1
    )
    grad_terms = jnp.dot(coef.T, queries, precision=lax.Precision.HIGHEST) * scale
    pass_grad = lax.psum_scatter(grad_terms, "dp", scatter_dimension=0, tiled=True)
    loss = lax.psum(local_loss, "dp")
    upward = jnp.dot(member.T, pass_grad, precision=lax.Precision.HIGHEST) * norm_gain
    inner = jnp.mean(hidden * upward, axis=-1, keepdims=True)
    grad = 65536.0 * (inv * upward - hidden * inv * inv * inv * inner)
    return (grad, loss)


MESH = pl.DeviceIdType.MESH
LANES = 128
LAG = 3
LAG_X = (24, 6)
RING = 6
TOP = 32600.0
FULL, LOW, SIDE = 0, 1, 2
NEAR, NEXT, END, FAR = 0, 1, 2, 3
CHUNKS = 7

MIDDLE = (
    (FULL, NEAR, 0, 0, 7),
    (FULL, NEXT, 0, 0, 3),
    (SIDE, NEXT, 0, 0, 4),
    (FULL, NEXT, 0, 3, 4),
    (FULL, END, 0, 0, 1),
    (SIDE, NEXT, 0, 4, 5),
    (FULL, NEXT, 0, 4, 5),
    (FULL, END, 0, 1, 2),
    (SIDE, NEXT, 0, 5, 6),
    (FULL, NEXT, 0, 5, 6),
    (FULL, END, 0, 2, 3),
    (SIDE, NEXT, 0, 6, 7),
    (FULL, NEXT, 0, 6, 7),
    (FULL, NEAR, 1, 0, 4),
    (SIDE, FAR, 0, 0, 1),
    (FULL, NEAR, 1, 4, 7),
    (FULL, NEXT, 1, 0, 2),
    (SIDE, FAR, 0, 1, 2),
    (FULL, NEXT, 1, 2, 7),
    (SIDE, FAR, 0, 2, 3),
    (FULL, END, 1, 0, 5),
    (SIDE, FAR, 0, 3, 4),
    (FULL, END, 1, 5, 6),
    (SIDE, NEXT, 1, 0, 7),
    (SIDE, FAR, 1, 0, 6),
    (SIDE, FAR, 0, 4, 6),
    (FULL, END, 1, 6, 7),
    (FULL, FAR, 1, 0, 1),
    (SIDE, FAR, 1, 6, 7),
    (SIDE, FAR, 0, 6, 7),
    (FULL, FAR, 1, 1, 7),
    (FULL, END, 0, 3, 7),
    (FULL, FAR, 0, 0, 7),
)

ENDS = (
    (FULL, END, 0, 0, 7),
    (FULL, NEAR, 0, 0, 7),
    (FULL, END, 1, 0, 7),
    (FULL, NEAR, 1, 0, 7),
    (LOW, NEXT, 0, 0, 7),
    (LOW, FAR, 0, 0, 4),
    (LOW, NEXT, 1, 0, 7),
    (LOW, FAR, 1, 0, 6),
    (LOW, FAR, 0, 4, 6),
    (LOW, FAR, 1, 6, 7),
    (LOW, FAR, 0, 6, 7),
)

MIDDLE_RELAYS = (
    (6, NEXT, 0),
    (8, NEXT, 1),
    (9, NEXT, 2),
    (13, NEXT, 3),
    (15, END, 0),
    (15, NEXT, 4),
    (18, END, 1),
    (18, NEXT, 5),
    (21, END, 2),
    (21, NEXT, 6),
    (25, END, 3),
    (26, FAR, 0),
    (31, END, 4),
    (32, FAR, 1),
    (37, END, 5),
    (38, FAR, 2),
    (43, END, 6),
    (44, FAR, 3),
    (49, FAR, 4),
    (57, FAR, 5),
    (63, FAR, 6),
)
END_RELAYS = (
    (5, NEAR, 0),
    (6, NEAR, 1),
    (7, NEAR, 2),
    (8, NEAR, 3),
    (9, NEAR, 4),
    (10, NEAR, 5),
    (11, NEAR, 6),
    (15, NEXT, 0),
    (16, NEXT, 1),
    (19, NEXT, 2),
    (22, NEXT, 3),
    (27, NEXT, 4),
    (31, NEXT, 5),
    (32, NEXT, 6),
    (33, FAR, 0),
    (34, FAR, 1),
    (35, FAR, 2),
    (36, FAR, 3),
    (41, FAR, 4),
    (49, FAR, 5),
    (52, FAR, 6),
)
LENT = 10


def listed(runs):
    return [(kind, role, rx, j) for kind, role, rx, lo, hi in runs for j in range(lo, hi)]


def coded(tasks):
    met, last, marks = set(), -1, []
    for i, (kind, role, rx, j) in enumerate(tasks):
        new = (role, j) not in met
        met.add((role, j))
        code = j + 8 * rx + 16 * role + 64 * kind + 256 * new
        if code != last + 1 or i == 0:
            marks.append((i, code - (last + 1)))
        last = code
    return marks


def events(relays):
    first, second, steps = [], [], set()
    for step, role, j in relays:
        (second if step in steps else first).append((step, 8 * role + j + 1))
        steps.add(step)
    return first, second


def tile_kernel(
    nz,
    ctx_ref,
    weight_ref,
    resid_ref,
    gain_ref,
    query_ref,
    positive_ref,
    negative_ref,
    margin_ref,
    count_ref,
    out_ref,
    factor_ref,
    up_ref,
    loss_ref,
    ctx,
    ctx_end,
    wgt,
    from_y,
    from_x,
    side,
    hid,
    res,
    stage,
    hold,
    sums,
    ctx_load,
    ctx_core,
    ctx_x,
    end_z,
    end_x,
    w_load,
    w_end,
    w_mid,
    w_recv,
    w_core,
    y_send,
    y_recv,
    side_send,
    side_recv,
    x_send,
    x_recv,
    res_sem,
    out_sem,
    every_q,
    square,
    pooled,
    board,
    q_z,
    q_x,
    q_y,
    q_core,
    s_z,
    s_plane,
):
    dp_at, t_at = lax.axis_index("dp"), lax.axis_index("tensor")
    z, x = dp_at // 2, dp_at % 2
    y, core = t_at // 2, t_at % 2
    chunks = wgt.shape[2]
    depth = wgt.shape[3]
    low, deep = pl.ds(0, depth // 2), pl.ds(depth // 2, depth // 2)
    rows = hid.shape[1]
    group = 4 * x + t_at
    mid_z = jnp.where(z < nz // 2, 1, nz - 2)
    end_z_at = jnp.where(z < nz // 2, 0, nz - 1)
    ends = z == end_z_at
    middle = jnp.logical_not(ends)
    own = jnp.where(ends, END, NEAR)
    other_core = (dp_at, 2 * y + 1 - core)
    y_peer = (dp_at, 2 * (1 - y) + core)
    x_peer = (2 * z + 1 - x, t_at)
    end_peer = (2 * end_z_at + x, t_at)
    mid_peer = (2 * mid_z + x, t_at)
    next_peer = (2 * (nz - 1 - mid_z) + x, t_at)

    def z_peer(other):
        return (2 * other + x, t_at)

    def plane_peer(other):
        return (2 * z + other // 4, other % 4)

    def other_groups():
        return [(group + m) % 8 for m in range(1, 8)]

    def other_planes():
        return [(z + m) % nz for m in range(1, nz)]

    barrier = pltpu.get_barrier_semaphore()
    for other in other_groups():
        pl.semaphore_signal(barrier, inc=1, device_id=plane_peer(other), device_id_type=MESH)
    for other in other_planes():
        pl.semaphore_signal(barrier, inc=1, device_id=z_peer(other), device_id_type=MESH)

    def remote(src, dst, send, recv, peer):
        return pltpu.make_async_remote_copy(
            src_ref=src,
            dst_ref=dst,
            send_sem=send,
            recv_sem=recv,
            device_id=peer,
            device_id_type=MESH,
        )

    def load_weight(j):
        return pltpu.make_async_copy(
            weight_ref.at[:, pl.ds(j * LANES, LANES)], wgt.at[0, own, j], w_load.at[j]
        )

    def quarter(r, c):
        return pl.ds(pl.multiple_of((2 * ((y + r) % 2) + c) * rows, rows), rows)

    def load_ctx(r):
        return pltpu.make_async_copy(
            ctx_ref.at[quarter(r, core)], ctx.at[0, 0, pl.ds(r * rows, rows)], ctx_load.at[r]
        )

    def core_ctx(r):
        return remote(
            ctx_ref.at[quarter(r, 1 - core)],
            ctx.at[1, 0, pl.ds(r * rows, rows)],
            ctx_core.at[0, r],
            ctx_core.at[1, r],
            other_core,
        )

    def swap_ctx(k, r):
        block = pl.ds(r * rows, rows)
        return remote(
            ctx.at[k, 0, block], ctx.at[k, 1, block], ctx_x.at[0, k, r], ctx_x.at[1, k, r], x_peer
        )

    def lend_ctx(k):
        return remote(
            ctx.at[k, 0, :, deep], ctx_end.at[k, 0], end_z.at[0, k], end_z.at[1, k], mid_peer
        )

    def lend_swap(k):
        return remote(
            ctx_end.at[k, 0], ctx_end.at[k, 1], end_x.at[0, k], end_x.at[1, k], x_peer
        )

    def to_end(role, j):
        return remote(
            wgt.at[0, role, j, low],
            wgt.at[0, role, j, low],
            w_end.at[role, j],
            w_recv.at[role, j],
            end_peer,
        )

    def to_end_whole(j):
        return remote(
            wgt.at[0, NEAR, j], wgt.at[0, NEAR, j], w_end.at[NEAR, j], w_recv.at[NEAR, j], end_peer
        )

    def to_next(role, j):
        return remote(
            wgt.at[0, role, j],
            wgt.at[0, role + 1, j],
            w_mid.at[role, j],
            w_recv.at[role + 1, j],
            next_peer,
        )

    def to_mid(j):
        return remote(
            wgt.at[0, END, j], wgt.at[0, END, j], w_mid.at[END, j], w_recv.at[END, j], mid_peer
        )

    def to_core(role, j):
        return remote(
            wgt.at[0, role, j],
            wgt.at[1, role, j],
            w_core.at[0, role, j],
            w_core.at[1, role, j],
            other_core,
        )

    def to_core_low(role, j):
        return remote(
            wgt.at[0, role, j, low],
            wgt.at[1, role, j, low],
            w_core.at[0, role, j],
            w_core.at[1, role, j],
            other_core,
        )

    def to_y(role, j, rx, slot):
        return remote(
            stage.at[slot], from_y.at[role, j, rx], y_send.at[slot], y_recv.at[role, j, rx], y_peer
        )

    def place(role):
        return role // 2

    def side_to_y(role, j, rx, slot):
        at = place(role)
        return remote(
            stage.at[slot], side.at[at, j, rx], y_send.at[slot], side_recv.at[at, j, rx], y_peer
        )

    def side_to_end(role, j, rx):
        at = place(role)
        return remote(
            side.at[at, j, rx],
            side.at[at, j, rx],
            side_send.at[at, j, rx],
            side_recv.at[at, j, rx],
            end_peer,
        )

    def piece(role, xt, j):
        first = jnp.where(role < END, mid_z, end_z_at)
        zt = jnp.where(role % 2 == 0, first, nz - 1 - first)
        return (2 * zt + xt) * chunks + j

    def to_x(role, j):
        return remote(
            from_y.at[role, j, 1], from_x.at[role, j], x_send.at[role, j], x_recv.at[role, j], x_peer
        )

    def lanes(k):
        return pl.ds(pl.multiple_of(k * LANES, LANES), LANES)

    def write_out(k):
        return pltpu.make_async_copy(hid.at[k], out_ref.at[:, lanes(k)], out_sem.at[k])

    def scale_of(level):
        return jnp.exp2(level * (1.0 / 128.0)) * (1.0 / TOP)

    def pack(ref, value):
        top = jnp.maximum(jnp.max(jnp.abs(value), axis=0, keepdims=True), 1e-30)
        level = jnp.ceil(jnp.log2(top) * 128.0)
        ref[:rows] = jnp.round(value * (1.0 / scale_of(level))).astype(jnp.int32).astype(jnp.int16)
        level = jnp.broadcast_to(level, (16, LANES))
        ref[rows:] = level.astype(jnp.int32).astype(jnp.int16)

    def unpack(ref):
        level = ref[rows:].astype(jnp.int32).astype(jnp.float32)[:1]
        return ref[:rows].astype(jnp.int32).astype(jnp.float32) * scale_of(level)

    load_res = pltpu.make_async_copy(resid_ref, res, res_sem)

    def queries_z(source, target):
        mine = every_q.at[t_at, x, source]
        return remote(mine, mine, q_z.at[0, target], q_z.at[1, source], z_peer(target))

    def queries_x(xs):
        mine = every_q.at[t_at, xs]
        return remote(mine, mine, q_x.at[0], q_x.at[1], x_peer)

    def queries_y(ts):
        return remote(every_q.at[ts], every_q.at[ts], q_y.at[0], q_y.at[1], y_peer)

    def queries_core(n, ts):
        return remote(
            every_q.at[ts], every_q.at[ts], q_core.at[0, n], q_core.at[1, n], other_core
        )

    def scores_z(source, target):
        mine = board.at[group, source]
        return remote(mine, mine, s_z.at[0, target], s_z.at[1, source], z_peer(target))

    def scores_plane(source, target):
        return remote(
            board.at[source],
            board.at[source],
            s_plane.at[0, target],
            s_plane.at[1, source],
            plane_peer(target),
        )

    for j in range(chunks):
        load_weight(j).start()
    for r in range(2):
        load_ctx(r).start()
    load_res.start()
    square[...] = jnp.zeros_like(square)
    pooled[...] = jnp.zeros_like(pooled)

    f32, high = jnp.float32, lax.Precision.HIGHEST
    width = 2 * nz * chunks * LANES
    half, share = nz * chunks, every_q.shape[4] - 2 * LANES
    row = lax.broadcasted_iota(jnp.int32, (8, LANES), 0)
    lane = lax.broadcasted_iota(jnp.int32, (8, LANES), 1)
    own_q = every_q.at[t_at, x, z]
    at = lane - 8 * (nz * x + z)
    ids = jnp.zeros((8, LANES), f32)
    facts = jnp.zeros((8, LANES), f32)
    for r in range(Q_DEV):
        for h in range(2):
            part = pl.ds(pl.multiple_of(h * (width // 2) + t_at * share, LANES), share)
            own_q[2 * r + h : 2 * r + h + 1, :share] = query_ref[r : r + 1, part]
        mine = (at == 2 * r) | (at == 2 * r + 1)
        ids = jnp.where(mine & (row == 0), positive_ref[r].astype(f32), ids)
        facts = jnp.where(mine & (row == 0), count_ref[r].astype(f32), facts)
        for k in range(NEG):
            ids = jnp.where(mine & (row == k + 1), negative_ref[r, k].astype(f32), ids)
            facts = jnp.where(mine & (row == k + 1), margin_ref[r, k], facts)
    own_q[:, share : share + LANES] = ids
    own_q[:, share + LANES :] = facts
    pl.semaphore_wait(barrier, 7 + nz - 1)
    for other in other_planes():
        queries_z(z, other).start()
    for r in range(2):
        core_ctx(r).start()
    for r in range(2):
        load_ctx(r).wait()
        swap_ctx(0, r).start()

    @pl.when(ends)
    def _():
        lend_ctx(0).start()

    for r in range(2):
        core_ctx(r).wait_recv()
        swap_ctx(1, r).start()

    @pl.when(ends)
    def _():
        lend_ctx(1).start()

    for j in range(chunks):
        load_weight(j).wait()

        @pl.when(ends)
        def _():
            to_mid(j).start()

        @pl.when(middle)
        def _():
            to_end_whole(j).start()
            to_next(NEAR, j).start()

        to_core(own, j).start()
    load_res.wait()

    mid_tasks, end_tasks = listed(MIDDLE), listed(ENDS)
    mid_marks, end_marks = coded(mid_tasks), coded(end_tasks)
    steps = jnp.where(ends, len(end_tasks), len(mid_tasks))
    lent_swapped = [task[0] == SIDE and task[2] == 1 for task in mid_tasks].index(True)
    own_swapped = [task[0] == FULL and task[2] == 1 for task in mid_tasks].index(True)
    end_swapped = [task[2] for task in end_tasks].index(1)
    swapped = jnp.where(ends, end_swapped, own_swapped)
    spread = jnp.where(ends, end_swapped + chunks, max(lent_swapped, own_swapped + chunks))
    spread_core = jnp.where(ends, len(end_tasks) - chunks, len(mid_tasks) - chunks)
    lag_x = jnp.where(ends, LAG_X[1], LAG_X[0])
    mid_events, end_events = events(MIDDLE_RELAYS), events(END_RELAYS)

    def task(i):
        mid_code, end_code = i, i
        for start, more in mid_marks:
            mid_code += jnp.where(i >= start, more, 0)
        for start, more in end_marks:
            end_code += jnp.where(i >= start, more, 0)
        code = jnp.where(ends, end_code, mid_code)
        return code // 64 % 4, code // 16 % 4, code % 8, code // 8 % 2, code // 256

    def relay(code):
        role, j = (code - 1) // 8, (code - 1) % 8

        @pl.when((code > 0) & middle)
        def _():
            arriving = remote(
                wgt.at[0, role, j],
                wgt.at[0, role, j],
                w_mid.at[role, j],
                w_recv.at[role, j],
                next_peer,
            )
            arriving.wait_recv()

            @pl.when(role == END)
            def _():
                to_next(END, j).start()

            @pl.when(role != END)
            def _():
                to_end(role, j).start()

            to_core(role, j).start()

        @pl.when((code > 0) & ends & (role == NEAR))
        def _():
            to_end_whole(j).wait_recv()
            to_core(role, j).start()

        @pl.when((code > 0) & ends & (role != NEAR))
        def _():
            to_end(role, j).wait_recv()
            to_core_low(role, j).start()

    def relays(i):
        for mid_list, end_list in zip(mid_events, end_events):
            mid_code, end_code = 0, 0
            for at, code in mid_list:
                mid_code += jnp.where(i == at, code, 0)
            for at, code in end_list:
                end_code += jnp.where(i == at, code, 0)
            relay(jnp.where(ends, end_code, mid_code))

    def compute(i):
        kind, role, j, rx, new = task(i)
        slot = i % RING

        whole = middle | (role == END) | (role == NEAR)

        @pl.when((new == 1) & whole)
        def _():
            to_core(role, j).wait_recv()

        @pl.when((new == 1) & jnp.logical_not(whole))
        def _():
            to_core_low(role, j).wait_recv()

        @pl.when(middle & (i == LENT))
        def _():
            for k in range(2):
                lend_ctx(k).wait_recv()
                lend_swap(k).start()

        @pl.when(middle & (i == lent_swapped))
        def _():
            for k in range(2):
                lend_swap(k).wait_recv()

        @pl.when(i == swapped)
        def _():
            for k in range(2):
                for r in range(2):
                    swap_ctx(k, r).wait_recv()
            for other in other_planes():
                queries_z(other, z).wait_recv()
            queries_x(x).start()

        @pl.when(i == spread)
        def _():
            queries_x(1 - x).wait_recv()
            queries_y(t_at).start()
            queries_core(0, t_at).start()

        @pl.when(i == spread_core)
        def _():
            queries_y((t_at + 2) % 4).wait_recv()
            queries_core(1, (t_at + 2) % 4).start()

        def product(acts, block):
            return jnp.dot(acts, block, preferred_element_type=f32)

        @pl.when(kind == FULL)
        def _():
            sums[...] = product(ctx[0, rx], wgt[0, role, j]) + product(ctx[1, rx], wgt[1, role, j])

        @pl.when(kind == LOW)
        def _():
            sums[...] = product(ctx[0, rx, :, low], wgt[0, role, j, low]) + product(
                ctx[1, rx, :, low], wgt[1, role, j, low]
            )

        @pl.when(kind == SIDE)
        def _():
            sums[...] = product(ctx_end[0, rx], wgt[0, role, j, deep]) + product(
                ctx_end[1, rx], wgt[1, role, j, deep]
            )

        @pl.when(i >= RING)
        def _():
            to_y(role, j, rx, slot).wait_send()

        pack(stage.at[slot], sums[rows:])
        hold[slot] = sums[:rows]

        @pl.when(kind == SIDE)
        def _():
            side_to_y(role, j, rx, slot).start()

        @pl.when(kind != SIDE)
        def _():
            to_y(role, j, rx, slot).start()

    def settle(k, total):
        total = total + res[:, lanes(k)].astype(f32)
        hid[k] = total
        square[...] += total * total
        write_out(k).start()

    def add_y(i):
        kind, role, j, rx, _ = task(i)
        slot = i % RING
        at = place(role)

        @pl.when(kind == SIDE)
        def _():
            side_to_y(role, j, rx, slot).wait_recv()
            pack(side.at[at, j, rx], hold[slot] + unpack(side.at[at, j, rx]))
            side_to_end(role, j, rx).start()

        @pl.when(kind != SIDE)
        def _():
            to_y(role, j, rx, slot).wait_recv()

        @pl.when(kind == LOW)
        def _():
            side_to_end(role, j, rx).wait_recv()
            hold[slot] += unpack(side.at[at, j, rx])

        @pl.when((kind != SIDE) & (rx == 0))
        def _():
            settle(piece(role, x, j), hold[slot] + unpack(from_y.at[role, j, 0]))

        @pl.when((kind != SIDE) & (rx == 1))
        def _():
            pack(from_y.at[role, j, 1], hold[slot] + unpack(from_y.at[role, j, 1]))
            to_x(role, j).start()

    def add_x(i):
        kind, role, j, rx, _ = task(i)

        @pl.when((kind != SIDE) & (rx == 1))
        def _():
            to_x(role, j).wait_recv()
            settle(piece(role, 1 - x, j), unpack(from_x.at[role, j]))

    def step(i, carry):
        relays(i)

        @pl.when(i >= lag_x)
        def _():
            add_x(i - lag_x)

        @pl.when((i >= LAG) & (i < steps + LAG))
        def _():
            add_y(i - LAG)

        @pl.when(i < steps)
        def _():
            compute(i)

        return carry

    lax.fori_loop(0, steps + lag_x, step, 0)

    near_core = t_at + 1 - 2 * core
    queries_core(0, near_core).wait_recv()
    queries_core(1, (near_core + 2) % 4).wait_recv()
    inv = lax.rsqrt(jnp.sum(square[...], axis=1, keepdims=True) / width + 1e-05)
    inv_lanes = jnp.broadcast_to(inv, (rows, LANES))
    square[...] = inv_lanes

    def pool(n, carry):
        for h in range(2):
            k = h * half + n
            total = jnp.sum(hid[k] * square[...], axis=0, keepdims=True)
            pooled[h : h + 1, lanes(n)] = total * gain_ref[pl.ds(k, 1), :]
        return carry

    lax.fori_loop(0, half, pool, 0)
    scale = 1.0 / math.sqrt(width * SEQ)
    count = 8 * 2 * nz
    found = jnp.zeros((8, count), f32)
    for t in range(4):
        here = pl.ds(t * share, share)
        block = every_q[t, :, :, :, :share].reshape(count, share)
        found += lax.dot_general(
            pooled[:, here],
            block,
            (((1,), (1,)), ((), ())),
            precision=high,
            preferred_element_type=f32,
        )
    found = jnp.concatenate([found, jnp.zeros((8, LANES - count), f32)], axis=1) * scale
    kept = jnp.sum(jnp.where(row == lane % 2, found, 0.0), axis=0, keepdims=True)
    kept = jnp.broadcast_to(kept, (8, LANES))
    after, before = pltpu.roll(kept, LANES - 1, 1), pltpu.roll(kept, 1, 1)
    board[group, z] = kept + jnp.where(lane % 2 == 0, after, before)

    for other in other_planes():
        scores_z(z, other).start()
    info = jnp.zeros((8, 2 * LANES), f32)
    for xs in range(2):
        for zs in range(nz):
            info += every_q[0, xs, zs, :, share:]
    ids, facts = info[:, :LANES], info[:, LANES:]
    for other in other_planes():
        scores_z(other, z).wait_recv()
    for other in other_groups():
        scores_plane(group, other).start()
    for other in other_groups():
        scores_plane(other, group).wait_recv()

    picked = jnp.zeros((8, LANES), f32)
    for zs in range(nz):
        for xs in range(2):
            for ys in range(2):
                score = board[4 * xs + 2 * ys, zs] + board[4 * xs + 2 * ys + 1, zs]
                picked += jnp.where(ids == 2 * (2 * zs + xs) + ys, score, 0.0)
    counts = jnp.broadcast_to(facts[0:1], (8, LANES))
    err = jnp.broadcast_to(picked[0:1], (8, LANES)) - picked - facts
    live = (row >= 1) & ((row - 1).astype(f32) < counts)
    err = jnp.where(live, err, 0.0)
    counts = jnp.where(counts > 0, counts, 1.0)
    nquery = Q_DEV * 2 * nz
    terms = jnp.where(lane % 2 == 0, err * err / counts, 0.0)
    loss_ref[0, 0] = jnp.sum(terms) / nquery
    weight = 2.0 * err / (counts * nquery)
    passage = (PASS_DEV * dp_at + y).astype(f32)
    at_pos = jnp.broadcast_to(jnp.where(ids[0:1] == passage, 1.0, 0.0), (8, LANES))
    at_neg = jnp.where(ids == passage, 1.0, 0.0)
    coef = jnp.sum(weight * (at_pos - at_neg), axis=0, keepdims=True)
    coef = jnp.where(row == lane % 2, jnp.broadcast_to(coef, (8, LANES)), 0.0)[:, :count]
    for t in range(4):
        here = pl.ds(t * share, share)
        block = every_q[t, :, :, :, :share].reshape(count, share)
        grad = jnp.dot(coef, block, precision=high, preferred_element_type=f32)
        pooled[:, here] = grad * scale

    def align(n, total):
        for h in range(2):
            k = h * half + n
            up = pooled[h : h + 1, lanes(n)] * gain_ref[pl.ds(k, 1), :]
            up_ref[0:1, lanes(k)] = up
            total += hid[k] * up
        return total

    total = lax.fori_loop(0, half, align, jnp.zeros((rows, LANES), f32))
    inner = jnp.sum(total, axis=1, keepdims=True) / width
    up_ref[1:, :] = jnp.zeros((7, width), f32)
    factor_ref[0] = 65536.0 * square[...]
    factor_ref[1] = jnp.broadcast_to(-65536.0 * (inv * inv * inv * inner), (rows, LANES))

    for other in other_planes():
        queries_z(z, other).wait_send()
        scores_z(z, other).wait_send()
    for other in other_groups():
        scores_plane(group, other).wait_send()
    queries_x(x).wait_send()
    queries_y(t_at).wait_send()
    for n in range(2):
        queries_core(n, t_at).wait_send()

    for n in range(RING):
        to_y(0, 0, 0, n).wait_send()
    for r in range(2):
        core_ctx(r).wait_send()
        for k in range(2):
            swap_ctx(k, r).wait_send()

    @pl.when(ends)
    def _():
        for k in range(2):
            lend_ctx(k).wait_send()

    @pl.when(middle)
    def _():
        for k in range(2):
            lend_swap(k).wait_send()

    def drain(j, carry):
        for role in (NEAR, NEXT, END, FAR):
            to_x(role, j).wait_send()
            for xt in range(2):
                write_out(piece(role, xt, j)).wait()
        for role in (NEAR, END):
            to_core(role, j).wait_send()

        @pl.when(ends)
        def _():
            to_mid(j).wait_send()
            for role in (NEXT, FAR):
                to_core_low(role, j).wait_send()

        @pl.when(middle)
        def _():
            for role in (NEAR, END):
                to_next(role, j).wait_send()
            to_end_whole(j).wait_send()
            for role in (NEXT, FAR):
                to_core(role, j).wait_send()
                to_end(role, j).wait_send()
                for rx in range(2):
                    side_to_end(role, j, rx).wait_send()

        return carry

    lax.fori_loop(0, chunks, drain, 0)


def tile_hidden(context, o_weight, resid, gain, queries, facts):
    rows, width = resid.shape
    depth, columns = o_weight.shape
    chunks = columns // LANES
    nz = width // (2 * columns)
    f32, bf16 = jnp.float32, jnp.bfloat16
    coded_rows = rows + 16
    dma = pltpu.SemaphoreType.DMA
    return pl.pallas_call(
        functools.partial(tile_kernel, nz),
        out_shape=(
            jax.ShapeDtypeStruct((rows, width), f32),
            jax.ShapeDtypeStruct((2, rows, LANES), f32),
            jax.ShapeDtypeStruct((8, width), f32),
            jax.ShapeDtypeStruct((1, 1), f32),
        ),
        in_specs=[pl.BlockSpec(memory_space=pl.ANY)] * 3
        + [pl.BlockSpec(memory_space=pltpu.VMEM)] * 2
        + [pl.BlockSpec(memory_space=pltpu.SMEM)] * 4,
        out_specs=(
            pl.BlockSpec(memory_space=pl.ANY),
            pl.BlockSpec(memory_space=pltpu.VMEM),
            pl.BlockSpec(memory_space=pltpu.VMEM),
            pl.BlockSpec(memory_space=pltpu.SMEM),
        ),
        scratch_shapes=[
            pltpu.VMEM((2, 2, 2 * rows, depth), bf16),
            pltpu.VMEM((2, 2, 2 * rows, depth // 2), bf16),
            pltpu.VMEM((2, nz, chunks, depth, LANES), bf16),
            pltpu.VMEM((nz, chunks, 2, coded_rows, LANES), jnp.int16),
            pltpu.VMEM((nz, chunks, coded_rows, LANES), jnp.int16),
            pltpu.VMEM((nz // 2, chunks, 2, coded_rows, LANES), jnp.int16),
            pltpu.VMEM((2 * nz * chunks, rows, LANES), f32),
            pltpu.VMEM((rows, width), bf16),
            pltpu.VMEM((RING, coded_rows, LANES), jnp.int16),
            pltpu.VMEM((RING, rows, LANES), f32),
            pltpu.VMEM((2 * rows, LANES), f32),
            dma((2,)),
            dma((2, 2)),
            dma((2, 2, 2)),
            dma((2, 2)),
            dma((2, 2)),
            dma((chunks,)),
            dma((nz, chunks)),
            dma((nz, chunks)),
            dma((nz, chunks)),
            dma((2, nz, chunks)),
            dma((RING,)),
            dma((nz, chunks, 2)),
            dma((nz // 2, chunks, 2)),
            dma((nz // 2, chunks, 2)),
            dma((nz, chunks)),
            dma((nz, chunks)),
            dma,
            dma((2 * nz * chunks,)),
            pltpu.VMEM((4, 2, nz, 2 * Q_DEV, width // 8 + 2 * LANES), f32),
            pltpu.VMEM((rows, LANES), f32),
            pltpu.VMEM((8, width // 2), f32),
            pltpu.VMEM((8, nz, 8, LANES), f32),
            dma((2, nz)),
            dma((2,)),
            dma((2,)),
            dma((2, 2)),
            dma((2, nz)),
            dma((2, 8)),
        ],
        compiler_params=pltpu.CompilerParams(
            collective_id=0, has_side_effects=True, vmem_limit_bytes=58 << 20
        ),
        cost_estimate=pl.CostEstimate(
            flops=2 * 4 * rows * depth * width, bytes_accessed=4 * rows * width, transcendentals=0
        ),
    )(context, o_weight, resid, gain, queries, *facts)


def grad_kernel(hidden_ref, factor_ref, up_ref, grad_ref):
    for n in range(grad_ref.shape[1] // LANES):
        here = pl.ds(n * LANES, LANES)
        grad_ref[:, here] = factor_ref[0] * up_ref[0:1, here] + factor_ref[1] * hidden_ref[:, here]


def gradient(hidden, factors, upward):
    rows, width = hidden.shape
    step = rows // 8
    return pl.pallas_call(
        grad_kernel,
        out_shape=jax.ShapeDtypeStruct((rows, width), jnp.float32),
        grid=(rows // step,),
        in_specs=[
            pl.BlockSpec((step, width), lambda n: (n, 0)),
            pl.BlockSpec((2, step, LANES), lambda n: (0, n, 0)),
            pl.BlockSpec((8, width), lambda n: (0, 0)),
        ],
        out_specs=pl.BlockSpec((step, width), lambda n: (n, 0)),
        compiler_params=pltpu.CompilerParams(vmem_limit_bytes=58 << 20),
    )(hidden, factors, upward)


def line_shards(
    context, resid, o_weight, norm_gain, queries, positive_ids, negative_ids, margins, pair_counts
):
    gain = norm_gain.reshape(-1, LANES)
    facts = (positive_ids, negative_ids, margins, pair_counts)
    hidden, factors, upward, loss = tile_hidden(context, o_weight, resid, gain, queries, facts)
    return (gradient(hidden, factors, upward), loss.reshape(()))


def solution(mesh):
    body = line_shards if dict(mesh.shape) == {"dp": 8, "tensor": 4} else shards
    return jax.shard_map(
        body,
        mesh=mesh,
        in_specs=(
            P("dp", "tensor"),
            P(("dp", "tensor"), None),
            P("tensor", "dp"),
            P(),
            P("dp", None),
            P("dp"),
            P("dp", None),
            P("dp", None),
            P("dp"),
        ),
        out_specs=(P(("dp", "tensor"), None), P()),
        check_vma=False,
    )
```

```python
import functools
import math

import jax
import jax.numpy as jnp
from jax import lax
from jax.experimental import pallas as pl
from jax.experimental.pallas import tpu as pltpu
from jax.sharding import PartitionSpec as P

D = 7168
SEQ = 512
PASS_DEV = 2
Q_DEV = 4
NEG = 7


def shards(
    context, resid, o_weight, norm_gain, queries, positive_ids, negative_ids, margins, pair_counts
):
    full_weight = lax.all_gather(o_weight, "dp", axis=1, tiled=True)
    tok_rows = resid.shape[0]
    attn = lax.psum_scatter(
        jnp.dot(context, full_weight, preferred_element_type=jnp.float32),
        "tensor",
        scatter_dimension=0,
        tiled=True,
    )
    hidden = resid.astype(jnp.float32) + attn
    inv = lax.rsqrt(jnp.mean(hidden * hidden, axis=-1, keepdims=True) + 1e-05)
    normed = hidden * inv * norm_gain
    first = lax.axis_index("tensor") * tok_rows
    passage_of = (first + jnp.arange(tok_rows, dtype=jnp.int32)) // SEQ
    member = (passage_of[None, :] == jnp.arange(PASS_DEV, dtype=jnp.int32)[:, None]).astype(
        jnp.float32
    )
    partial_value = jnp.dot(member, normed, precision=lax.Precision.HIGHEST)
    scale = 1.0 / jnp.sqrt(jnp.float32(D * SEQ))
    npass = PASS_DEV * lax.axis_size("dp")
    nquery = Q_DEV * lax.axis_size("dp")
    pooled = lax.psum(partial_value, "tensor")
    every_pass = lax.all_gather(pooled, "dp", axis=0, tiled=True)
    scores = jnp.dot(queries, every_pass.T, precision=lax.Precision.HIGHEST) * scale
    passes = jnp.arange(npass, dtype=jnp.int32)
    onehot_pos = (positive_ids[:, None] == passes[None, :]).astype(jnp.float32)
    onehot_neg = (negative_ids[:, :, None] == passes[None, None, :]).astype(jnp.float32)
    score_pos = jnp.sum(onehot_pos * scores, axis=-1)
    score_neg = jnp.sum(onehot_neg * scores[:, None, :], axis=-1)
    err = score_pos[:, None] - score_neg - margins
    live = (jnp.arange(NEG, dtype=jnp.int32)[None, :] < pair_counts[:, None]).astype(jnp.float32)
    counts = pair_counts.astype(jnp.float32)
    local_loss = jnp.sum(jnp.sum(live * err * err, axis=1) / counts) / nquery
    weight = 2.0 * live * err / (counts[:, None] * nquery)
    coef = onehot_pos * jnp.sum(weight, axis=1)[:, None] - jnp.sum(
        weight[:, :, None] * onehot_neg, axis=1
    )
    grad_terms = jnp.dot(coef.T, queries, precision=lax.Precision.HIGHEST) * scale
    pass_grad = lax.psum_scatter(grad_terms, "dp", scatter_dimension=0, tiled=True)
    loss = lax.psum(local_loss, "dp")
    upward = jnp.dot(member.T, pass_grad, precision=lax.Precision.HIGHEST) * norm_gain
    inner = jnp.mean(hidden * upward, axis=-1, keepdims=True)
    grad = 65536.0 * (inv * upward - hidden * inv * inv * inv * inner)
    return (grad, loss)


MESH = pl.DeviceIdType.MESH
LANES = 128
LAG = 5
LAG_X = (32, 8)
RING = 7
TOP = 32600.0
FULL, LOW, SIDE = 0, 1, 2
NEAR, NEXT, END, FAR = 0, 1, 2, 3
CHUNKS = 7

MIDDLE = (
    (FULL, NEAR, 0, 0, 7),
    (FULL, NEXT, 0, 0, 3),
    (SIDE, NEXT, 0, 0, 4),
    (FULL, NEXT, 0, 3, 4),
    (FULL, END, 0, 0, 1),
    (SIDE, NEXT, 0, 4, 5),
    (FULL, NEXT, 0, 4, 5),
    (FULL, END, 0, 1, 2),
    (SIDE, NEXT, 0, 5, 6),
    (FULL, NEXT, 0, 5, 6),
    (FULL, END, 0, 2, 3),
    (SIDE, NEXT, 0, 6, 7),
    (FULL, NEXT, 0, 6, 7),
    (FULL, NEAR, 1, 0, 4),
    (SIDE, FAR, 0, 0, 1),
    (FULL, NEAR, 1, 4, 7),
    (FULL, NEXT, 1, 0, 2),
    (SIDE, FAR, 0, 1, 2),
    (FULL, NEXT, 1, 2, 7),
    (SIDE, FAR, 0, 2, 3),
    (FULL, END, 1, 0, 5),
    (SIDE, FAR, 0, 3, 4),
    (FULL, END, 1, 5, 7),
    (SIDE, NEXT, 1, 0, 7),
    (SIDE, FAR, 1, 0, 6),
    (SIDE, FAR, 0, 4, 6),
    (FULL, FAR, 1, 0, 4),
    (SIDE, FAR, 1, 6, 7),
    (SIDE, FAR, 0, 6, 7),
    (FULL, FAR, 1, 4, 7),
    (FULL, END, 0, 3, 7),
    (FULL, FAR, 0, 0, 7),
)

ENDS = (
    (FULL, END, 0, 0, 7),
    (FULL, NEAR, 0, 0, 7),
    (FULL, END, 1, 0, 7),
    (FULL, NEAR, 1, 0, 7),
    (LOW, NEXT, 0, 0, 7),
    (LOW, FAR, 0, 0, 4),
    (LOW, NEXT, 1, 0, 7),
    (LOW, FAR, 1, 0, 6),
    (LOW, FAR, 0, 4, 6),
    (LOW, FAR, 1, 6, 7),
    (LOW, FAR, 0, 6, 7),
)

MIDDLE_RELAYS = (
    (6, NEXT, 0),
    (8, NEXT, 1),
    (9, NEXT, 2),
    (13, NEXT, 3),
    (15, END, 0),
    (15, NEXT, 4),
    (18, END, 1),
    (18, NEXT, 5),
    (21, END, 2),
    (21, NEXT, 6),
    (25, END, 3),
    (26, FAR, 0),
    (31, END, 4),
    (32, FAR, 1),
    (37, END, 5),
    (38, FAR, 2),
    (43, END, 6),
    (44, FAR, 3),
    (51, FAR, 4),
    (59, FAR, 5),
    (66, FAR, 6),
)
END_RELAYS = (
    (5, NEAR, 0),
    (6, NEAR, 1),
    (7, NEAR, 2),
    (8, NEAR, 3),
    (9, NEAR, 4),
    (10, NEAR, 5),
    (11, NEAR, 6),
    (15, NEXT, 0),
    (16, NEXT, 1),
    (19, NEXT, 2),
    (22, NEXT, 3),
    (26, NEXT, 4),
    (31, NEXT, 5),
    (32, NEXT, 6),
    (33, FAR, 0),
    (34, FAR, 1),
    (35, FAR, 2),
    (36, FAR, 3),
    (42, FAR, 4),
    (49, FAR, 5),
    (52, FAR, 6),
)
LENT = 10


def listed(runs):
    return [(kind, role, rx, j) for kind, role, rx, lo, hi in runs for j in range(lo, hi)]


def coded(tasks):
    met, last, marks = set(), -1, []
    for i, (kind, role, rx, j) in enumerate(tasks):
        new = (role, j) not in met
        met.add((role, j))
        code = j + 8 * rx + 16 * role + 64 * kind + 256 * new
        if code != last + 1 or i == 0:
            marks.append((i, code - (last + 1)))
        last = code
    return marks


def events(relays):
    first, second, steps = [], [], set()
    for step, role, j in relays:
        (second if step in steps else first).append((step, 8 * role + j + 1))
        steps.add(step)
    return first, second


def tile_kernel(
    nz,
    ctx_ref,
    weight_ref,
    resid_ref,
    gain_ref,
    query_ref,
    positive_ref,
    negative_ref,
    margin_ref,
    count_ref,
    out_ref,
    factor_ref,
    up_ref,
    loss_ref,
    ctx,
    ctx_end,
    wgt,
    from_y,
    from_x,
    side,
    hid,
    res,
    stage,
    hold,
    sums,
    ctx_load,
    ctx_core,
    ctx_x,
    end_z,
    end_x,
    w_load,
    w_end,
    w_mid,
    w_recv,
    w_core,
    y_send,
    y_recv,
    side_send,
    side_recv,
    x_send,
    x_recv,
    res_sem,
    out_sem,
    every_q,
    square,
    pooled,
    board,
    q_z,
    q_x,
    q_y,
    q_core,
    s_z,
    s_plane,
):
    dp_at, t_at = lax.axis_index("dp"), lax.axis_index("tensor")
    z, x = dp_at // 2, dp_at % 2
    y, core = t_at // 2, t_at % 2
    chunks = wgt.shape[2]
    depth = wgt.shape[3]
    low, deep = pl.ds(0, depth // 2), pl.ds(depth // 2, depth // 2)
    rows = hid.shape[1]
    group = 4 * x + t_at
    mid_z = jnp.where(z < nz // 2, 1, nz - 2)
    end_z_at = jnp.where(z < nz // 2, 0, nz - 1)
    ends = z == end_z_at
    middle = jnp.logical_not(ends)
    own = jnp.where(ends, END, NEAR)
    other_core = (dp_at, 2 * y + 1 - core)
    y_peer = (dp_at, 2 * (1 - y) + core)
    x_peer = (2 * z + 1 - x, t_at)
    end_peer = (2 * end_z_at + x, t_at)
    mid_peer = (2 * mid_z + x, t_at)
    next_peer = (2 * (nz - 1 - mid_z) + x, t_at)

    def z_peer(other):
        return (2 * other + x, t_at)

    def plane_peer(other):
        return (2 * z + other // 4, other % 4)

    def other_groups():
        return [(group + m) % 8 for m in range(1, 8)]

    def other_planes():
        return [(z + m) % nz for m in range(1, nz)]

    barrier = pltpu.get_barrier_semaphore()
    for other in other_groups():
        pl.semaphore_signal(barrier, inc=1, device_id=plane_peer(other), device_id_type=MESH)
    for other in other_planes():
        pl.semaphore_signal(barrier, inc=1, device_id=z_peer(other), device_id_type=MESH)

    def remote(src, dst, send, recv, peer):
        return pltpu.make_async_remote_copy(
            src_ref=src,
            dst_ref=dst,
            send_sem=send,
            recv_sem=recv,
            device_id=peer,
            device_id_type=MESH,
        )

    def load_weight(j):
        return pltpu.make_async_copy(
            weight_ref.at[:, pl.ds(j * LANES, LANES)], wgt.at[0, own, j], w_load.at[j]
        )

    def quarter(r, c):
        return pl.ds(pl.multiple_of((2 * ((y + r) % 2) + c) * rows, rows), rows)

    def load_ctx(r):
        return pltpu.make_async_copy(
            ctx_ref.at[quarter(r, core)], ctx.at[0, 0, pl.ds(r * rows, rows)], ctx_load.at[r]
        )

    def core_ctx(r):
        return remote(
            ctx_ref.at[quarter(r, 1 - core)],
            ctx.at[1, 0, pl.ds(r * rows, rows)],
            ctx_core.at[0, r],
            ctx_core.at[1, r],
            other_core,
        )

    def swap_ctx(k, r):
        block = pl.ds(r * rows, rows)
        return remote(
            ctx.at[k, 0, block], ctx.at[k, 1, block], ctx_x.at[0, k, r], ctx_x.at[1, k, r], x_peer
        )

    def lend_ctx(k):
        return remote(
            ctx.at[k, 0, :, deep], ctx_end.at[k, 0], end_z.at[0, k], end_z.at[1, k], mid_peer
        )

    def lend_swap(k):
        return remote(
            ctx_end.at[k, 0], ctx_end.at[k, 1], end_x.at[0, k], end_x.at[1, k], x_peer
        )

    def to_end(role, j):
        return remote(
            wgt.at[0, role, j, low],
            wgt.at[0, role, j, low],
            w_end.at[role, j],
            w_recv.at[role, j],
            end_peer,
        )

    def to_end_whole(j):
        return remote(
            wgt.at[0, NEAR, j], wgt.at[0, NEAR, j], w_end.at[NEAR, j], w_recv.at[NEAR, j], end_peer
        )

    def to_next(role, j):
        return remote(
            wgt.at[0, role, j],
            wgt.at[0, role + 1, j],
            w_mid.at[role, j],
            w_recv.at[role + 1, j],
            next_peer,
        )

    def to_mid(j):
        return remote(
            wgt.at[0, END, j], wgt.at[0, END, j], w_mid.at[END, j], w_recv.at[END, j], mid_peer
        )

    def to_core(role, j):
        return remote(
            wgt.at[0, role, j],
            wgt.at[1, role, j],
            w_core.at[0, role, j],
            w_core.at[1, role, j],
            other_core,
        )

    def to_core_low(role, j):
        return remote(
            wgt.at[0, role, j, low],
            wgt.at[1, role, j, low],
            w_core.at[0, role, j],
            w_core.at[1, role, j],
            other_core,
        )

    def to_y(role, j, rx, slot):
        return remote(
            stage.at[slot], from_y.at[role, j, rx], y_send.at[slot], y_recv.at[role, j, rx], y_peer
        )

    def place(role):
        return role // 2

    def side_to_y(role, j, rx, slot):
        at = place(role)
        return remote(
            stage.at[slot], side.at[at, j, rx], y_send.at[slot], side_recv.at[at, j, rx], y_peer
        )

    def side_to_end(role, j, rx):
        at = place(role)
        return remote(
            side.at[at, j, rx],
            side.at[at, j, rx],
            side_send.at[at, j, rx],
            side_recv.at[at, j, rx],
            end_peer,
        )

    def piece(role, xt, j):
        first = jnp.where(role < END, mid_z, end_z_at)
        zt = jnp.where(role % 2 == 0, first, nz - 1 - first)
        return (2 * zt + xt) * chunks + j

    def to_x(role, j):
        return remote(
            from_y.at[role, j, 1], from_x.at[role, j], x_send.at[role, j], x_recv.at[role, j], x_peer
        )

    def lanes(k):
        return pl.ds(pl.multiple_of(k * LANES, LANES), LANES)

    def write_out(k):
        return pltpu.make_async_copy(hid.at[k], out_ref.at[:, lanes(k)], out_sem.at[k])

    def scale_of(level):
        return jnp.exp2(level * (1.0 / 128.0)) * (1.0 / TOP)

    def pack(ref, value):
        top = jnp.maximum(jnp.max(jnp.abs(value), axis=0, keepdims=True), 1e-30)
        level = jnp.ceil(jnp.log2(top) * 128.0)
        ref[:rows] = jnp.round(value * (1.0 / scale_of(level))).astype(jnp.int32).astype(jnp.int16)
        level = jnp.broadcast_to(level, (16, LANES))
        ref[rows:] = level.astype(jnp.int32).astype(jnp.int16)

    def unpack(ref):
        level = ref[rows:].astype(jnp.int32).astype(jnp.float32)[:1]
        return ref[:rows].astype(jnp.int32).astype(jnp.float32) * scale_of(level)

    load_res = pltpu.make_async_copy(resid_ref, res, res_sem)

    def queries_z(source, target):
        mine = every_q.at[t_at, x, source]
        return remote(mine, mine, q_z.at[0, target], q_z.at[1, source], z_peer(target))

    def queries_x(xs):
        mine = every_q.at[t_at, xs]
        return remote(mine, mine, q_x.at[0], q_x.at[1], x_peer)

    def queries_y(ts):
        return remote(every_q.at[ts], every_q.at[ts], q_y.at[0], q_y.at[1], y_peer)

    def queries_core(n, ts):
        return remote(
            every_q.at[ts], every_q.at[ts], q_core.at[0, n], q_core.at[1, n], other_core
        )

    def scores_z(source, target):
        mine = board.at[group, source]
        return remote(mine, mine, s_z.at[0, target], s_z.at[1, source], z_peer(target))

    def scores_plane(source, target):
        return remote(
            board.at[source],
            board.at[source],
            s_plane.at[0, target],
            s_plane.at[1, source],
            plane_peer(target),
        )

    for j in range(chunks):
        load_weight(j).start()
    for r in range(2):
        load_ctx(r).start()
    load_res.start()
    f32, high = jnp.float32, lax.Precision.HIGHEST
    width = 2 * nz * chunks * LANES
    half, share = nz * chunks, every_q.shape[4] - 2 * LANES
    row = lax.broadcasted_iota(jnp.int32, (8, LANES), 0)
    lane = lax.broadcasted_iota(jnp.int32, (8, LANES), 1)
    own_q = every_q.at[t_at, x, z]
    at = lane - 8 * (nz * x + z)
    ids = jnp.zeros((8, LANES), f32)
    facts = jnp.zeros((8, LANES), f32)
    for r in range(Q_DEV):
        for h in range(2):
            part = pl.ds(pl.multiple_of(h * (width // 2) + t_at * share, LANES), share)
            own_q[2 * r + h : 2 * r + h + 1, :share] = query_ref[r : r + 1, part]
        mine = (at == 2 * r) | (at == 2 * r + 1)
        ids = jnp.where(mine & (row == 0), positive_ref[r].astype(f32), ids)
        facts = jnp.where(mine & (row == 0), count_ref[r].astype(f32), facts)
        for k in range(NEG):
            ids = jnp.where(mine & (row == k + 1), negative_ref[r, k].astype(f32), ids)
            facts = jnp.where(mine & (row == k + 1), margin_ref[r, k], facts)
    own_q[:, share : share + LANES] = ids
    own_q[:, share + LANES :] = facts
    pl.semaphore_wait(barrier, 7 + nz - 1)
    for other in other_planes():
        queries_z(z, other).start()
    for r in range(2):
        core_ctx(r).start()

    @pl.when(middle)
    def _():
        for j in range(chunks):
            load_weight(j).wait()
            to_end_whole(j).start()
            to_next(NEAR, j).start()
            to_core(NEAR, j).start()

    for r in range(2):
        load_ctx(r).wait()
        swap_ctx(0, r).start()

    @pl.when(ends)
    def _():
        lend_ctx(0).start()

    for r in range(2):
        core_ctx(r).wait_recv()
        swap_ctx(1, r).start()

    @pl.when(ends)
    def _():
        lend_ctx(1).start()
        for j in range(chunks):
            load_weight(j).wait()
            to_mid(j).start()
            to_core(END, j).start()

    square[...] = jnp.zeros_like(square)
    pooled[...] = jnp.zeros_like(pooled)
    load_res.wait()

    mid_tasks, end_tasks = listed(MIDDLE), listed(ENDS)
    mid_marks, end_marks = coded(mid_tasks), coded(end_tasks)
    steps = jnp.where(ends, len(end_tasks), len(mid_tasks))
    lent_swapped = [task[0] == SIDE and task[2] == 1 for task in mid_tasks].index(True)
    own_swapped = [task[0] == FULL and task[2] == 1 for task in mid_tasks].index(True)
    end_swapped = [task[2] for task in end_tasks].index(1)
    swapped = jnp.where(ends, end_swapped, own_swapped)
    spread = jnp.where(ends, end_swapped + chunks, max(lent_swapped, own_swapped + chunks))
    spread_core = jnp.where(ends, len(end_tasks) - chunks, len(mid_tasks) - chunks)
    lag_x = jnp.where(ends, LAG_X[1], LAG_X[0])
    mid_events, end_events = events(MIDDLE_RELAYS), events(END_RELAYS)

    def task(i):
        mid_code, end_code = i, i
        for start, more in mid_marks:
            mid_code += jnp.where(i >= start, more, 0)
        for start, more in end_marks:
            end_code += jnp.where(i >= start, more, 0)
        code = jnp.where(ends, end_code, mid_code)
        return code // 64 % 4, code // 16 % 4, code % 8, code // 8 % 2, code // 256

    def relay(code):
        role, j = (code - 1) // 8, (code - 1) % 8

        @pl.when((code > 0) & middle)
        def _():
            arriving = remote(
                wgt.at[0, role, j],
                wgt.at[0, role, j],
                w_mid.at[role, j],
                w_recv.at[role, j],
                next_peer,
            )
            arriving.wait_recv()

            @pl.when(role == END)
            def _():
                to_next(END, j).start()

            @pl.when(role != END)
            def _():
                to_end(role, j).start()

            to_core(role, j).start()

        @pl.when((code > 0) & ends & (role == NEAR))
        def _():
            to_end_whole(j).wait_recv()
            to_core(role, j).start()

        @pl.when((code > 0) & ends & (role != NEAR))
        def _():
            to_end(role, j).wait_recv()
            to_core_low(role, j).start()

    def relays(i):
        for mid_list, end_list in zip(mid_events, end_events):
            mid_code, end_code = 0, 0
            for at, code in mid_list:
                mid_code += jnp.where(i == at, code, 0)
            for at, code in end_list:
                end_code += jnp.where(i == at, code, 0)
            relay(jnp.where(ends, end_code, mid_code))

    def compute(i):
        kind, role, j, rx, new = task(i)
        slot = i % RING

        whole = middle | (role == END) | (role == NEAR)

        @pl.when((new == 1) & whole)
        def _():
            to_core(role, j).wait_recv()

        @pl.when((new == 1) & jnp.logical_not(whole))
        def _():
            to_core_low(role, j).wait_recv()

        @pl.when(middle & (i == LENT))
        def _():
            for k in range(2):
                lend_ctx(k).wait_recv()
                lend_swap(k).start()

        @pl.when(middle & (i == lent_swapped))
        def _():
            for k in range(2):
                lend_swap(k).wait_recv()

        @pl.when(i == swapped)
        def _():
            for k in range(2):
                for r in range(2):
                    swap_ctx(k, r).wait_recv()
            pass

        @pl.when(i == spread)
        def _():
            for other in other_planes():
                queries_z(other, z).wait_recv()
            queries_x(x).start()

        @pl.when(i == spread_core)
        def _():
            queries_x(1 - x).wait_recv()
            queries_y(t_at).start()
            queries_core(0, t_at).start()

        def product(acts, block):
            return jnp.dot(acts, block, preferred_element_type=f32)

        @pl.when(kind == FULL)
        def _():
            sums[...] = product(ctx[0, rx], wgt[0, role, j]) + product(ctx[1, rx], wgt[1, role, j])

        @pl.when(kind == LOW)
        def _():
            sums[...] = product(ctx[0, rx, :, low], wgt[0, role, j, low]) + product(
                ctx[1, rx, :, low], wgt[1, role, j, low]
            )

        @pl.when(kind == SIDE)
        def _():
            sums[...] = product(ctx_end[0, rx], wgt[0, role, j, deep]) + product(
                ctx_end[1, rx], wgt[1, role, j, deep]
            )

        @pl.when(i >= RING)
        def _():
            to_y(role, j, rx, slot).wait_send()

        pack(stage.at[slot], sums[rows:])
        hold[slot] = sums[:rows]

        @pl.when(kind == SIDE)
        def _():
            side_to_y(role, j, rx, slot).start()

        @pl.when(kind != SIDE)
        def _():
            to_y(role, j, rx, slot).start()

    def settle(k, total):
        total = total + res[:, lanes(k)].astype(f32)
        hid[k] = total
        square[...] += total * total
        write_out(k).start()

    def add_y(i):
        kind, role, j, rx, _ = task(i)
        slot = i % RING
        at = place(role)

        @pl.when(kind == SIDE)
        def _():
            side_to_y(role, j, rx, slot).wait_recv()
            pack(side.at[at, j, rx], hold[slot] + unpack(side.at[at, j, rx]))
            side_to_end(role, j, rx).start()

        @pl.when(kind != SIDE)
        def _():
            to_y(role, j, rx, slot).wait_recv()

        @pl.when(kind == LOW)
        def _():
            side_to_end(role, j, rx).wait_recv()
            hold[slot] += unpack(side.at[at, j, rx])

        @pl.when((kind != SIDE) & (rx == 0))
        def _():
            settle(piece(role, x, j), hold[slot] + unpack(from_y.at[role, j, 0]))

        @pl.when((kind != SIDE) & (rx == 1))
        def _():
            pack(from_y.at[role, j, 1], hold[slot] + unpack(from_y.at[role, j, 1]))
            to_x(role, j).start()

    def add_x(i):
        kind, role, j, rx, _ = task(i)

        @pl.when((kind != SIDE) & (rx == 1))
        def _():
            to_x(role, j).wait_recv()
            settle(piece(role, 1 - x, j), unpack(from_x.at[role, j]))

    def step(i, carry):
        relays(i)

        @pl.when(i >= lag_x)
        def _():
            add_x(i - lag_x)

        @pl.when((i >= LAG) & (i < steps + LAG))
        def _():
            add_y(i - LAG)

        @pl.when(i < steps)
        def _():
            compute(i)

        return carry

    lax.fori_loop(0, steps + lag_x, step, 0)

    near_core = t_at + 1 - 2 * core
    queries_y((t_at + 2) % 4).wait_recv()
    queries_core(1, (t_at + 2) % 4).start()
    queries_core(0, near_core).wait_recv()
    queries_core(1, (near_core + 2) % 4).wait_recv()
    inv = lax.rsqrt(jnp.sum(square[...], axis=1, keepdims=True) / width + 1e-05)
    inv_lanes = jnp.broadcast_to(inv, (rows, LANES))
    square[...] = inv_lanes

    def pool(n, carry):
        for h in range(2):
            k = h * half + n
            total = jnp.sum(hid[k] * square[...], axis=0, keepdims=True)
            pooled[h : h + 1, lanes(n)] = total * gain_ref[pl.ds(k, 1), :]
        return carry

    lax.fori_loop(0, half, pool, 0)
    scale = 1.0 / math.sqrt(width * SEQ)
    count = 8 * 2 * nz
    found = jnp.zeros((8, count), f32)
    for t in range(4):
        here = pl.ds(t * share, share)
        block = every_q[t, :, :, :, :share].reshape(count, share)
        found += lax.dot_general(
            pooled[:, here],
            block,
            (((1,), (1,)), ((), ())),
            precision=high,
            preferred_element_type=f32,
        )
    found = jnp.concatenate([found, jnp.zeros((8, LANES - count), f32)], axis=1) * scale
    kept = jnp.sum(jnp.where(row == lane % 2, found, 0.0), axis=0, keepdims=True)
    kept = jnp.broadcast_to(kept, (8, LANES))
    after, before = pltpu.roll(kept, LANES - 1, 1), pltpu.roll(kept, 1, 1)
    board[group, z] = kept + jnp.where(lane % 2 == 0, after, before)

    for other in other_planes():
        scores_z(z, other).start()
    info = jnp.zeros((8, 2 * LANES), f32)
    for xs in range(2):
        for zs in range(nz):
            info += every_q[0, xs, zs, :, share:]
    ids, facts = info[:, :LANES], info[:, LANES:]
    for other in other_planes():
        scores_z(other, z).wait_recv()
    for other in other_groups():
        scores_plane(group, other).start()
    for other in other_groups():
        scores_plane(other, group).wait_recv()

    picked = jnp.zeros((8, LANES), f32)
    for zs in range(nz):
        for xs in range(2):
            for ys in range(2):
                score = board[4 * xs + 2 * ys, zs] + board[4 * xs + 2 * ys + 1, zs]
                picked += jnp.where(ids == 2 * (2 * zs + xs) + ys, score, 0.0)
    counts = jnp.broadcast_to(facts[0:1], (8, LANES))
    err = jnp.broadcast_to(picked[0:1], (8, LANES)) - picked - facts
    live = (row >= 1) & ((row - 1).astype(f32) < counts)
    err = jnp.where(live, err, 0.0)
    counts = jnp.where(counts > 0, counts, 1.0)
    nquery = Q_DEV * 2 * nz
    terms = jnp.where(lane % 2 == 0, err * err / counts, 0.0)
    loss_ref[0, 0] = jnp.sum(terms) / nquery
    weight = 2.0 * err / (counts * nquery)
    passage = (PASS_DEV * dp_at + y).astype(f32)
    at_pos = jnp.broadcast_to(jnp.where(ids[0:1] == passage, 1.0, 0.0), (8, LANES))
    at_neg = jnp.where(ids == passage, 1.0, 0.0)
    coef = jnp.sum(weight * (at_pos - at_neg), axis=0, keepdims=True)
    coef = jnp.where(row == lane % 2, jnp.broadcast_to(coef, (8, LANES)), 0.0)[:, :count]
    for t in range(4):
        here = pl.ds(t * share, share)
        block = every_q[t, :, :, :, :share].reshape(count, share)
        grad = jnp.dot(coef, block, precision=high, preferred_element_type=f32)
        pooled[:, here] = grad * scale

    def align(n, total):
        for h in range(2):
            k = h * half + n
            up = pooled[h : h + 1, lanes(n)] * gain_ref[pl.ds(k, 1), :]
            up_ref[0:1, lanes(k)] = up
            total += hid[k] * up
        return total

    total = lax.fori_loop(0, half, align, jnp.zeros((rows, LANES), f32))
    inner = jnp.sum(total, axis=1, keepdims=True) / width
    up_ref[1:, :] = jnp.zeros((7, width), f32)
    factor_ref[0] = 65536.0 * square[...]
    factor_ref[1] = jnp.broadcast_to(-65536.0 * (inv * inv * inv * inner), (rows, LANES))

    for other in other_planes():
        queries_z(z, other).wait_send()
        scores_z(z, other).wait_send()
    for other in other_groups():
        scores_plane(group, other).wait_send()
    queries_x(x).wait_send()
    queries_y(t_at).wait_send()
    for n in range(2):
        queries_core(n, t_at).wait_send()

    for n in range(RING):
        to_y(0, 0, 0, n).wait_send()
    for r in range(2):
        core_ctx(r).wait_send()
        for k in range(2):
            swap_ctx(k, r).wait_send()

    @pl.when(ends)
    def _():
        for k in range(2):
            lend_ctx(k).wait_send()

    @pl.when(middle)
    def _():
        for k in range(2):
            lend_swap(k).wait_send()

    def drain(j, carry):
        for role in (NEAR, NEXT, END, FAR):
            to_x(role, j).wait_send()
            for xt in range(2):
                write_out(piece(role, xt, j)).wait()
        for role in (NEAR, END):
            to_core(role, j).wait_send()

        @pl.when(ends)
        def _():
            to_mid(j).wait_send()
            for role in (NEXT, FAR):
                to_core_low(role, j).wait_send()

        @pl.when(middle)
        def _():
            for role in (NEAR, END):
                to_next(role, j).wait_send()
            to_end_whole(j).wait_send()
            for role in (NEXT, FAR):
                to_core(role, j).wait_send()
                to_end(role, j).wait_send()
                for rx in range(2):
                    side_to_end(role, j, rx).wait_send()

        return carry

    lax.fori_loop(0, chunks, drain, 0)


def tile_hidden(context, o_weight, resid, gain, queries, facts):
    rows, width = resid.shape
    depth, columns = o_weight.shape
    chunks = columns // LANES
    nz = width // (2 * columns)
    f32, bf16 = jnp.float32, jnp.bfloat16
    coded_rows = rows + 16
    dma = pltpu.SemaphoreType.DMA
    return pl.pallas_call(
        functools.partial(tile_kernel, nz),
        out_shape=(
            jax.ShapeDtypeStruct((rows, width), f32),
            jax.ShapeDtypeStruct((2, rows, LANES), f32),
            jax.ShapeDtypeStruct((8, width), f32),
            jax.ShapeDtypeStruct((1, 1), f32),
        ),
        in_specs=[pl.BlockSpec(memory_space=pl.ANY)] * 3
        + [pl.BlockSpec(memory_space=pltpu.VMEM)] * 2
        + [pl.BlockSpec(memory_space=pltpu.SMEM)] * 4,
        out_specs=(
            pl.BlockSpec(memory_space=pl.ANY),
            pl.BlockSpec(memory_space=pltpu.VMEM),
            pl.BlockSpec(memory_space=pltpu.VMEM),
            pl.BlockSpec(memory_space=pltpu.SMEM),
        ),
        scratch_shapes=[
            pltpu.VMEM((2, 2, 2 * rows, depth), bf16),
            pltpu.VMEM((2, 2, 2 * rows, depth // 2), bf16),
            pltpu.VMEM((2, nz, chunks, depth, LANES), bf16),
            pltpu.VMEM((nz, chunks, 2, coded_rows, LANES), jnp.int16),
            pltpu.VMEM((nz, chunks, coded_rows, LANES), jnp.int16),
            pltpu.VMEM((nz // 2, chunks, 2, coded_rows, LANES), jnp.int16),
            pltpu.VMEM((2 * nz * chunks, rows, LANES), f32),
            pltpu.VMEM((rows, width), bf16),
            pltpu.VMEM((RING, coded_rows, LANES), jnp.int16),
            pltpu.VMEM((RING, rows, LANES), f32),
            pltpu.VMEM((2 * rows, LANES), f32),
            dma((2,)),
            dma((2, 2)),
            dma((2, 2, 2)),
            dma((2, 2)),
            dma((2, 2)),
            dma((chunks,)),
            dma((nz, chunks)),
            dma((nz, chunks)),
            dma((nz, chunks)),
            dma((2, nz, chunks)),
            dma((RING,)),
            dma((nz, chunks, 2)),
            dma((nz // 2, chunks, 2)),
            dma((nz // 2, chunks, 2)),
            dma((nz, chunks)),
            dma((nz, chunks)),
            dma,
            dma((2 * nz * chunks,)),
            pltpu.VMEM((4, 2, nz, 2 * Q_DEV, width // 8 + 2 * LANES), f32),
            pltpu.VMEM((rows, LANES), f32),
            pltpu.VMEM((8, width // 2), f32),
            pltpu.VMEM((8, nz, 8, LANES), f32),
            dma((2, nz)),
            dma((2,)),
            dma((2,)),
            dma((2, 2)),
            dma((2, nz)),
            dma((2, 8)),
        ],
        compiler_params=pltpu.CompilerParams(
            collective_id=0, has_side_effects=True, vmem_limit_bytes=58 << 20
        ),
        cost_estimate=pl.CostEstimate(
            flops=2 * 4 * rows * depth * width, bytes_accessed=4 * rows * width, transcendentals=0
        ),
    )(context, o_weight, resid, gain, queries, *facts)


def grad_kernel(hidden_ref, factor_ref, up_ref, grad_ref):
    for n in range(grad_ref.shape[1] // LANES):
        here = pl.ds(n * LANES, LANES)
        grad_ref[:, here] = factor_ref[0] * up_ref[0:1, here] + factor_ref[1] * hidden_ref[:, here]


def gradient(hidden, factors, upward):
    rows, width = hidden.shape
    step = rows // 4
    return pl.pallas_call(
        grad_kernel,
        out_shape=jax.ShapeDtypeStruct((rows, width), jnp.float32),
        grid=(rows // step,),
        in_specs=[
            pl.BlockSpec((step, width), lambda n: (n, 0)),
            pl.BlockSpec((2, step, LANES), lambda n: (0, n, 0)),
            pl.BlockSpec((8, width), lambda n: (0, 0)),
        ],
        out_specs=pl.BlockSpec((step, width), lambda n: (n, 0)),
        compiler_params=pltpu.CompilerParams(vmem_limit_bytes=58 << 20),
    )(hidden, factors, upward)


def line_shards(
    context, resid, o_weight, norm_gain, queries, positive_ids, negative_ids, margins, pair_counts
):
    gain = norm_gain.reshape(-1, LANES)
    facts = (positive_ids, negative_ids, margins, pair_counts)
    hidden, factors, upward, loss = tile_hidden(context, o_weight, resid, gain, queries, facts)
    return (gradient(hidden, factors, upward), loss.reshape(()))


def solution(mesh):
    body = line_shards if dict(mesh.shape) == {"dp": 8, "tensor": 4} else shards
    return jax.shard_map(
        body,
        mesh=mesh,
        in_specs=(
            P("dp", "tensor"),
            P(("dp", "tensor"), None),
            P("tensor", "dp"),
            P(),
            P("dp", None),
            P("dp"),
            P("dp", None),
            P("dp", None),
            P("dp"),
        ),
        out_specs=(P(("dp", "tensor"), None), P()),
        check_vma=False,
    )
```

```python
import functools
import math

import jax
import jax.numpy as jnp
from jax import lax
from jax.experimental import pallas as pl
from jax.experimental.pallas import tpu as pltpu
from jax.sharding import PartitionSpec as P

D = 7168
SEQ = 512
PASS_DEV = 2
Q_DEV = 4
NEG = 7


def shards(
    context, resid, o_weight, norm_gain, queries, positive_ids, negative_ids, margins, pair_counts
):
    full_weight = lax.all_gather(o_weight, "dp", axis=1, tiled=True)
    tok_rows = resid.shape[0]
    attn = lax.psum_scatter(
        jnp.dot(context, full_weight, preferred_element_type=jnp.float32),
        "tensor",
        scatter_dimension=0,
        tiled=True,
    )
    hidden = resid.astype(jnp.float32) + attn
    inv = lax.rsqrt(jnp.mean(hidden * hidden, axis=-1, keepdims=True) + 1e-05)
    normed = hidden * inv * norm_gain
    first = lax.axis_index("tensor") * tok_rows
    passage_of = (first + jnp.arange(tok_rows, dtype=jnp.int32)) // SEQ
    member = (passage_of[None, :] == jnp.arange(PASS_DEV, dtype=jnp.int32)[:, None]).astype(
        jnp.float32
    )
    partial_value = jnp.dot(member, normed, precision=lax.Precision.HIGHEST)
    scale = 1.0 / jnp.sqrt(jnp.float32(D * SEQ))
    npass = PASS_DEV * lax.axis_size("dp")
    nquery = Q_DEV * lax.axis_size("dp")
    pooled = lax.psum(partial_value, "tensor")
    every_pass = lax.all_gather(pooled, "dp", axis=0, tiled=True)
    scores = jnp.dot(queries, every_pass.T, precision=lax.Precision.HIGHEST) * scale
    passes = jnp.arange(npass, dtype=jnp.int32)
    onehot_pos = (positive_ids[:, None] == passes[None, :]).astype(jnp.float32)
    onehot_neg = (negative_ids[:, :, None] == passes[None, None, :]).astype(jnp.float32)
    score_pos = jnp.sum(onehot_pos * scores, axis=-1)
    score_neg = jnp.sum(onehot_neg * scores[:, None, :], axis=-1)
    err = score_pos[:, None] - score_neg - margins
    live = (jnp.arange(NEG, dtype=jnp.int32)[None, :] < pair_counts[:, None]).astype(jnp.float32)
    counts = pair_counts.astype(jnp.float32)
    local_loss = jnp.sum(jnp.sum(live * err * err, axis=1) / counts) / nquery
    weight = 2.0 * live * err / (counts[:, None] * nquery)
    coef = onehot_pos * jnp.sum(weight, axis=1)[:, None] - jnp.sum(
        weight[:, :, None] * onehot_neg, axis=1
    )
    grad_terms = jnp.dot(coef.T, queries, precision=lax.Precision.HIGHEST) * scale
    pass_grad = lax.psum_scatter(grad_terms, "dp", scatter_dimension=0, tiled=True)
    loss = lax.psum(local_loss, "dp")
    upward = jnp.dot(member.T, pass_grad, precision=lax.Precision.HIGHEST) * norm_gain
    inner = jnp.mean(hidden * upward, axis=-1, keepdims=True)
    grad = 65536.0 * (inv * upward - hidden * inv * inv * inv * inner)
    return (grad, loss)


MESH = pl.DeviceIdType.MESH
LANES = 128
LAG_Y = (5, 3)
LAG_X = (32, 6)
RING = 7
TOP = 32600.0
FULL, LOW, SIDE = 0, 1, 2
NEAR, NEXT, END, FAR = 0, 1, 2, 3
CHUNKS = 7

MIDDLE = (
    (FULL, NEAR, 0, 0, 7),
    (FULL, NEXT, 0, 0, 3),
    (SIDE, NEXT, 0, 0, 4),
    (FULL, NEXT, 0, 3, 4),
    (FULL, END, 0, 0, 1),
    (SIDE, NEXT, 0, 4, 5),
    (FULL, NEXT, 0, 4, 5),
    (FULL, END, 0, 1, 2),
    (SIDE, NEXT, 0, 5, 6),
    (FULL, NEXT, 0, 5, 6),
    (FULL, END, 0, 2, 3),
    (SIDE, NEXT, 0, 6, 7),
    (FULL, NEXT, 0, 6, 7),
    (FULL, NEAR, 1, 0, 6),
    (SIDE, FAR, 0, 0, 1),
    (FULL, NEAR, 1, 6, 7),
    (FULL, NEXT, 1, 0, 6),
    (SIDE, FAR, 0, 1, 2),
    (FULL, NEXT, 1, 6, 7),
    (FULL, END, 1, 0, 4),
    (SIDE, FAR, 0, 2, 3),
    (FULL, END, 1, 4, 6),
    (FULL, FAR, 1, 0, 2),
    (FULL, END, 1, 6, 7),
    (SIDE, FAR, 0, 3, 4),
    (FULL, FAR, 1, 2, 4),
    (SIDE, NEXT, 1, 0, 7),
    (SIDE, FAR, 1, 0, 6),
    (SIDE, FAR, 0, 4, 6),
    (FULL, FAR, 1, 4, 6),
    (FULL, END, 0, 3, 4),
    (SIDE, FAR, 1, 6, 7),
    (SIDE, FAR, 0, 6, 7),
    (FULL, FAR, 1, 6, 7),
    (FULL, END, 0, 4, 7),
    (FULL, FAR, 0, 0, 7),
)

ENDS = (
    (FULL, END, 0, 0, 7),
    (FULL, NEAR, 0, 0, 7),
    (FULL, END, 1, 0, 7),
    (FULL, NEAR, 1, 0, 7),
    (LOW, NEXT, 0, 0, 7),
    (LOW, FAR, 0, 0, 4),
    (LOW, NEXT, 1, 0, 7),
    (LOW, FAR, 1, 0, 6),
    (LOW, FAR, 0, 4, 6),
    (LOW, FAR, 1, 6, 7),
    (LOW, FAR, 0, 6, 7),
)

MIDDLE_RELAYS = (
    (7, NEXT, 0),
    (8, NEXT, 1),
    (9, NEXT, 2),
    (13, NEXT, 3),
    (15, END, 0),
    (15, NEXT, 4),
    (18, END, 1),
    (18, NEXT, 5),
    (21, END, 2),
    (21, NEXT, 6),
    (25, END, 3),
    (27, FAR, 0),
    (33, END, 4),
    (35, FAR, 1),
    (40, END, 5),
    (41, FAR, 2),
    (47, END, 6),
    (48, FAR, 3),
    (56, FAR, 4),
    (62, FAR, 5),
    (69, FAR, 6),
)
END_RELAYS = (
    (4, NEAR, 0),
    (5, NEAR, 1),
    (6, NEAR, 2),
    (7, NEAR, 3),
    (8, NEAR, 4),
    (9, NEAR, 5),
    (10, NEAR, 6),
    (15, NEXT, 0),
    (17, NEXT, 1),
    (20, NEXT, 2),
    (23, NEXT, 3),
    (28, NEXT, 4),
    (30, NEXT, 5),
    (31, NEXT, 6),
    (32, FAR, 0),
    (33, FAR, 1),
    (34, FAR, 2),
    (35, FAR, 3),
    (42, FAR, 4),
    (47, FAR, 5),
    (51, FAR, 6),
)
MIDDLE_PAIRS = (
    4, 10, 24, 26, 28, 32, 34, 36, 40, 42, 45, 47, 51, 53, 55, 57, 60, 62, 64, 66, 68, 74, 77, 79,
    81,
)
END_PAIRS = (
    0, 2, 4, 7, 9, 11, 14, 16, 18, 21, 23, 25, 28, 30, 32, 35, 37, 39, 41, 43, 46, 48, 50, 52,
)
LENT = 10


def listed(runs):
    return [(kind, role, rx, j) for kind, role, rx, lo, hi in runs for j in range(lo, hi)]


def coded(tasks, pairs):
    met, fresh = set(), []
    for kind, role, rx, j in tasks:
        fresh.append((role, j) not in met)
        met.add((role, j))
    last, marks = -1, []
    for i, (kind, role, rx, j) in enumerate(tasks):
        lead, follow = i in pairs, i - 1 in pairs
        code = j + 8 * rx + 16 * role + 64 * kind + 256 * (fresh[i] and not follow)
        code += 512 * lead + 1024 * follow + 2048 * (lead and fresh[i + 1])
        if code != last + 1 or i == 0:
            marks.append((i, code - (last + 1)))
        last = code
    return marks


def events(relays):
    first, second, steps = [], [], set()
    for step, role, j in relays:
        (second if step in steps else first).append((step, 8 * role + j + 1))
        steps.add(step)
    return first, second


def tile_kernel(
    nz,
    ctx_ref,
    weight_ref,
    resid_ref,
    gain_ref,
    query_ref,
    positive_ref,
    negative_ref,
    margin_ref,
    count_ref,
    out_ref,
    factor_ref,
    up_ref,
    loss_ref,
    ctx,
    ctx_end,
    wgt,
    from_y,
    from_x,
    side,
    hid,
    res,
    stage,
    hold,
    sums,
    ctx_load,
    ctx_core,
    ctx_x,
    end_z,
    end_x,
    w_load,
    w_end,
    w_mid,
    w_recv,
    w_core,
    y_send,
    y_recv,
    side_send,
    side_recv,
    x_send,
    x_recv,
    res_sem,
    out_sem,
    every_q,
    square,
    pooled,
    board,
    q_z,
    q_x,
    q_y,
    q_core,
    s_z,
    s_plane,
):
    dp_at, t_at = lax.axis_index("dp"), lax.axis_index("tensor")
    z, x = dp_at // 2, dp_at % 2
    y, core = t_at // 2, t_at % 2
    chunks = wgt.shape[2]
    depth = wgt.shape[3]
    low, deep = pl.ds(0, depth // 2), pl.ds(depth // 2, depth // 2)
    rows = hid.shape[1]
    group = 4 * x + t_at
    mid_z = jnp.where(z < nz // 2, 1, nz - 2)
    end_z_at = jnp.where(z < nz // 2, 0, nz - 1)
    ends = z == end_z_at
    middle = jnp.logical_not(ends)
    own = jnp.where(ends, END, NEAR)
    other_core = (dp_at, 2 * y + 1 - core)
    y_peer = (dp_at, 2 * (1 - y) + core)
    x_peer = (2 * z + 1 - x, t_at)
    end_peer = (2 * end_z_at + x, t_at)
    mid_peer = (2 * mid_z + x, t_at)
    next_peer = (2 * (nz - 1 - mid_z) + x, t_at)

    def z_peer(other):
        return (2 * other + x, t_at)

    def plane_peer(other):
        return (2 * z + other // 4, other % 4)

    def other_groups():
        return [(group + m) % 8 for m in range(1, 8)]

    def other_planes():
        return [(z + m) % nz for m in range(1, nz)]

    barrier = pltpu.get_barrier_semaphore()
    for other in other_groups():
        pl.semaphore_signal(barrier, inc=1, device_id=plane_peer(other), device_id_type=MESH)
    for other in other_planes():
        pl.semaphore_signal(barrier, inc=1, device_id=z_peer(other), device_id_type=MESH)

    def remote(src, dst, send, recv, peer):
        return pltpu.make_async_remote_copy(
            src_ref=src,
            dst_ref=dst,
            send_sem=send,
            recv_sem=recv,
            device_id=peer,
            device_id_type=MESH,
        )

    def load_weight(j):
        return pltpu.make_async_copy(
            weight_ref.at[:, pl.ds(j * LANES, LANES)], wgt.at[0, own, j], w_load.at[j]
        )

    def quarter(r, c):
        return pl.ds(pl.multiple_of((2 * ((y + r) % 2) + c) * rows, rows), rows)

    def load_ctx(r):
        return pltpu.make_async_copy(
            ctx_ref.at[quarter(r, core)], ctx.at[0, 0, pl.ds(r * rows, rows)], ctx_load.at[r]
        )

    def core_ctx(r):
        return remote(
            ctx_ref.at[quarter(r, 1 - core)],
            ctx.at[1, 0, pl.ds(r * rows, rows)],
            ctx_core.at[0, r],
            ctx_core.at[1, r],
            other_core,
        )

    def swap_ctx(k, r):
        block = pl.ds(r * rows, rows)
        return remote(
            ctx.at[k, 0, block], ctx.at[k, 1, block], ctx_x.at[0, k, r], ctx_x.at[1, k, r], x_peer
        )

    def lend_ctx(k):
        return remote(
            ctx.at[k, 0, :, deep], ctx_end.at[k, 0], end_z.at[0, k], end_z.at[1, k], mid_peer
        )

    def lend_swap(k):
        return remote(
            ctx_end.at[k, 0], ctx_end.at[k, 1], end_x.at[0, k], end_x.at[1, k], x_peer
        )

    def to_end(role, j):
        return remote(
            wgt.at[0, role, j, low],
            wgt.at[0, role, j, low],
            w_end.at[role, j],
            w_recv.at[role, j],
            end_peer,
        )

    def to_end_whole(j):
        return remote(
            wgt.at[0, NEAR, j], wgt.at[0, NEAR, j], w_end.at[NEAR, j], w_recv.at[NEAR, j], end_peer
        )

    def to_next(role, j):
        return remote(
            wgt.at[0, role, j],
            wgt.at[0, role + 1, j],
            w_mid.at[role, j],
            w_recv.at[role + 1, j],
            next_peer,
        )

    def to_mid(j):
        return remote(
            wgt.at[0, END, j], wgt.at[0, END, j], w_mid.at[END, j], w_recv.at[END, j], mid_peer
        )

    def to_core(role, j):
        return remote(
            wgt.at[0, role, j],
            wgt.at[1, role, j],
            w_core.at[0, role, j],
            w_core.at[1, role, j],
            other_core,
        )

    def to_core_low(role, j):
        return remote(
            wgt.at[0, role, j, low],
            wgt.at[1, role, j, low],
            w_core.at[0, role, j],
            w_core.at[1, role, j],
            other_core,
        )

    def to_y(role, j, rx, slot):
        return remote(
            stage.at[slot], from_y.at[role, j, rx], y_send.at[slot], y_recv.at[role, j, rx], y_peer
        )

    def place(role):
        return role // 2

    def side_to_y(role, j, rx, slot):
        at = place(role)
        return remote(
            stage.at[slot], side.at[at, j, rx], y_send.at[slot], side_recv.at[at, j, rx], y_peer
        )

    def side_to_end(role, j, rx):
        at = place(role)
        return remote(
            side.at[at, j, rx],
            side.at[at, j, rx],
            side_send.at[at, j, rx],
            side_recv.at[at, j, rx],
            end_peer,
        )

    def piece(role, xt, j):
        first = jnp.where(role < END, mid_z, end_z_at)
        zt = jnp.where(role % 2 == 0, first, nz - 1 - first)
        return (2 * zt + xt) * chunks + j

    def to_x(role, j):
        return remote(
            from_y.at[role, j, 1], from_x.at[role, j], x_send.at[role, j], x_recv.at[role, j], x_peer
        )

    def lanes(k):
        return pl.ds(pl.multiple_of(k * LANES, LANES), LANES)

    def write_out(k):
        return pltpu.make_async_copy(hid.at[k], out_ref.at[:, lanes(k)], out_sem.at[k])

    def scale_of(level):
        return jnp.exp2(level * (1.0 / 128.0)) * (1.0 / TOP)

    def pack(ref, value):
        top = jnp.maximum(jnp.max(jnp.abs(value), axis=0, keepdims=True), 1e-30)
        level = jnp.ceil(jnp.log2(top) * 128.0)
        ref[:rows] = jnp.round(value * (1.0 / scale_of(level))).astype(jnp.int32).astype(jnp.int16)
        level = jnp.broadcast_to(level, (16, LANES))
        ref[rows:] = level.astype(jnp.int32).astype(jnp.int16)

    def unpack(ref):
        level = ref[rows:].astype(jnp.int32).astype(jnp.float32)[:1]
        return ref[:rows].astype(jnp.int32).astype(jnp.float32) * scale_of(level)

    load_res = pltpu.make_async_copy(resid_ref, res, res_sem)

    def queries_z(source, target):
        mine = every_q.at[t_at, x, source]
        return remote(mine, mine, q_z.at[0, target], q_z.at[1, source], z_peer(target))

    def queries_x(xs):
        mine = every_q.at[t_at, xs]
        return remote(mine, mine, q_x.at[0], q_x.at[1], x_peer)

    def queries_y(ts, xs, n):
        block = every_q.at[ts, xs, :, :, pl.ds(0, share)]
        return remote(block, block, q_y.at[0, n], q_y.at[1, n], y_peer)

    def queries_core(n, ts):
        block = every_q.at[ts, :, :, :, pl.ds(0, share)]
        return remote(block, block, q_core.at[0, n], q_core.at[1, n], other_core)

    def scores_z(source, target):
        mine = board.at[group, source]
        return remote(mine, mine, s_z.at[0, target], s_z.at[1, source], z_peer(target))

    def scores_plane(source, target):
        return remote(
            board.at[source],
            board.at[source],
            s_plane.at[0, target],
            s_plane.at[1, source],
            plane_peer(target),
        )

    for j in range(chunks):
        load_weight(j).start()
    for r in range(2):
        load_ctx(r).start()
    load_res.start()
    f32, high = jnp.float32, lax.Precision.HIGHEST
    width = 2 * nz * chunks * LANES
    half, share = nz * chunks, every_q.shape[4] - 2 * LANES
    row = lax.broadcasted_iota(jnp.int32, (8, LANES), 0)
    lane = lax.broadcasted_iota(jnp.int32, (8, LANES), 1)
    own_q = every_q.at[t_at, x, z]
    at = lane - 8 * (nz * x + z)
    ids = jnp.zeros((8, LANES), f32)
    facts = jnp.zeros((8, LANES), f32)
    for r in range(Q_DEV):
        for h in range(2):
            part = pl.ds(pl.multiple_of(h * (width // 2) + t_at * share, LANES), share)
            own_q[2 * r + h : 2 * r + h + 1, :share] = query_ref[r : r + 1, part]
        mine = (at == 2 * r) | (at == 2 * r + 1)
        ids = jnp.where(mine & (row == 0), positive_ref[r].astype(f32), ids)
        facts = jnp.where(mine & (row == 0), count_ref[r].astype(f32), facts)
        for k in range(NEG):
            ids = jnp.where(mine & (row == k + 1), negative_ref[r, k].astype(f32), ids)
            facts = jnp.where(mine & (row == k + 1), margin_ref[r, k], facts)
    own_q[:, share : share + LANES] = ids
    own_q[:, share + LANES :] = facts
    pl.semaphore_wait(barrier, 7 + nz - 1)
    for other in other_planes():
        queries_z(z, other).start()
    for r in range(2):
        core_ctx(r).start()

    @pl.when(middle)
    def _():
        for j in range(chunks):
            load_weight(j).wait()
            to_end_whole(j).start()
            to_next(NEAR, j).start()
            to_core(NEAR, j).start()

    for r in range(2):
        load_ctx(r).wait()
        swap_ctx(0, r).start()

    @pl.when(ends)
    def _():
        lend_ctx(0).start()

    for r in range(2):
        core_ctx(r).wait_recv()
        swap_ctx(1, r).start()

    @pl.when(ends)
    def _():
        lend_ctx(1).start()
        for j in range(chunks):
            load_weight(j).wait()
            to_mid(j).start()
            to_core(END, j).start()

    square[...] = jnp.zeros_like(square)
    pooled[...] = jnp.zeros_like(pooled)
    load_res.wait()

    mid_tasks, end_tasks = listed(MIDDLE), listed(ENDS)
    mid_marks, end_marks = coded(mid_tasks, MIDDLE_PAIRS), coded(end_tasks, END_PAIRS)
    steps = jnp.where(ends, len(end_tasks), len(mid_tasks))
    lent_swapped = [task[0] == SIDE and task[2] == 1 for task in mid_tasks].index(True)
    own_swapped = [task[0] == FULL and task[2] == 1 for task in mid_tasks].index(True)
    end_swapped = [task[2] for task in end_tasks].index(1)
    swapped = jnp.where(ends, end_swapped, own_swapped)
    gathered = jnp.where(ends, chunks, LENT)
    spread_core = jnp.where(ends, len(end_tasks) - chunks, len(mid_tasks) - chunks)
    lag_y = jnp.where(ends, LAG_Y[1], LAG_Y[0])
    lag_x = jnp.where(ends, LAG_X[1], LAG_X[0])
    mid_events, end_events = events(MIDDLE_RELAYS), events(END_RELAYS)

    def task(i):
        mid_code, end_code = i, i
        for start, more in mid_marks:
            mid_code += jnp.where(i >= start, more, 0)
        for start, more in end_marks:
            end_code += jnp.where(i >= start, more, 0)
        code = jnp.where(ends, end_code, mid_code)
        return code // 64 % 4, code // 16 % 4, code % 8, code // 8 % 2, code // 256

    def relay(code):
        role, j = (code - 1) // 8, (code - 1) % 8

        @pl.when((code > 0) & middle)
        def _():
            arriving = remote(
                wgt.at[0, role, j],
                wgt.at[0, role, j],
                w_mid.at[role, j],
                w_recv.at[role, j],
                next_peer,
            )
            arriving.wait_recv()

            @pl.when(role == END)
            def _():
                to_next(END, j).start()

            @pl.when(role != END)
            def _():
                to_end(role, j).start()

            to_core(role, j).start()

        @pl.when((code > 0) & ends & (role == NEAR))
        def _():
            to_end_whole(j).wait_recv()
            to_core(role, j).start()

        @pl.when((code > 0) & ends & (role != NEAR))
        def _():
            to_end(role, j).wait_recv()
            to_core_low(role, j).start()

    def relays(i):
        for mid_list, end_list in zip(mid_events, end_events):
            mid_code, end_code = 0, 0
            for at, code in mid_list:
                mid_code += jnp.where(i == at, code, 0)
            for at, code in end_list:
                end_code += jnp.where(i == at, code, 0)
            relay(jnp.where(ends, end_code, mid_code))

    def compute(i):
        kind, role, j, rx, flags = task(i)
        new, lead, follow, new_next = flags % 2, flags // 2 % 2, flags // 4 % 2, flags // 8
        slot = i % RING

        whole = middle | (role == END) | (role == NEAR)

        @pl.when((new == 1) & whole)
        def _():
            to_core(role, j).wait_recv()

        @pl.when((new == 1) & jnp.logical_not(whole))
        def _():
            to_core_low(role, j).wait_recv()

        @pl.when(new_next == 1)
        def _():
            whole_next = middle | (role == END) | (role == NEAR)

            @pl.when(whole_next)
            def _():
                to_core(role, j + 1).wait_recv()

            @pl.when(jnp.logical_not(whole_next))
            def _():
                to_core_low(role, j + 1).wait_recv()

        @pl.when(middle & (i == LENT))
        def _():
            for k in range(2):
                lend_ctx(k).wait_recv()
                lend_swap(k).start()

        @pl.when(middle & (i == lent_swapped))
        def _():
            for k in range(2):
                lend_swap(k).wait_recv()

        @pl.when(i == swapped)
        def _():
            for k in range(2):
                for r in range(2):
                    swap_ctx(k, r).wait_recv()

        @pl.when(i == gathered)
        def _():
            for other in other_planes():
                queries_z(other, z).wait_recv()
            queries_y(t_at, x, 0).start()
            queries_x(x).start()

        @pl.when(i == spread_core)
        def _():
            queries_x(1 - x).wait_recv()
            queries_y(t_at, 1 - x, 1).start()
            queries_core(0, t_at).start()

        def product(acts, block):
            return jnp.dot(acts, block, preferred_element_type=f32)

        one, two = pl.ds(0, LANES), pl.ds(0, 2 * LANES)

        def pieces(k, part):
            return jnp.concatenate([wgt[k, role, j, part], wgt[k, role, j + 1, part]], axis=1)

        @pl.when((kind == FULL) & (lead == 1))
        def _():
            every = pl.ds(0, depth)
            sums[:, two] = product(ctx[0, rx], pieces(0, every)) + product(ctx[1, rx], pieces(1, every))

        @pl.when((kind == LOW) & (lead == 1))
        def _():
            sums[:, two] = product(ctx[0, rx, :, low], pieces(0, low)) + product(
                ctx[1, rx, :, low], pieces(1, low)
            )

        @pl.when((kind == SIDE) & (lead == 1))
        def _():
            sums[:, two] = product(ctx_end[0, rx], pieces(0, deep)) + product(
                ctx_end[1, rx], pieces(1, deep)
            )

        alone = (lead == 0) & (follow == 0)

        @pl.when((kind == FULL) & alone)
        def _():
            sums[:, one] = product(ctx[0, rx], wgt[0, role, j]) + product(ctx[1, rx], wgt[1, role, j])

        @pl.when((kind == LOW) & alone)
        def _():
            sums[:, one] = product(ctx[0, rx, :, low], wgt[0, role, j, low]) + product(
                ctx[1, rx, :, low], wgt[1, role, j, low]
            )

        @pl.when((kind == SIDE) & alone)
        def _():
            sums[:, one] = product(ctx_end[0, rx], wgt[0, role, j, deep]) + product(
                ctx_end[1, rx], wgt[1, role, j, deep]
            )

        @pl.when(i >= RING)
        def _():
            to_y(role, j, rx, slot).wait_send()

        here = pl.ds(pl.multiple_of(follow * LANES, LANES), LANES)
        pack(stage.at[slot], sums[rows:, here])
        hold[slot] = sums[:rows, here]

        @pl.when(kind == SIDE)
        def _():
            side_to_y(role, j, rx, slot).start()

        @pl.when(kind != SIDE)
        def _():
            to_y(role, j, rx, slot).start()

    def settle(k, total):
        total = total + res[:, lanes(k)].astype(f32)
        hid[k] = total
        square[...] += total * total
        write_out(k).start()

    def add_y(i):
        kind, role, j, rx, _ = task(i)
        slot = i % RING
        at = place(role)

        @pl.when(kind == SIDE)
        def _():
            side_to_y(role, j, rx, slot).wait_recv()
            pack(side.at[at, j, rx], hold[slot] + unpack(side.at[at, j, rx]))
            side_to_end(role, j, rx).start()

        @pl.when(kind != SIDE)
        def _():
            to_y(role, j, rx, slot).wait_recv()

        @pl.when(kind == LOW)
        def _():
            side_to_end(role, j, rx).wait_recv()
            hold[slot] += unpack(side.at[at, j, rx])

        @pl.when((kind != SIDE) & (rx == 0))
        def _():
            settle(piece(role, x, j), hold[slot] + unpack(from_y.at[role, j, 0]))

        @pl.when((kind != SIDE) & (rx == 1))
        def _():
            pack(from_y.at[role, j, 1], hold[slot] + unpack(from_y.at[role, j, 1]))
            to_x(role, j).start()

    def add_x(i):
        kind, role, j, rx, _ = task(i)

        @pl.when((kind != SIDE) & (rx == 1))
        def _():
            to_x(role, j).wait_recv()
            settle(piece(role, 1 - x, j), unpack(from_x.at[role, j]))

    def step(i, carry):
        relays(i)

        @pl.when(i >= lag_x)
        def _():
            add_x(i - lag_x)

        @pl.when((i >= lag_y) & (i < steps + lag_y))
        def _():
            add_y(i - lag_y)

        @pl.when(i < steps)
        def _():
            compute(i)

        return carry

    lax.fori_loop(0, steps + lag_x, step, 0)

    near_core = t_at + 1 - 2 * core
    queries_y((t_at + 2) % 4, x, 0).wait_recv()
    queries_y((t_at + 2) % 4, 1 - x, 1).wait_recv()
    queries_core(1, (t_at + 2) % 4).start()
    queries_core(0, near_core).wait_recv()
    queries_core(1, (near_core + 2) % 4).wait_recv()
    inv = lax.rsqrt(jnp.sum(square[...], axis=1, keepdims=True) / width + 1e-05)
    inv_lanes = jnp.broadcast_to(inv, (rows, LANES))
    square[...] = inv_lanes

    def pool(n, carry):
        for h in range(2):
            k = h * half + n
            total = jnp.sum(hid[k] * square[...], axis=0, keepdims=True)
            pooled[h : h + 1, lanes(n)] = total * gain_ref[pl.ds(k, 1), :]
        return carry

    lax.fori_loop(0, half, pool, 0)
    scale = 1.0 / math.sqrt(width * SEQ)
    count = 8 * 2 * nz
    found = jnp.zeros((8, count), f32)
    for t in range(4):
        here = pl.ds(t * share, share)
        block = every_q[t, :, :, :, :share].reshape(count, share)
        found += lax.dot_general(
            pooled[:, here],
            block,
            (((1,), (1,)), ((), ())),
            precision=high,
            preferred_element_type=f32,
        )
    found = jnp.concatenate([found, jnp.zeros((8, LANES - count), f32)], axis=1) * scale
    kept = jnp.sum(jnp.where(row == lane % 2, found, 0.0), axis=0, keepdims=True)
    kept = jnp.broadcast_to(kept, (8, LANES))
    after, before = pltpu.roll(kept, LANES - 1, 1), pltpu.roll(kept, 1, 1)
    board[group, z] = kept + jnp.where(lane % 2 == 0, after, before)

    for other in other_planes():
        scores_z(z, other).start()
    info = jnp.zeros((8, 2 * LANES), f32)
    for xs in range(2):
        for zs in range(nz):
            info += every_q[t_at, xs, zs, :, share:]
    ids, facts = info[:, :LANES], info[:, LANES:]
    for other in other_planes():
        scores_z(other, z).wait_recv()
    for other in other_groups():
        scores_plane(group, other).start()
    for other in other_groups():
        scores_plane(other, group).wait_recv()

    picked = jnp.zeros((8, LANES), f32)
    for zs in range(nz):
        for xs in range(2):
            for ys in range(2):
                score = board[4 * xs + 2 * ys, zs] + board[4 * xs + 2 * ys + 1, zs]
                picked += jnp.where(ids == 2 * (2 * zs + xs) + ys, score, 0.0)
    counts = jnp.broadcast_to(facts[0:1], (8, LANES))
    err = jnp.broadcast_to(picked[0:1], (8, LANES)) - picked - facts
    live = (row >= 1) & ((row - 1).astype(f32) < counts)
    err = jnp.where(live, err, 0.0)
    counts = jnp.where(counts > 0, counts, 1.0)
    nquery = Q_DEV * 2 * nz
    terms = jnp.where(lane % 2 == 0, err * err / counts, 0.0)
    loss_ref[0, 0] = jnp.sum(terms) / nquery
    weight = 2.0 * err / (counts * nquery)
    passage = (PASS_DEV * dp_at + y).astype(f32)
    at_pos = jnp.broadcast_to(jnp.where(ids[0:1] == passage, 1.0, 0.0), (8, LANES))
    at_neg = jnp.where(ids == passage, 1.0, 0.0)
    coef = jnp.sum(weight * (at_pos - at_neg), axis=0, keepdims=True)
    coef = jnp.where(row == lane % 2, jnp.broadcast_to(coef, (8, LANES)), 0.0)[:, :count]
    for t in range(4):
        here = pl.ds(t * share, share)
        block = every_q[t, :, :, :, :share].reshape(count, share)
        grad = jnp.dot(coef, block, precision=high, preferred_element_type=f32)
        pooled[:, here] = grad * scale

    def align(n, total):
        for h in range(2):
            k = h * half + n
            up = pooled[h : h + 1, lanes(n)] * gain_ref[pl.ds(k, 1), :]
            up_ref[0:1, lanes(k)] = up
            total += hid[k] * up
        return total

    total = lax.fori_loop(0, half, align, jnp.zeros((rows, LANES), f32))
    inner = jnp.sum(total, axis=1, keepdims=True) / width
    up_ref[1:, :] = jnp.zeros((7, width), f32)
    factor_ref[0] = 65536.0 * square[...]
    factor_ref[1] = jnp.broadcast_to(-65536.0 * (inv * inv * inv * inner), (rows, LANES))

    for other in other_planes():
        queries_z(z, other).wait_send()
        scores_z(z, other).wait_send()
    for other in other_groups():
        scores_plane(group, other).wait_send()
    queries_x(x).wait_send()
    queries_y(t_at, x, 0).wait_send()
    queries_y(t_at, 1 - x, 1).wait_send()
    for n in range(2):
        queries_core(n, t_at).wait_send()

    for n in range(RING):
        to_y(0, 0, 0, n).wait_send()
    for r in range(2):
        core_ctx(r).wait_send()
        for k in range(2):
            swap_ctx(k, r).wait_send()

    @pl.when(ends)
    def _():
        for k in range(2):
            lend_ctx(k).wait_send()

    @pl.when(middle)
    def _():
        for k in range(2):
            lend_swap(k).wait_send()

    def drain(j, carry):
        for role in (NEAR, NEXT, END, FAR):
            to_x(role, j).wait_send()
            for xt in range(2):
                write_out(piece(role, xt, j)).wait()
        for role in (NEAR, END):
            to_core(role, j).wait_send()

        @pl.when(ends)
        def _():
            to_mid(j).wait_send()
            for role in (NEXT, FAR):
                to_core_low(role, j).wait_send()

        @pl.when(middle)
        def _():
            for role in (NEAR, END):
                to_next(role, j).wait_send()
            to_end_whole(j).wait_send()
            for role in (NEXT, FAR):
                to_core(role, j).wait_send()
                to_end(role, j).wait_send()
                for rx in range(2):
                    side_to_end(role, j, rx).wait_send()

        return carry

    lax.fori_loop(0, chunks, drain, 0)


def tile_hidden(context, o_weight, resid, gain, queries, facts):
    rows, width = resid.shape
    depth, columns = o_weight.shape
    chunks = columns // LANES
    nz = width // (2 * columns)
    f32, bf16 = jnp.float32, jnp.bfloat16
    coded_rows = rows + 16
    dma = pltpu.SemaphoreType.DMA
    return pl.pallas_call(
        functools.partial(tile_kernel, nz),
        out_shape=(
            jax.ShapeDtypeStruct((rows, width), f32),
            jax.ShapeDtypeStruct((2, rows, LANES), f32),
            jax.ShapeDtypeStruct((8, width), f32),
            jax.ShapeDtypeStruct((1, 1), f32),
        ),
        in_specs=[pl.BlockSpec(memory_space=pl.ANY)] * 3
        + [pl.BlockSpec(memory_space=pltpu.VMEM)] * 2
        + [pl.BlockSpec(memory_space=pltpu.SMEM)] * 4,
        out_specs=(
            pl.BlockSpec(memory_space=pl.ANY),
            pl.BlockSpec(memory_space=pltpu.VMEM),
            pl.BlockSpec(memory_space=pltpu.VMEM),
            pl.BlockSpec(memory_space=pltpu.SMEM),
        ),
        scratch_shapes=[
            pltpu.VMEM((2, 2, 2 * rows, depth), bf16),
            pltpu.VMEM((2, 2, 2 * rows, depth // 2), bf16),
            pltpu.VMEM((2, nz, chunks, depth, LANES), bf16),
            pltpu.VMEM((nz, chunks, 2, coded_rows, LANES), jnp.int16),
            pltpu.VMEM((nz, chunks, coded_rows, LANES), jnp.int16),
            pltpu.VMEM((nz // 2, chunks, 2, coded_rows, LANES), jnp.int16),
            pltpu.VMEM((2 * nz * chunks, rows, LANES), f32),
            pltpu.VMEM((rows, width), bf16),
            pltpu.VMEM((RING, coded_rows, LANES), jnp.int16),
            pltpu.VMEM((RING, rows, LANES), f32),
            pltpu.VMEM((2 * rows, 2 * LANES), f32),
            dma((2,)),
            dma((2, 2)),
            dma((2, 2, 2)),
            dma((2, 2)),
            dma((2, 2)),
            dma((chunks,)),
            dma((nz, chunks)),
            dma((nz, chunks)),
            dma((nz, chunks)),
            dma((2, nz, chunks)),
            dma((RING,)),
            dma((nz, chunks, 2)),
            dma((nz // 2, chunks, 2)),
            dma((nz // 2, chunks, 2)),
            dma((nz, chunks)),
            dma((nz, chunks)),
            dma,
            dma((2 * nz * chunks,)),
            pltpu.VMEM((4, 2, nz, 2 * Q_DEV, width // 8 + 2 * LANES), f32),
            pltpu.VMEM((rows, LANES), f32),
            pltpu.VMEM((8, width // 2), f32),
            pltpu.VMEM((8, nz, 8, LANES), f32),
            dma((2, nz)),
            dma((2,)),
            dma((2, 2)),
            dma((2, 2)),
            dma((2, nz)),
            dma((2, 8)),
        ],
        compiler_params=pltpu.CompilerParams(
            collective_id=0, has_side_effects=True, vmem_limit_bytes=60 << 20
        ),
        cost_estimate=pl.CostEstimate(
            flops=2 * 4 * rows * depth * width, bytes_accessed=4 * rows * width, transcendentals=0
        ),
    )(context, o_weight, resid, gain, queries, *facts)


def grad_kernel(hidden_ref, factor_ref, up_ref, grad_ref):
    for n in range(grad_ref.shape[1] // LANES):
        here = pl.ds(n * LANES, LANES)
        grad_ref[:, here] = factor_ref[0] * up_ref[0:1, here] + factor_ref[1] * hidden_ref[:, here]


def gradient(hidden, factors, upward):
    rows, width = hidden.shape
    step = rows // 4
    return pl.pallas_call(
        grad_kernel,
        out_shape=jax.ShapeDtypeStruct((rows, width), jnp.float32),
        grid=(rows // step,),
        in_specs=[
            pl.BlockSpec((step, width), lambda n: (n, 0)),
            pl.BlockSpec((2, step, LANES), lambda n: (0, n, 0)),
            pl.BlockSpec((8, width), lambda n: (0, 0)),
        ],
        out_specs=pl.BlockSpec((step, width), lambda n: (n, 0)),
        compiler_params=pltpu.CompilerParams(vmem_limit_bytes=58 << 20),
    )(hidden, factors, upward)


def line_shards(
    context, resid, o_weight, norm_gain, queries, positive_ids, negative_ids, margins, pair_counts
):
    gain = norm_gain.reshape(-1, LANES)
    facts = (positive_ids, negative_ids, margins, pair_counts)
    hidden, factors, upward, loss = tile_hidden(context, o_weight, resid, gain, queries, facts)
    return (gradient(hidden, factors, upward), loss.reshape(()))


def solution(mesh):
    body = line_shards if dict(mesh.shape) == {"dp": 8, "tensor": 4} else shards
    return jax.shard_map(
        body,
        mesh=mesh,
        in_specs=(
            P("dp", "tensor"),
            P(("dp", "tensor"), None),
            P("tensor", "dp"),
            P(),
            P("dp", None),
            P("dp"),
            P("dp", None),
            P("dp", None),
            P("dp"),
        ),
        out_specs=(P(("dp", "tensor"), None), P()),
        check_vma=False,
    )
```
